32 devices in a mesh: rows: 8 (over z, x), text: 4 (over y, core).
Axes of the slice: x: 2, y: 2, z: 4, core: 2. Of those that a mesh axis runs over, the one named last changes fastest.
Arguments:
- frames: bfloat16 [8, 1024, 1024], P('rows', 'text'), may hold values from -6 to 6
- text_states: bfloat16 [8, 384, 1024], P('rows', 'text'), may hold values from -6 to 6
- frame_segments: int32 [8, 1024], P('rows'), may hold values from 0 to 3, never falling along the last dimension, each value on 1 to 832 neighbouring positions
- text_lengths: int32 [8, 4], P('rows'), may hold values from 1 to 312, 384 in all within a row
- self_in: bfloat16 [1024, 3072], P('rows', 'text'), may hold values from -0.1875 to 0.1875
- self_out: bfloat16 [1024, 1024], P('rows', 'text'), may hold values from -0.375 to 0.375
- cross_query: bfloat16 [1024, 1024], P('rows', 'text'), may hold values from -0.1875 to 0.1875
- cross_kv: bfloat16 [1024, 2048], P('rows', 'text'), may hold values from -0.1875 to 0.1875
- cross_out: bfloat16 [1024, 1024], P('rows', 'text'), may hold values from -0.375 to 0.375
- ffn_in: bfloat16 [1024, 4096], P('rows', 'text'), may hold values from -0.1875 to 0.1875
- ffn_out: bfloat16 [4096, 1024], P('rows', 'text'), may hold values from -0.09375 to 0.09375
- norm_gains: bfloat16 [3, 1024], P(None, 'text'), may hold values from 0.099609375 to 1.8984375
- norm_biases: bfloat16 [3, 1024], P(None, 'text'), may hold values from -1.796875 to 1.796875
- out_grad: bfloat16 [8, 1024, 1024], P('rows', 'text'), may hold values from -6 to 6
Outputs:
- output: bfloat16 [8, 1024, 1024], P('rows', 'text')
- frame_grad: float32 [8, 1024, 1024], P('rows', 'text')
- text_grad: float32 [8, 384, 1024], P('rows', 'text')
- grad_self_in: float32 [1024, 3072], P('rows', 'text')
- grad_self_out: float32 [1024, 1024], P('rows', 'text')
- grad_cross_query: float32 [1024, 1024], P('rows', 'text')
- grad_cross_kv: float32 [1024, 2048], P('rows', 'text')
- grad_cross_out: float32 [1024, 1024], P('rows', 'text')
- grad_ffn_in: float32 [1024, 4096], P('rows', 'text')
- grad_ffn_out: float32 [4096, 1024], P('rows', 'text')
- grad_norm_gains: float32 [3, 1024], P(None, 'text')
- grad_norm_biases: float32 [3, 1024], P(None, 'text')
The draws below stay inside these ranges and needn't reach their ends.
Inputs may be any that keep to these rules, and one draw needn't show every extreme that they name: `frame_segments`: within a row the clip numbers never fall; each of the 4 clips has 1 to 832 frames, one exactly 832. `text_lengths`: each row's 4 lengths sum to 384; the largest is exactly 312.
All inputs are finite; a program needn't handle non-finite values.
Results may differ from the reference program's by a relative error of at most 0.024.
Values may be sent and summed in bfloat16 or wider, within the bound.
No kernel may reach another device: no remote copies, remote signals or barrier semaphores. Data moves between devices by JAX's collectives and lax.ppermute only.
A program may use at most 256 MiB of HBM per device.

```python
import math
import jax
import jax.numpy as jnp
import numpy as np
from jax import lax

D = 1024
HEADS = 16
HEAD_DIM = 64
FF = 4096
FRAMES = 1024
TXT = 384
CLIPS = 4
FRAMES_MOST = 832
TXT_MOST = 312
SEQS = 8


def steps_of(own_key, shape, split, low, high):
    def one(axis_at, blocks):
        heights = jax.random.uniform(jax.random.fold_in(jax.random.fold_in(own_key, 6), axis_at), (blocks,), jnp.float32, low / len(split), high / len(split))
        return jnp.repeat(jnp.exp(heights), shape[axis_at] // blocks).reshape((-1,) + (1,) * (len(shape) - axis_at - 1))

    gain = one(*split[0])
    for cut in split[1:]:
        gain = gain * one(*cut)
    return gain


def split_up(count, total, limit, lean):
    portions = [(1 << 20) // math.isqrt(grade ** lean) + 1 for grade in range(2, count + 1)]
    spare, given = total - limit - (count - 1), [1] * (count - 1)
    while spare > 0:
        movable = [i for i in range(count - 1) if given[i] < limit]
        mass, remaining = sum([portions[i] for i in movable]), spare
        for i in movable:
            addition = min(limit - given[i], max(1, remaining * portions[i] // mass), spare)
            given[i] = given[i] + addition
            spare = spare - addition
    return np.array([limit] + given)


def ragged(key, number_of, total, limit, skew):
    if number_of == 2:
        one = jax.random.randint(key, (), max(1, total - limit), min(limit, total - 1) + 1)
        return jnp.stack([one, total - one])
    sizes = jnp.asarray(split_up(number_of, total, limit, skew), jnp.int32)
    twos = (number_of - 1) // 2
    source_of, sink = sizes[1:1 + 2 * twos:2], sizes[2:2 + 2 * twos:2]
    margin = jnp.minimum(source_of - 1, limit - sink)
    moved = jax.random.randint(jax.random.fold_in(key, 1), (twos,), 0, 1 << 20) % (margin + 1)
    sizes = sizes.at[1:1 + 2 * twos:2].set(source_of - moved).at[2:2 + 2 * twos:2].set(sink + moved)
    return sizes[jax.random.permutation(jax.random.fold_in(key, 2), number_of)]


def noise(rng, extent, scale, reach, pieces=(), held_as=jnp.bfloat16):
    values = scale * jax.random.normal(rng, extent, jnp.float32)
    if pieces:
        values = values * steps_of(rng, extent, pieces, -0.22, 0.18)
    return jnp.clip(values, -reach, reach).astype(held_as)


def setup_inputs(seed: int = 0) -> dict:
    splits = jax.random.split(jax.random.key(seed), 15)
    return {
        "frames": noise(splits[0], (SEQS, FRAMES, D), 1.0, 6.0, ((0, 8), (1, 4))),
        "text_states": noise(splits[1], (SEQS, TXT, D), 1.0, 6.0, ((0, 8), (1, 4))),
        "frame_segments": jax.vmap(lambda own: jnp.searchsorted(jnp.cumsum(ragged(own, CLIPS, FRAMES, FRAMES_MOST, 2)), jnp.arange(FRAMES), side="right"))(jax.random.split(splits[2], SEQS)).reshape((SEQS, FRAMES)).astype(jnp.int32),
        "text_lengths": jax.vmap(lambda own: ragged(own, CLIPS, TXT, TXT_MOST, 2))(jax.random.split(splits[3], SEQS)).reshape((SEQS, CLIPS)).astype(jnp.int32),
        "self_in": noise(splits[4], (D, 3 * D), D ** -0.5, 0.1875, ((0, 8), (1, 4))),
        "self_out": noise(splits[5], (D, D), (D // 4) ** -0.5, 0.375, ((0, 8), (1, 4))),
        "cross_query": noise(splits[6], (D, D), D ** -0.5, 0.1875, ((0, 8), (1, 4))),
        "cross_kv": noise(splits[7], (D, 2 * D), D ** -0.5, 0.1875, ((0, 8), (1, 4))),
        "cross_out": noise(splits[8], (D, D), (D // 4) ** -0.5, 0.375, ((0, 8), (1, 4))),
        "ffn_in": noise(splits[9], (D, FF), D ** -0.5, 0.1875, ((0, 8), (1, 4))),
        "ffn_out": noise(splits[10], (FF, D), FF ** -0.5, 0.09375, ((0, 8), (1, 4))),
        "norm_gains": jnp.clip(1.0 + 0.18 * jax.random.normal(splits[11], (3, D), jnp.float32), 0.099609375, 1.8984375).astype(jnp.bfloat16),
        "norm_biases": noise(splits[12], (3, D), 0.3, 1.796875, ((1, 4),)),
        "out_grad": noise(splits[13], (SEQS, FRAMES, D), 1.0, 6.0, ((0, 8), (1, 4))),
    }


@jax.custom_vjp
def low(v):
    return lax.optimization_barrier(v.astype(jnp.bfloat16)).astype(jnp.float32)

@jax.custom_vjp
def low_back(v):
    return v

def low_keep(v):
    return (low(v), None)

def low_pass(kept, grad):
    return (grad,)

def back_keep(v):
    return (v, None)

def back_low(kept, grad):
    return (low(grad),)
low.defvjp(low_keep, low_pass)
low_back.defvjp(back_keep, back_low)

def matmul(pattern, left, right):
    return jnp.einsum(pattern, left, right, precision=lax.Precision.HIGHEST)

def layer_norm(values, scaling, offset):
    average = lax.optimization_barrier(jnp.mean(values, axis=-1, keepdims=True))
    centred = values - average
    spread = lax.optimization_barrier(jnp.mean(centred * centred, axis=-1, keepdims=True))
    return centred * lax.rsqrt(spread + 1e-05) * scaling + offset

def text_segment_ids(lengths_row):
    bounds = jnp.cumsum(lengths_row)[:-1].astype(jnp.int32)
    places = jnp.arange(TXT, dtype=jnp.int32)
    return lax.optimization_barrier(jnp.sum((places[:, None] >= bounds[None, :]).astype(jnp.int32), axis=1)).astype(jnp.int32)

def attend(queries, keys, values, allowed):
    scaling = HEAD_DIM ** (-0.5)
    scores = low_back(matmul('qhe,khe->hqk', queries, keys) * scaling)
    scores = jnp.where(allowed[None], scores, -1e+30)
    probs = low(jax.nn.softmax(scores, axis=-1))
    result = matmul('hqk,khe->qhe', probs, values)
    return result.reshape(queries.shape[0], HEADS * HEAD_DIM)

def one_row(weights, frames_row, text_row, segments_row, lengths_row):
    self_in, self_out, cross_query, cross_kv, cross_out, ffn_in, ffn_out, norm_gains, norm_biases = weights
    normed_one = low(layer_norm(frames_row, norm_gains[0], norm_biases[0]))
    mixed = low_back(low(matmul('fd,de->fe', normed_one, self_in)))
    queries = mixed[:, :D].reshape(FRAMES, HEADS, HEAD_DIM)
    keys = mixed[:, D:2 * D].reshape(FRAMES, HEADS, HEAD_DIM)
    values = mixed[:, 2 * D:].reshape(FRAMES, HEADS, HEAD_DIM)
    places = jnp.arange(FRAMES, dtype=jnp.int32)
    self_allowed = (places[None, :] <= places[:, None]) & (segments_row[:, None] == segments_row[None, :])
    self_att = low_back(low(attend(queries, keys, values, self_allowed)))
    hidden = frames_row + low_back(matmul('fe,ed->fd', self_att, self_out))
    normed_two = low(layer_norm(hidden, norm_gains[1], norm_biases[1]))
    cross_q = low_back(low(matmul('fd,de->fe', normed_two, cross_query)))
    text_pairs = low_back(low(matmul('td,de->te', text_row, cross_kv)))
    cross_allowed = segments_row[:, None] == text_segment_ids(lengths_row)[None, :]
    cross_att = low_back(low(attend(cross_q.reshape(FRAMES, HEADS, HEAD_DIM), text_pairs[:, :D].reshape(TXT, HEADS, HEAD_DIM), text_pairs[:, D:].reshape(TXT, HEADS, HEAD_DIM), cross_allowed)))
    hidden_two = hidden + low_back(matmul('fe,ed->fd', cross_att, cross_out))
    normed_three = low(layer_norm(hidden_two, norm_gains[2], norm_biases[2]))
    up_proj = low_back(matmul('fd,dh->fh', normed_three, ffn_in))
    activ = low(jax.nn.gelu(up_proj, approximate=False))
    return hidden_two + matmul('fh,hd->fd', activ, ffn_out)

def reference(frames, text_states, frame_segments, text_lengths, self_in, self_out, cross_query, cross_kv, cross_out, ffn_in, ffn_out, norm_gains, norm_biases, out_grad):
    weights = tuple((matrix.astype(jnp.float32) for matrix in (self_in, self_out, cross_query, cross_kv, cross_out, ffn_in, ffn_out, norm_gains, norm_biases)))
    row_step = jax.checkpoint(one_row)

    def forward(params, frames_all, text_all):

        def scan_step(state_now, row_inputs):
            return (state_now, row_step(params, row_inputs[0], row_inputs[1], row_inputs[2], row_inputs[3]))
        _, result = lax.scan(scan_step, jnp.zeros((), jnp.float32), (frames_all, text_all, frame_segments, text_lengths))
        return result
    output, pull_back = jax.vjp(forward, weights, frames.astype(jnp.float32), text_states.astype(jnp.float32))
    grad_weights, frame_grad, text_grad = pull_back(out_grad.astype(jnp.float32))
    return (output.astype(jnp.bfloat16), frame_grad, text_grad, grad_weights[0], grad_weights[1], grad_weights[2], grad_weights[3], grad_weights[4], grad_weights[5], grad_weights[6], grad_weights[7], grad_weights[8])
```

```python
import math

import jax
import jax.numpy as jnp
from jax import lax
from jax.experimental import pallas as pl
from jax.experimental.pallas import tpu as pltpu
from jax.sharding import PartitionSpec as P

HEADS = 16
WAYS = 4
SLOTS = (0, 2, 1, 3)
LOW = jnp.bfloat16
WIDE = jnp.float32
NEVER = -1e30


def mm(left, right, left_dim=1, right_dim=0):
    return lax.dot_general(
        left, right, (((left_dim,), (right_dim,)), ((), ())), preferred_element_type=WIDE
    )


def swap(values, mask):
    return lax.ppermute(values, "text", [(i, i ^ mask) for i in range(WAYS)])


def gather_slots(block):
    pair = jnp.concatenate([block, swap(block, 2)], axis=0)
    return jnp.concatenate([pair, swap(pair, 1)], axis=0)


def scatter_slots(left, right, right_dim):
    half = left.shape[0] // 2
    block = half // 2
    away = mm(left[half:], right, 1, right_dim).astype(LOW)
    here = mm(left[:half], right, 1, right_dim)
    here = here + swap(away, 1).astype(WIDE)
    return here[:block] + swap(here[block:].astype(LOW), 2).astype(WIDE)


def norm_forward(values, gain, bias):
    average = jnp.mean(values, axis=-1, keepdims=True)
    centred = values - average
    spread = jnp.mean(centred * centred, axis=-1, keepdims=True)
    inverse = lax.rsqrt(spread + 1e-05)
    hat = centred * inverse
    return (hat * gain + bias).astype(LOW), hat, inverse


def norm_backward(grad, hat, inverse, gain):
    weighted = grad * gain
    first = jnp.mean(weighted, axis=-1, keepdims=True)
    second = jnp.mean(weighted * hat, axis=-1, keepdims=True)
    return (
        (weighted - first - hat * second) * inverse,
        jnp.sum(grad * hat, axis=0),
        jnp.sum(grad, axis=0),
    )


def slot_of(index, here):
    other = index ^ here
    return ((other & 1) << 1) | (other >> 1)


def half_lanes(values, head):
    lane = lax.broadcasted_iota(jnp.int32, values.shape, 1)
    keep = (lane < 64) if head == 0 else (lane >= 64)
    return jnp.where(keep, values, jnp.zeros_like(values))


def nt(left, right):
    return mm(left, right, 1, 1)


def rows_at(ref, slot, size, pair, offset):
    start = pl.multiple_of(slot * size, size)
    return ref[pl.ds(start, size), offset + pair * 128 : offset + (pair + 1) * 128]


def transposed(values):
    return values.astype(WIDE).T


def self_forward(here_ref, marks_ref, mixed_ref, out_ref, lse_ref):
    here = here_ref[0]
    size = mixed_ref.shape[0] // WAYS
    down = lax.broadcasted_iota(jnp.int32, (size, size), 0)
    across = lax.broadcasted_iota(jnp.int32, (size, size), 1)
    for pair in range(2):
        keys = [rows_at(mixed_ref, slot_of(j, here), size, pair, 256) for j in range(WAYS)]
        values_t = [
            transposed(rows_at(mixed_ref, slot_of(j, here), size, pair, 512)).astype(LOW)
            for j in range(WAYS)
        ]
        for i in range(WAYS):
            mine = slot_of(i, here)
            query = rows_at(mixed_ref, mine, size, pair, 0) * LOW(0.125)
            first = marks_ref[0:1, i * size : (i + 1) * size]
            outs = []
            for head in range(2):
                scores = []
                for j in range(i + 1):
                    s = nt(half_lanes(keys[j], head), query)
                    allowed = (down + j * size) >= first
                    if j == i:
                        allowed = allowed & (down <= across)
                    scores.append(jnp.where(allowed, s, NEVER))
                top = jnp.max(scores[0], axis=0, keepdims=True)
                for s in scores[1:]:
                    top = jnp.maximum(top, jnp.max(s, axis=0, keepdims=True))
                total = jnp.zeros_like(top)
                result = jnp.zeros((64, size), WIDE)
                for j, s in enumerate(scores):
                    probs = jnp.exp(s - top)
                    total = total + jnp.sum(probs, axis=0, keepdims=True)
                    part = values_t[j][head * 64 : (head + 1) * 64]
                    result = result + mm(part, probs.astype(LOW))
                outs.append(result / total)
                lse_ref[2 * pair + head : 2 * pair + head + 1, i * size : (i + 1) * size] = (
                    top + jnp.log(total)
                )
            start = pl.multiple_of(mine * size, size)
            out_ref[pl.ds(start, size), pair * 128 : (pair + 1) * 128] = (
                jnp.concatenate(outs, axis=0).T.astype(LOW)
            )


def self_backward(here_ref, marks_ref, mixed_ref, grad_ref, lse_ref, out_ref, dk_ref, dv_ref):
    here = here_ref[0]
    size = mixed_ref.shape[0] // WAYS
    down = lax.broadcasted_iota(jnp.int32, (size, size), 0)
    across = lax.broadcasted_iota(jnp.int32, (size, size), 1)
    for pair in range(2):
        keys = [rows_at(mixed_ref, slot_of(j, here), size, pair, 256) for j in range(WAYS)]
        values = [rows_at(mixed_ref, slot_of(j, here), size, pair, 512) for j in range(WAYS)]
        keys_t = [transposed(k).astype(LOW) for k in keys]
        for i in reversed(range(WAYS)):
            mine = slot_of(i, here)
            query = rows_at(mixed_ref, mine, size, pair, 0) * LOW(0.125)
            grad = rows_at(grad_ref, mine, size, pair, 0)
            first = marks_ref[0:1, i * size : (i + 1) * size]
            grads_q = []
            dk_parts = [None] * (i + 1)
            dv_parts = [None] * (i + 1)
            for head in range(2):
                mass = lse_ref[2 * pair + head : 2 * pair + head + 1, i * size : (i + 1) * size]
                grad_head = half_lanes(grad, head)
                query_head = half_lanes(query, head)
                probs, grad_probs = [], []
                delta = jnp.zeros((1, size), WIDE)
                for j in range(i + 1):
                    s = nt(half_lanes(keys[j], head), query)
                    allowed = (down + j * size) >= first
                    if j == i:
                        allowed = allowed & (down <= across)
                    p = jnp.exp(jnp.where(allowed, s, NEVER) - mass)
                    dp = nt(half_lanes(values[j], head), grad)
                    delta = delta + jnp.sum(p * dp, axis=0, keepdims=True)
                    probs.append(p)
                    grad_probs.append(dp)
                grad_q = jnp.zeros((64, size), WIDE)
                for j in range(i + 1):
                    ds = (probs[j] * (grad_probs[j] - delta)).astype(LOW)
                    dv = mm(probs[j].astype(LOW), grad_head)
                    dk = mm(ds, query_head)
                    dv_parts[j] = dv if head == 0 else dv_parts[j] + dv
                    dk_parts[j] = dk if head == 0 else dk_parts[j] + dk
                    grad_q = grad_q + mm(keys_t[j][head * 64 : (head + 1) * 64], ds)
                grads_q.append(grad_q)
            start = pl.multiple_of(mine * size, size)
            out_ref[pl.ds(start, size), pair * 128 : (pair + 1) * 128] = (
                (jnp.concatenate(grads_q, axis=0) * 0.125).T.astype(LOW)
            )
            for j in range(i + 1):
                rows = slice(j * size, (j + 1) * size)
                if i == WAYS - 1:
                    dk_ref[rows] = dk_parts[j]
                    dv_ref[rows] = dv_parts[j]
                else:
                    dk_ref[rows] = dk_ref[rows] + dk_parts[j]
                    dv_ref[rows] = dv_ref[rows] + dv_parts[j]
        for j in range(WAYS):
            rows = slice(j * size, (j + 1) * size)
            start = pl.multiple_of(slot_of(j, here) * size, size)
            out_ref[pl.ds(start, size), 256 + pair * 128 : 256 + (pair + 1) * 128] = dk_ref[
                rows
            ].astype(LOW)
            out_ref[pl.ds(start, size), 512 + pair * 128 : 512 + (pair + 1) * 128] = dv_ref[
                rows
            ].astype(LOW)


def token_places(here, count, width):
    row = lax.broadcasted_iota(jnp.int32, (count, width), 0)
    size = count // WAYS
    place = row
    for slot, mask in enumerate(SLOTS):
        inside = (row >= slot * size) & (row < (slot + 1) * size)
        place = jnp.where(inside, row - slot * size + (here ^ mask) * size, place)
    return place


def cross_forward(here_ref, marks_ref, query_ref, pairs_ref, out_ref, lse_ref):
    here = here_ref[0]
    size = query_ref.shape[0] // WAYS
    place = token_places(here, pairs_ref.shape[0], size)
    for pair in range(2):
        keys = pairs_ref[:, pair * 128 : (pair + 1) * 128]
        values_t = transposed(pairs_ref[:, 256 + pair * 128 : 256 + (pair + 1) * 128]).astype(LOW)
        for i in range(WAYS):
            mine = slot_of(i, here)
            query = rows_at(query_ref, mine, size, pair, 0) * LOW(0.125)
            low = marks_ref[1:2, i * size : (i + 1) * size]
            high = marks_ref[2:3, i * size : (i + 1) * size]
            allowed = (place >= low) & (place < high)
            outs = []
            for head in range(2):
                s = jnp.where(allowed, nt(half_lanes(keys, head), query), NEVER)
                top = jnp.max(s, axis=0, keepdims=True)
                probs = jnp.exp(s - top)
                total = jnp.sum(probs, axis=0, keepdims=True)
                result = mm(values_t[head * 64 : (head + 1) * 64], probs.astype(LOW))
                outs.append(result / total)
                lse_ref[2 * pair + head : 2 * pair + head + 1, i * size : (i + 1) * size] = (
                    top + jnp.log(total)
                )
            start = pl.multiple_of(mine * size, size)
            out_ref[pl.ds(start, size), pair * 128 : (pair + 1) * 128] = (
                jnp.concatenate(outs, axis=0).T.astype(LOW)
            )


def cross_backward(here_ref, marks_ref, query_ref, pairs_ref, grad_ref, lse_ref, dq_ref, dkv_ref):
    here = here_ref[0]
    size = query_ref.shape[0] // WAYS
    place = token_places(here, pairs_ref.shape[0], size)
    for pair in range(2):
        keys = pairs_ref[:, pair * 128 : (pair + 1) * 128]
        values = pairs_ref[:, 256 + pair * 128 : 256 + (pair + 1) * 128]
        keys_t = transposed(keys).astype(LOW)
        sum_k = jnp.zeros(keys.shape, WIDE)
        sum_v = jnp.zeros(keys.shape, WIDE)
        for i in range(WAYS):
            mine = slot_of(i, here)
            query = rows_at(query_ref, mine, size, pair, 0) * LOW(0.125)
            grad = rows_at(grad_ref, mine, size, pair, 0)
            low = marks_ref[1:2, i * size : (i + 1) * size]
            high = marks_ref[2:3, i * size : (i + 1) * size]
            allowed = (place >= low) & (place < high)
            grads_q = []
            for head in range(2):
                mass = lse_ref[2 * pair + head : 2 * pair + head + 1, i * size : (i + 1) * size]
                s = jnp.where(allowed, nt(half_lanes(keys, head), query), NEVER)
                p = jnp.exp(s - mass)
                dp = nt(half_lanes(values, head), grad)
                delta = jnp.sum(p * dp, axis=0, keepdims=True)
                ds = (p * (dp - delta)).astype(LOW)
                sum_v = sum_v + mm(p.astype(LOW), half_lanes(grad, head))
                sum_k = sum_k + mm(ds, half_lanes(query, head))
                grads_q.append(mm(keys_t[head * 64 : (head + 1) * 64], ds))
            start = pl.multiple_of(mine * size, size)
            dq_ref[pl.ds(start, size), pair * 128 : (pair + 1) * 128] = (
                (jnp.concatenate(grads_q, axis=0) * 0.125).T.astype(LOW)
            )
        dkv_ref[:, pair * 128 : (pair + 1) * 128] = sum_k.astype(LOW)
        dkv_ref[:, 256 + pair * 128 : 256 + (pair + 1) * 128] = sum_v.astype(LOW)


def call(body, outs, operands, scratch=(), flops=0, exps=0):
    specs = [pl.BlockSpec(memory_space=pltpu.SMEM)] + [
        pl.BlockSpec(memory_space=pltpu.VMEM) for _ in operands[1:]
    ]
    moved = sum(v.size * v.dtype.itemsize for v in operands)
    moved += sum(o.size * o.dtype.itemsize for o in outs)
    return pl.pallas_call(
        body,
        out_shape=outs,
        in_specs=specs,
        out_specs=[pl.BlockSpec(memory_space=pltpu.VMEM) for _ in outs],
        scratch_shapes=list(scratch),
        cost_estimate=pl.CostEstimate(flops=flops, bytes_accessed=moved, transcendentals=exps),
        compiler_params=pltpu.CompilerParams(vmem_limit_bytes=48 << 20),
    )(*operands)


def shaped(shape, dtype):
    return jax.ShapeDtypeStruct(shape, dtype)


def deal(matrix, groups):
    depth, width = matrix.shape
    piece = width // (groups * WAYS)
    return jnp.moveaxis(matrix.reshape(depth, groups, WAYS, piece), 2, 0).reshape(
        WAYS, depth, groups * piece
    )


def undeal(dealt, groups):
    _, depth, width = dealt.shape
    return jnp.moveaxis(dealt.reshape(WAYS, depth, groups, width // groups), 0, 2).reshape(
        depth, WAYS * width
    )


def exchange(dealt):
    return lax.all_to_all(dealt, "text", 0, 0, tiled=True)


def side_by_side(parts):
    return jnp.moveaxis(parts, 0, 1).reshape(parts.shape[1], -1)


def apart(columns):
    depth, width = columns.shape
    return jnp.moveaxis(columns.reshape(depth, WAYS, width // WAYS), 1, 0)


def gather_rows(block):
    return lax.all_gather(block, "rows", axis=0, tiled=True)


def sum_rows(whole):
    return lax.psum_scatter(whole, "rows", scatter_dimension=0, tiled=True)


def own_heads(matrix, here):
    rows = gather_rows(lax.all_gather(matrix, "text", axis=1, tiled=True))
    width = rows.shape[1]
    grouped = rows.reshape(HEADS // WAYS, WAYS, -1, width)
    return lax.dynamic_index_in_dim(grouped, here, 1, keepdims=False).reshape(-1, width)


def return_heads(grad, here):
    count, width = grad.shape
    spread = jnp.zeros((HEADS // WAYS, WAYS, count * WAYS // HEADS, width), grad.dtype)
    spread = lax.dynamic_update_index_in_dim(
        spread, grad.reshape(HEADS // WAYS, 1, -1, width), here, 1
    )
    columns = lax.psum_scatter(
        spread.reshape(count * WAYS, width), "text", scatter_dimension=1, tiled=True
    )
    return sum_rows(columns)


def local(
    frames,
    text_states,
    frame_segments,
    text_lengths,
    self_in,
    self_out,
    cross_query,
    cross_kv,
    cross_out,
    ffn_in,
    ffn_out,
    norm_gains,
    norm_biases,
    out_grad,
):
    here = lax.axis_index("text")
    here_low = here.astype(jnp.int32).reshape(1)
    row_count = lax.axis_size("rows")
    width = frames.shape[2]
    count = frames.shape[1] * WAYS
    inner = width // WAYS

    chunk = ffn_out.shape[0] // WAYS
    packed = jnp.concatenate(
        [deal(self_in, 3), deal(cross_query, 1), deal(cross_kv, 2)], axis=2
    )
    packed = exchange(packed)
    piece = inner // WAYS
    w_mixed = gather_rows(side_by_side(packed[:, :, : 3 * piece]))
    w_query = gather_rows(side_by_side(packed[:, :, 3 * piece : 4 * piece]))
    w_pairs = gather_rows(side_by_side(packed[:, :, 4 * piece :]))
    w_self = own_heads(self_out, here)
    w_cross = own_heads(cross_out, here)
    w_up = gather_rows(side_by_side(exchange(deal(ffn_in, row_count // WAYS))))
    w_down = gather_rows(
        side_by_side(exchange(ffn_out.reshape(WAYS, chunk, ffn_out.shape[1])))
    )

    norms = jnp.concatenate([norm_gains, norm_biases], axis=0)
    norms = lax.all_gather(norms, "text", axis=1, tiled=True).astype(WIDE)
    gains, biases = norms[:3], norms[3:]
    segments = frame_segments[0]
    clips = text_lengths.shape[1]
    ends = jnp.cumsum(text_lengths[0])
    clip = jnp.arange(clips, dtype=jnp.int32)
    begins = jnp.sum((segments[None, :] < clip[:, None]).astype(jnp.int32), axis=1)
    same = (segments[None, :] == clip[:, None]).astype(jnp.int32)
    marks = jnp.stack(
        [
            jnp.sum(same * begins[:, None], axis=0),
            jnp.sum(same * (ends - text_lengths[0])[:, None], axis=0),
            jnp.sum(same * ends[:, None], axis=0),
        ]
    )
    marks = jnp.concatenate([marks, jnp.zeros((5, count), jnp.int32)], axis=0)

    frames_wide = frames[0].astype(WIDE)
    one, hat_one, inverse_one = norm_forward(frames_wide, gains[0], biases[0])
    one_all = gather_slots(one)
    mixed = mm(one_all, w_mixed).astype(LOW)
    self_flops = count * count * inner * 2 * 5 // 8
    self_att, self_lse = call(
        self_forward,
        [shaped((count, inner), LOW), shaped((4, count), WIDE)],
        (here_low, marks, mixed),
        flops=2 * self_flops,
        exps=count * count * 5 // 2,
    )
    hidden = frames_wide + scatter_slots(self_att, w_self, 0)
    two, hat_two, inverse_two = norm_forward(hidden, gains[1], biases[1])
    two_all = gather_slots(two)
    query = mm(two_all, w_query).astype(LOW)
    text_all = gather_slots(text_states[0])
    text_count = text_all.shape[0]
    text_pairs = mm(text_all, w_pairs).astype(LOW)
    cross_flops = count * text_count * inner * 2
    cross_att, cross_lse = call(
        cross_forward,
        [shaped((count, inner), LOW), shaped((4, count), WIDE)],
        (here_low, marks, query, text_pairs),
        flops=2 * cross_flops,
        exps=count * text_count * 4,
    )
    hidden_two = hidden + scatter_slots(cross_att, w_cross, 0)
    three, hat_three, inverse_three = norm_forward(hidden_two, gains[2], biases[2])
    three_all = gather_slots(three)
    up = mm(three_all, w_up)
    phi = 0.5 * (1.0 + lax.erf(up * math.sqrt(0.5)))
    activ = (up * phi).astype(LOW)
    output = (hidden_two + scatter_slots(activ, w_down, 0)).astype(LOW)

    grad_all = gather_slots(out_grad[0])
    g_down = mm(activ, grad_all, 0, 0).astype(LOW)
    slope = phi + up * (jnp.exp(-0.5 * up * up) * (1.0 / math.sqrt(2.0 * math.pi)))
    grad_up = (mm(grad_all, w_down, 1, 1) * slope).astype(LOW)
    g_up = mm(three_all, grad_up, 0, 0).astype(LOW)
    part, gain_three, bias_three = norm_backward(
        scatter_slots(grad_up, w_up, 1), hat_three, inverse_three, gains[2]
    )
    grad_two = out_grad[0].astype(WIDE) + part
    branch_two = gather_slots(grad_two.astype(LOW))
    grad_cross = mm(branch_two, w_cross, 1, 1).astype(LOW)
    g_cross = mm(cross_att, branch_two, 0, 0).astype(LOW)
    grad_query, grad_pairs = call(
        cross_backward,
        [shaped((count, inner), LOW), shaped((text_count, 2 * inner), LOW)],
        (here_low, marks, query, text_pairs, grad_cross, cross_lse),
        flops=5 * cross_flops,
        exps=count * text_count * 4,
    )
    g_query = mm(two_all, grad_query, 0, 0).astype(LOW)
    g_pairs = mm(text_all, grad_pairs, 0, 0).astype(LOW)
    text_grad = scatter_slots(grad_pairs, w_pairs, 1)
    part, gain_two, bias_two = norm_backward(
        scatter_slots(grad_query, w_query, 1), hat_two, inverse_two, gains[1]
    )
    grad_hidden = grad_two + part
    branch = gather_slots(grad_hidden.astype(LOW))
    grad_self = mm(branch, w_self, 1, 1).astype(LOW)
    g_self = mm(self_att, branch, 0, 0).astype(LOW)
    (grad_mixed,) = call(
        self_backward,
        [shaped((count, 3 * inner), LOW)],
        (here_low, marks, mixed, grad_self, self_lse),
        scratch=[pltpu.VMEM((count, 128), WIDE), pltpu.VMEM((count, 128), WIDE)],
        flops=5 * self_flops,
        exps=count * count * 5 // 2,
    )
    g_mixed = mm(one_all, grad_mixed, 0, 0).astype(LOW)
    part, gain_one, bias_one = norm_backward(
        scatter_slots(grad_mixed, w_mixed, 1), hat_one, inverse_one, gains[0]
    )
    frame_grad = grad_hidden + part

    norm_sums = jnp.stack([gain_one, gain_two, gain_three, bias_one, bias_two, bias_three])
    norm_sums = lax.psum(norm_sums, ("rows", "text"))
    norm_sums = lax.dynamic_slice_in_dim(norm_sums, here * inner, inner, 1)

    d_down = exchange(apart(sum_rows(g_down))).reshape(ffn_out.shape).astype(WIDE)
    d_up = undeal(exchange(apart(sum_rows(g_up))), row_count // WAYS).astype(WIDE)
    d_cross = return_heads(g_cross, here).astype(WIDE)
    d_self = return_heads(g_self, here).astype(WIDE)
    d_query = undeal(exchange(apart(sum_rows(g_query))), 1).astype(WIDE)
    d_pairs = undeal(exchange(apart(sum_rows(g_pairs))), 2).astype(WIDE)
    d_mixed = undeal(exchange(apart(sum_rows(g_mixed))), 3).astype(WIDE)
    return (
        output[None],
        frame_grad[None],
        text_grad[None],
        d_mixed,
        d_self,
        d_query,
        d_pairs,
        d_cross,
        d_up,
        d_down,
        norm_sums[:3],
        norm_sums[3:],
    )


def solution(mesh):
    in_specs = (
        P("rows", "text", None),
        P("rows", "text", None),
        P("rows", None),
        P("rows", None),
        P("rows", "text"),
        P("rows", "text"),
        P("rows", "text"),
        P("rows", "text"),
        P("rows", "text"),
        P("rows", "text"),
        P("rows", "text"),
        P(None, "text"),
        P(None, "text"),
        P("rows", "text", None),
    )
    out_specs = (
        P("rows", "text", None),
        P("rows", "text", None),
        P("rows", "text", None),
        P("rows", "text"),
        P("rows", "text"),
        P("rows", "text"),
        P("rows", "text"),
        P("rows", "text"),
        P("rows", "text"),
        P("rows", "text"),
        P(None, "text"),
        P(None, "text"),
    )
    return jax.shard_map(local, mesh=mesh, in_specs=in_specs, out_specs=out_specs, check_vma=False)
```

```python
import math

import jax
import jax.numpy as jnp
from jax import lax
from jax.experimental import pallas as pl
from jax.experimental.pallas import tpu as pltpu
from jax.sharding import PartitionSpec as P

HEADS = 16
WAYS = 4
SLOTS = (0, 2, 1, 3)
LOW = jnp.bfloat16
WIDE = jnp.float32
NEVER = -1e30


def mm(left, right, left_dim=1, right_dim=0):
    return lax.dot_general(
        left, right, (((left_dim,), (right_dim,)), ((), ())), preferred_element_type=WIDE
    )


def swap(values, mask):
    return lax.ppermute(values, "text", [(i, i ^ mask) for i in range(WAYS)])


def gather_slots(block):
    pair = jnp.concatenate([block, swap(block, 2)], axis=0)
    return jnp.concatenate([pair, swap(pair, 1)], axis=0)


def scatter_slots(left, right, right_dim):
    half = left.shape[0] // 2
    block = half // 2
    away = mm(left[half:], right, 1, right_dim).astype(LOW)
    here = mm(left[:half], right, 1, right_dim)
    here = here + swap(away, 1).astype(WIDE)
    return here[:block] + swap(here[block:].astype(LOW), 2).astype(WIDE)


def norm_forward(values, gain, bias):
    average = jnp.mean(values, axis=-1, keepdims=True)
    centred = values - average
    spread = jnp.mean(centred * centred, axis=-1, keepdims=True)
    inverse = lax.rsqrt(spread + 1e-05)
    hat = centred * inverse
    return (hat * gain + bias).astype(LOW), hat, inverse


def norm_backward(grad, hat, inverse, gain):
    weighted = grad * gain
    first = jnp.mean(weighted, axis=-1, keepdims=True)
    second = jnp.mean(weighted * hat, axis=-1, keepdims=True)
    return (
        (weighted - first - hat * second) * inverse,
        jnp.sum(grad * hat, axis=0),
        jnp.sum(grad, axis=0),
    )


def slot_of(index, here):
    other = index ^ here
    return ((other & 1) << 1) | (other >> 1)


def half_lanes(values, head):
    lane = lax.broadcasted_iota(jnp.int32, values.shape, 1)
    keep = (lane < 64) if head == 0 else (lane >= 64)
    return jnp.where(keep, values, jnp.zeros_like(values))


def nt(left, right):
    return mm(left, right, 1, 1)


def rows_at(ref, slot, size, pair, offset):
    start = pl.multiple_of(slot * size, size)
    return ref[pl.ds(start, size), offset + pair * 128 : offset + (pair + 1) * 128]


def transposed(values):
    return values.astype(WIDE).T


def self_forward(here_ref, marks_ref, mixed_ref, out_ref, lse_ref):
    here = here_ref[0]
    size = mixed_ref.shape[0] // WAYS
    down = lax.broadcasted_iota(jnp.int32, (size, size), 0)
    across = lax.broadcasted_iota(jnp.int32, (size, size), 1)
    for pair in range(2):
        keys = [rows_at(mixed_ref, slot_of(j, here), size, pair, 256) for j in range(WAYS)]
        values_t = [
            transposed(rows_at(mixed_ref, slot_of(j, here), size, pair, 512)).astype(LOW)
            for j in range(WAYS)
        ]
        for i in range(WAYS):
            mine = slot_of(i, here)
            query = rows_at(mixed_ref, mine, size, pair, 0) * LOW(0.125)
            first = marks_ref[0:1, i * size : (i + 1) * size]
            outs = []
            for head in range(2):
                scores = []
                for j in range(i + 1):
                    s = nt(half_lanes(keys[j], head), query)
                    allowed = (down + j * size) >= first
                    if j == i:
                        allowed = allowed & (down <= across)
                    scores.append(jnp.where(allowed, s, NEVER))
                top = jnp.max(scores[0], axis=0, keepdims=True)
                for s in scores[1:]:
                    top = jnp.maximum(top, jnp.max(s, axis=0, keepdims=True))
                total = jnp.zeros_like(top)
                result = jnp.zeros((64, size), WIDE)
                for j, s in enumerate(scores):
                    probs = jnp.exp(s - top)
                    total = total + jnp.sum(probs, axis=0, keepdims=True)
                    part = values_t[j][head * 64 : (head + 1) * 64]
                    result = result + mm(part, probs.astype(LOW))
                outs.append(result / total)
                lse_ref[2 * pair + head : 2 * pair + head + 1, i * size : (i + 1) * size] = (
                    top + jnp.log(total)
                )
            start = pl.multiple_of(mine * size, size)
            out_ref[pl.ds(start, size), pair * 128 : (pair + 1) * 128] = (
                jnp.concatenate(outs, axis=0).T.astype(LOW)
            )


def self_backward(here_ref, marks_ref, mixed_ref, grad_ref, lse_ref, out_ref, dk_ref, dv_ref):
    here = here_ref[0]
    size = mixed_ref.shape[0] // WAYS
    down = lax.broadcasted_iota(jnp.int32, (size, size), 0)
    across = lax.broadcasted_iota(jnp.int32, (size, size), 1)
    for pair in range(2):
        keys = [rows_at(mixed_ref, slot_of(j, here), size, pair, 256) for j in range(WAYS)]
        values = [rows_at(mixed_ref, slot_of(j, here), size, pair, 512) for j in range(WAYS)]
        keys_t = [transposed(k).astype(LOW) for k in keys]
        for i in reversed(range(WAYS)):
            mine = slot_of(i, here)
            query = rows_at(mixed_ref, mine, size, pair, 0) * LOW(0.125)
            grad = rows_at(grad_ref, mine, size, pair, 0)
            first = marks_ref[0:1, i * size : (i + 1) * size]
            grads_q = []
            dk_parts = [None] * (i + 1)
            dv_parts = [None] * (i + 1)
            for head in range(2):
                mass = lse_ref[2 * pair + head : 2 * pair + head + 1, i * size : (i + 1) * size]
                grad_head = half_lanes(grad, head)
                query_head = half_lanes(query, head)
                probs, grad_probs = [], []
                delta = jnp.zeros((1, size), WIDE)
                for j in range(i + 1):
                    s = nt(half_lanes(keys[j], head), query)
                    allowed = (down + j * size) >= first
                    if j == i:
                        allowed = allowed & (down <= across)
                    p = jnp.exp(jnp.where(allowed, s, NEVER) - mass)
                    dp = nt(half_lanes(values[j], head), grad)
                    delta = delta + jnp.sum(p * dp, axis=0, keepdims=True)
                    probs.append(p)
                    grad_probs.append(dp)
                grad_q = jnp.zeros((64, size), WIDE)
                for j in range(i + 1):
                    ds = (probs[j] * (grad_probs[j] - delta)).astype(LOW)
                    dv = mm(probs[j].astype(LOW), grad_head)
                    dk = mm(ds, query_head)
                    dv_parts[j] = dv if head == 0 else dv_parts[j] + dv
                    dk_parts[j] = dk if head == 0 else dk_parts[j] + dk
                    grad_q = grad_q + mm(keys_t[j][head * 64 : (head + 1) * 64], ds)
                grads_q.append(grad_q)
            start = pl.multiple_of(mine * size, size)
            out_ref[pl.ds(start, size), pair * 128 : (pair + 1) * 128] = (
                (jnp.concatenate(grads_q, axis=0) * 0.125).T.astype(LOW)
            )
            for j in range(i + 1):
                rows = slice(j * size, (j + 1) * size)
                if i == WAYS - 1:
                    dk_ref[rows] = dk_parts[j]
                    dv_ref[rows] = dv_parts[j]
                else:
                    dk_ref[rows] = dk_ref[rows] + dk_parts[j]
                    dv_ref[rows] = dv_ref[rows] + dv_parts[j]
        for j in range(WAYS):
            rows = slice(j * size, (j + 1) * size)
            start = pl.multiple_of(slot_of(j, here) * size, size)
            out_ref[pl.ds(start, size), 256 + pair * 128 : 256 + (pair + 1) * 128] = dk_ref[
                rows
            ].astype(LOW)
            out_ref[pl.ds(start, size), 512 + pair * 128 : 512 + (pair + 1) * 128] = dv_ref[
                rows
            ].astype(LOW)


def token_places(here, count, width):
    row = lax.broadcasted_iota(jnp.int32, (count, width), 0)
    size = count // WAYS
    place = row
    for slot, mask in enumerate(SLOTS):
        inside = (row >= slot * size) & (row < (slot + 1) * size)
        place = jnp.where(inside, row - slot * size + (here ^ mask) * size, place)
    return place


def cross_forward(here_ref, marks_ref, query_ref, pairs_ref, out_ref, lse_ref):
    here = here_ref[0]
    size = query_ref.shape[0] // WAYS
    place = token_places(here, pairs_ref.shape[0], size)
    for pair in range(2):
        keys = pairs_ref[:, pair * 128 : (pair + 1) * 128]
        values_t = transposed(pairs_ref[:, 256 + pair * 128 : 256 + (pair + 1) * 128]).astype(LOW)
        for i in range(WAYS):
            mine = slot_of(i, here)
            query = rows_at(query_ref, mine, size, pair, 0) * LOW(0.125)
            low = marks_ref[1:2, i * size : (i + 1) * size]
            high = marks_ref[2:3, i * size : (i + 1) * size]
            allowed = (place >= low) & (place < high)
            outs = []
            for head in range(2):
                s = jnp.where(allowed, nt(half_lanes(keys, head), query), NEVER)
                top = jnp.max(s, axis=0, keepdims=True)
                probs = jnp.exp(s - top)
                total = jnp.sum(probs, axis=0, keepdims=True)
                result = mm(values_t[head * 64 : (head + 1) * 64], probs.astype(LOW))
                outs.append(result / total)
                lse_ref[2 * pair + head : 2 * pair + head + 1, i * size : (i + 1) * size] = (
                    top + jnp.log(total)
                )
            start = pl.multiple_of(mine * size, size)
            out_ref[pl.ds(start, size), pair * 128 : (pair + 1) * 128] = (
                jnp.concatenate(outs, axis=0).T.astype(LOW)
            )


def cross_backward(here_ref, marks_ref, query_ref, pairs_ref, grad_ref, lse_ref, dq_ref, dkv_ref):
    here = here_ref[0]
    size = query_ref.shape[0] // WAYS
    place = token_places(here, pairs_ref.shape[0], size)
    for pair in range(2):
        keys = pairs_ref[:, pair * 128 : (pair + 1) * 128]
        values = pairs_ref[:, 256 + pair * 128 : 256 + (pair + 1) * 128]
        keys_t = transposed(keys).astype(LOW)
        sum_k = jnp.zeros(keys.shape, WIDE)
        sum_v = jnp.zeros(keys.shape, WIDE)
        for i in range(WAYS):
            mine = slot_of(i, here)
            query = rows_at(query_ref, mine, size, pair, 0) * LOW(0.125)
            grad = rows_at(grad_ref, mine, size, pair, 0)
            low = marks_ref[1:2, i * size : (i + 1) * size]
            high = marks_ref[2:3, i * size : (i + 1) * size]
            allowed = (place >= low) & (place < high)
            grads_q = []
            for head in range(2):
                mass = lse_ref[2 * pair + head : 2 * pair + head + 1, i * size : (i + 1) * size]
                s = jnp.where(allowed, nt(half_lanes(keys, head), query), NEVER)
                p = jnp.exp(s - mass)
                dp = nt(half_lanes(values, head), grad)
                delta = jnp.sum(p * dp, axis=0, keepdims=True)
                ds = (p * (dp - delta)).astype(LOW)
                sum_v = sum_v + mm(p.astype(LOW), half_lanes(grad, head))
                sum_k = sum_k + mm(ds, half_lanes(query, head))
                grads_q.append(mm(keys_t[head * 64 : (head + 1) * 64], ds))
            start = pl.multiple_of(mine * size, size)
            dq_ref[pl.ds(start, size), pair * 128 : (pair + 1) * 128] = (
                (jnp.concatenate(grads_q, axis=0) * 0.125).T.astype(LOW)
            )
        dkv_ref[:, pair * 128 : (pair + 1) * 128] = sum_k.astype(LOW)
        dkv_ref[:, 256 + pair * 128 : 256 + (pair + 1) * 128] = sum_v.astype(LOW)


def call(body, outs, operands, scratch=(), flops=0, exps=0):
    specs = [pl.BlockSpec(memory_space=pltpu.SMEM)] + [
        pl.BlockSpec(memory_space=pltpu.VMEM) for _ in operands[1:]
    ]
    moved = sum(v.size * v.dtype.itemsize for v in operands)
    moved += sum(o.size * o.dtype.itemsize for o in outs)
    return pl.pallas_call(
        body,
        out_shape=outs,
        in_specs=specs,
        out_specs=[pl.BlockSpec(memory_space=pltpu.VMEM) for _ in outs],
        scratch_shapes=list(scratch),
        cost_estimate=pl.CostEstimate(flops=flops, bytes_accessed=moved, transcendentals=exps),
        compiler_params=pltpu.CompilerParams(vmem_limit_bytes=48 << 20),
    )(*operands)


def shaped(shape, dtype):
    return jax.ShapeDtypeStruct(shape, dtype)


def deal(matrix, groups):
    depth, width = matrix.shape
    piece = width // (groups * WAYS)
    return jnp.moveaxis(matrix.reshape(depth, groups, WAYS, piece), 2, 0).reshape(
        WAYS, depth, groups * piece
    )


def undeal(dealt, groups):
    _, depth, width = dealt.shape
    return jnp.moveaxis(dealt.reshape(WAYS, depth, groups, width // groups), 0, 2).reshape(
        depth, WAYS * width
    )


def pick(values, index, axis):
    return lax.dynamic_index_in_dim(values, index, axis, keepdims=False)


def ordered(mine, other, bit, axis=0):
    return jnp.stack([jnp.where(bit == 0, mine, other), jnp.where(bit == 0, other, mine)], axis)


def exchange(dealt, here):
    core, far = here & 1, here >> 1
    tail = dealt.shape[1:]
    dealt = dealt.reshape((2, 2) + tail)
    stage = ordered(pick(dealt, core, 1), swap(pick(dealt, 1 - core, 1), 1), core, 1)
    return ordered(pick(stage, far, 0), swap(pick(stage, 1 - far, 0), 2), far).reshape(
        (WAYS,) + tail
    )


def side_by_side(parts):
    return jnp.moveaxis(parts, 0, 1).reshape(parts.shape[1], -1)


def apart(columns):
    depth, width = columns.shape
    return jnp.moveaxis(columns.reshape(depth, WAYS, width // WAYS), 1, 0)


def row_swap(values, mask):
    size = lax.axis_size("rows")
    return lax.ppermute(values, "rows", [(i, i ^ mask) for i in range(size)])


def gather_rows(block):
    return lax.all_gather(block, "rows", axis=0, tiled=True)


def sum_rows(whole):
    return lax.psum_scatter(whole, "rows", scatter_dimension=0, tiled=True)


def place_pieces(depth, splits, heads_width, row_ref, *refs):
    row = row_ref[0]
    pieces, other = refs[:4], refs[4]
    outs, sem = refs[5:-1], refs[-1]
    copies = []

    def copy(source, target):
        copies.append(pltpu.make_async_copy(source, target, sem.at[len(copies)]))
        copies[-1].start()

    for k in range(4):
        for flip in range(2):
            owner = (row ^ flip) ^ (2 * k)
            start = pl.multiple_of(owner * depth, depth)
            column = 0
            for index, width in enumerate(splits):
                if flip:
                    source = other.at[k, :, column : column + width]
                else:
                    source = pieces[k].at[:, column : column + width]
                copy(source, outs[index].at[pl.ds(start, depth)])
                column += width
        if heads_width:
            half = depth // 2
            start = pl.multiple_of(((row >> 1) ^ k) * half, half)
            for index in range(2):
                source = pieces[k].at[index * half : (index + 1) * half, column:]
                copy(source, outs[len(splits) + index].at[pl.ds(start, half)])
    for pending in copies:
        pending.wait()


def gather_grid(block, row, splits, heads_width=0):
    depth = block.shape[0]
    uniform = sum(splits)
    pieces = [block] + [row_swap(block, 2 * k) for k in range(1, 4)]
    other = row_swap(jnp.stack([p[:, :uniform] for p in pieces]), 1)
    outs = [shaped((8 * depth, width), LOW) for width in splits]
    if heads_width:
        outs += [shaped((2 * depth, heads_width), LOW)] * 2
    copies = 8 * len(splits) + (8 if heads_width else 0)
    moved = 4 * 8 * depth * uniform + 16 * depth * heads_width
    body = lambda *refs: place_pieces(depth, splits, heads_width, *refs)
    return pl.pallas_call(
        body,
        out_shape=outs,
        in_specs=[pl.BlockSpec(memory_space=pltpu.SMEM)] + [pl.BlockSpec(memory_space=pl.ANY)] * 5,
        out_specs=[pl.BlockSpec(memory_space=pl.ANY) for _ in outs],
        scratch_shapes=[pltpu.SemaphoreType.DMA((copies,))],
        cost_estimate=pl.CostEstimate(flops=0, bytes_accessed=moved, transcendentals=0),
    )(row.astype(jnp.int32).reshape(1), *pieces, other)


def sum_grid(whole, row):
    grouped = whole.reshape(4, 2, -1, whole.shape[1])
    far, x = row >> 1, row & 1
    column = pick(grouped, x, 1).astype(WIDE) + row_swap(pick(grouped, 1 - x, 1), 1).astype(WIDE)
    return sum_column(column, far)


def sum_column(column, far):
    low = column.astype(LOW)
    total = pick(column, far, 0)
    for k in range(1, 4):
        total = total + row_swap(pick(low, far ^ k, 0), 2 * k).astype(WIDE)
    return total


def own_heads(matrix, here):
    rows = gather_rows(lax.all_gather(matrix, "text", axis=1, tiled=True))
    width = rows.shape[1]
    grouped = rows.reshape(HEADS // WAYS, WAYS, -1, width)
    return pick(grouped, here, 1).reshape(-1, width)


def return_heads(grad, here):
    count, width = grad.shape
    spread = jnp.zeros((HEADS // WAYS, WAYS, count * WAYS // HEADS, width), grad.dtype)
    spread = lax.dynamic_update_index_in_dim(
        spread, grad.reshape(HEADS // WAYS, 1, -1, width), here, 1
    )
    columns = lax.psum_scatter(
        spread.reshape(count * WAYS, width), "text", scatter_dimension=1, tiled=True
    )
    return sum_rows(columns)


def lift_heads(both, here, row):
    core, far, x = here & 1, here >> 1, row & 1
    grouped = both.reshape(2, 2, -1, both.shape[2])
    stage = ordered(pick(grouped, core, 1), swap(pick(grouped, 1 - core, 1), 1), core)
    stage = ordered(stage, swap(stage, 2), far)
    sorted_lines = stage.reshape(WAYS, 2 * grouped.shape[2], -1)
    lines = jnp.concatenate([sorted_lines[i] for i in range(WAYS)], axis=1)
    return jnp.where(x == far, lines, row_swap(lines, 1))


def lower_heads(grads, here, row):
    core, far, x = here & 1, here >> 1, row & 1
    width = grads[0].shape[1]
    column = jnp.stack([g.reshape(4, -1, width) for g in grads], axis=1)
    total = sum_column(column, row >> 1)
    total = total + row_swap(total.astype(LOW), 1).astype(WIDE)
    half = total.reshape(total.shape[:2] + (2, width // 2))
    sent = swap(pick(half, 1 - far, 2).astype(LOW), 2).astype(WIDE)
    lines = jnp.where(x == far, pick(half, far, 2), sent)
    quarter = lines.reshape(lines.shape[:2] + (2, width // WAYS))
    sent = swap(pick(quarter, 1 - core, 2).astype(LOW), 1).astype(WIDE)
    return ordered(pick(quarter, core, 2), sent, core, 1).reshape(2, -1, width // WAYS)


def local(
    frames,
    text_states,
    frame_segments,
    text_lengths,
    self_in,
    self_out,
    cross_query,
    cross_kv,
    cross_out,
    ffn_in,
    ffn_out,
    norm_gains,
    norm_biases,
    out_grad,
):
    here = lax.axis_index("text")
    here_low = here.astype(jnp.int32).reshape(1)
    row_count = lax.axis_size("rows")
    width = frames.shape[2]
    count = frames.shape[1] * WAYS
    inner = width // WAYS

    row = lax.axis_index("rows")
    grid = row_count == 8
    chunk = ffn_out.shape[0] // WAYS
    norms = jnp.concatenate([norm_gains, norm_biases], axis=0)
    norms = ordered(norms, swap(norms, 2), here >> 1)
    norms = ordered(norms, swap(norms, 1), here & 1, 1)
    norms = jnp.moveaxis(norms, 2, 0).reshape(6, width).astype(WIDE)
    gains, biases = norms[:3], norms[3:]
    mixed_block = side_by_side(exchange(deal(self_in, 3), here))
    dealt = jnp.concatenate([deal(cross_query, 1), deal(cross_kv, 2)], axis=2)
    parts = exchange(dealt, here)
    piece = inner // WAYS
    query_block = side_by_side(parts[:, :, :piece])
    pairs_block = side_by_side(parts[:, :, piece:])
    if grid:
        (w_mixed,) = gather_grid(mixed_block, row, (3 * inner,))
        lines = lift_heads(jnp.stack([self_out, cross_out]), here, row)
        block = jnp.concatenate([query_block, pairs_block, lines], axis=1)
        w_query, w_pairs, w_self, w_cross = gather_grid(block, row, (inner, 2 * inner), width)
    else:
        w_mixed = gather_rows(mixed_block)
        w_query = gather_rows(query_block)
        w_pairs = gather_rows(pairs_block)
        w_self = own_heads(self_out, here)
        w_cross = own_heads(cross_out, here)
    w_up = gather_rows(side_by_side(exchange(deal(ffn_in, row_count // WAYS), here)))
    w_down = gather_rows(
        side_by_side(exchange(ffn_out.reshape(WAYS, chunk, ffn_out.shape[1]), here))
    )

    segments = frame_segments[0]
    clips = text_lengths.shape[1]
    ends = jnp.cumsum(text_lengths[0])
    clip = jnp.arange(clips, dtype=jnp.int32)
    begins = jnp.sum((segments[None, :] < clip[:, None]).astype(jnp.int32), axis=1)
    same = (segments[None, :] == clip[:, None]).astype(jnp.int32)
    marks = jnp.stack(
        [
            jnp.sum(same * begins[:, None], axis=0),
            jnp.sum(same * (ends - text_lengths[0])[:, None], axis=0),
            jnp.sum(same * ends[:, None], axis=0),
        ]
    )
    marks = jnp.concatenate([marks, jnp.zeros((5, count), jnp.int32)], axis=0)

    frames_wide = frames[0].astype(WIDE)
    one, hat_one, inverse_one = norm_forward(frames_wide, gains[0], biases[0])
    one_all = gather_slots(one)
    mixed = mm(one_all, w_mixed).astype(LOW)
    self_flops = count * count * inner * 2 * 5 // 8
    self_att, self_lse = call(
        self_forward,
        [shaped((count, inner), LOW), shaped((4, count), WIDE)],
        (here_low, marks, mixed),
        flops=2 * self_flops,
        exps=count * count * 5 // 2,
    )
    hidden = frames_wide + scatter_slots(self_att, w_self, 0)
    two, hat_two, inverse_two = norm_forward(hidden, gains[1], biases[1])
    two_all = gather_slots(two)
    query = mm(two_all, w_query).astype(LOW)
    text_all = gather_slots(text_states[0])
    text_count = text_all.shape[0]
    text_pairs = mm(text_all, w_pairs).astype(LOW)
    cross_flops = count * text_count * inner * 2
    cross_att, cross_lse = call(
        cross_forward,
        [shaped((count, inner), LOW), shaped((4, count), WIDE)],
        (here_low, marks, query, text_pairs),
        flops=2 * cross_flops,
        exps=count * text_count * 4,
    )
    hidden_two = hidden + scatter_slots(cross_att, w_cross, 0)
    three, hat_three, inverse_three = norm_forward(hidden_two, gains[2], biases[2])
    three_all = gather_slots(three)
    up = mm(three_all, w_up)
    phi = 0.5 * (1.0 + lax.erf(up * math.sqrt(0.5)))
    activ = (up * phi).astype(LOW)
    output = (hidden_two + scatter_slots(activ, w_down, 0)).astype(LOW)

    grad_all = gather_slots(out_grad[0])
    g_down = mm(activ, grad_all, 0, 0).astype(LOW)
    slope = phi + up * (jnp.exp(-0.5 * up * up) * (1.0 / math.sqrt(2.0 * math.pi)))
    grad_up = (mm(grad_all, w_down, 1, 1) * slope).astype(LOW)
    g_up = mm(three_all, grad_up, 0, 0).astype(LOW)
    part, gain_three, bias_three = norm_backward(
        scatter_slots(grad_up, w_up, 1), hat_three, inverse_three, gains[2]
    )
    grad_two = out_grad[0].astype(WIDE) + part
    branch_two = gather_slots(grad_two.astype(LOW))
    grad_cross = mm(branch_two, w_cross, 1, 1).astype(LOW)
    g_cross = mm(cross_att, branch_two, 0, 0).astype(LOW)
    grad_query, grad_pairs = call(
        cross_backward,
        [shaped((count, inner), LOW), shaped((text_count, 2 * inner), LOW)],
        (here_low, marks, query, text_pairs, grad_cross, cross_lse),
        flops=5 * cross_flops,
        exps=count * text_count * 4,
    )
    g_query = mm(two_all, grad_query, 0, 0).astype(LOW)
    g_pairs = mm(text_all, grad_pairs, 0, 0).astype(LOW)
    text_grad = scatter_slots(grad_pairs, w_pairs, 1)
    part, gain_two, bias_two = norm_backward(
        scatter_slots(grad_query, w_query, 1), hat_two, inverse_two, gains[1]
    )
    grad_hidden = grad_two + part
    branch = gather_slots(grad_hidden.astype(LOW))
    grad_self = mm(branch, w_self, 1, 1).astype(LOW)
    g_self = mm(self_att, branch, 0, 0).astype(LOW)
    (grad_mixed,) = call(
        self_backward,
        [shaped((count, 3 * inner), LOW)],
        (here_low, marks, mixed, grad_self, self_lse),
        scratch=[pltpu.VMEM((count, 128), WIDE), pltpu.VMEM((count, 128), WIDE)],
        flops=5 * self_flops,
        exps=count * count * 5 // 2,
    )
    g_mixed = mm(one_all, grad_mixed, 0, 0).astype(LOW)
    part, gain_one, bias_one = norm_backward(
        scatter_slots(grad_mixed, w_mixed, 1), hat_one, inverse_one, gains[0]
    )
    frame_grad = grad_hidden + part

    norm_sums = jnp.stack([gain_one, gain_two, gain_three, bias_one, bias_two, bias_three])
    split = norm_sums.reshape(6, 2, 2, inner)
    split = pick(split, here & 1, 2) + swap(pick(split, 1 - (here & 1), 2), 1)
    norm_sums = pick(split, here >> 1, 1) + swap(pick(split, 1 - (here >> 1), 1), 2)
    mask = 1
    while mask < row_count:
        norm_sums = norm_sums + row_swap(norm_sums, mask)
        mask = 2 * mask

    d_down = exchange(apart(sum_rows(g_down)), here).reshape(ffn_out.shape).astype(WIDE)
    d_up = undeal(exchange(apart(sum_rows(g_up)), here), row_count // WAYS).astype(WIDE)
    if grid:
        d_self, d_cross = lower_heads([g_self, g_cross], here, row)
        other = sum_grid(jnp.concatenate([g_query, g_pairs], axis=1), row).astype(LOW)
        s_query, s_pairs = other[:, :inner], other[:, inner:]
        s_mixed = sum_grid(g_mixed, row).astype(LOW)
    else:
        d_cross = return_heads(g_cross, here).astype(WIDE)
        d_self = return_heads(g_self, here).astype(WIDE)
        s_query, s_pairs, s_mixed = sum_rows(g_query), sum_rows(g_pairs), sum_rows(g_mixed)
    parts = exchange(jnp.concatenate([apart(s_query), apart(s_pairs)], axis=2), here)
    d_query = undeal(parts[:, :, :piece], 1).astype(WIDE)
    d_pairs = undeal(parts[:, :, piece:], 2).astype(WIDE)
    d_mixed = undeal(exchange(apart(s_mixed), here), 3).astype(WIDE)
    return (
        output[None],
        frame_grad[None],
        text_grad[None],
        d_mixed,
        d_self,
        d_query,
        d_pairs,
        d_cross,
        d_up,
        d_down,
        norm_sums[:3],
        norm_sums[3:],
    )


def solution(mesh):
    in_specs = (
        P("rows", "text", None),
        P("rows", "text", None),
        P("rows", None),
        P("rows", None),
        P("rows", "text"),
        P("rows", "text"),
        P("rows", "text"),
        P("rows", "text"),
        P("rows", "text"),
        P("rows", "text"),
        P("rows", "text"),
        P(None, "text"),
        P(None, "text"),
        P("rows", "text", None),
    )
    out_specs = (
        P("rows", "text", None),
        P("rows", "text", None),
        P("rows", "text", None),
        P("rows", "text"),
        P("rows", "text"),
        P("rows", "text"),
        P("rows", "text"),
        P("rows", "text"),
        P("rows", "text"),
        P("rows", "text"),
        P(None, "text"),
        P(None, "text"),
    )
    return jax.shard_map(local, mesh=mesh, in_specs=in_specs, out_specs=out_specs, check_vma=False)
```

```python
import functools
import math

import jax
import jax.numpy as jnp
from jax import lax
from jax.experimental import pallas as pl
from jax.experimental.pallas import tpu as pltpu
from jax.sharding import PartitionSpec as P

HEADS = 16
WAYS = 4
SLOTS = (0, 2, 1, 3)
LOW = jnp.bfloat16
WIDE = jnp.float32
NEVER = -1e30


def mm(left, right, left_dim=1, right_dim=0):
    return lax.dot_general(
        left, right, (((left_dim,), (right_dim,)), ((), ())), preferred_element_type=WIDE
    )


def swap(values, mask):
    return lax.ppermute(values, "text", [(i, i ^ mask) for i in range(WAYS)])


def after(value, *events):
    return lax.optimization_barrier((value,) + events)[0]


def copy_all(pairs, sem):
    copies = [pltpu.make_async_copy(*pair, sem.at[i]) for i, pair in enumerate(pairs)]
    for copy in copies:
        copy.start()
    for copy in copies:
        copy.wait()


def join_rows(_, *refs):
    *blocks, whole, sem = refs
    size = whole.shape[0] // len(blocks)
    copy_all(
        [(block, whole.at[i * size : (i + 1) * size]) for i, block in enumerate(blocks)], sem
    )


def join(ids, *blocks):
    rows = sum(b.shape[0] for b in blocks)
    (whole,) = call(
        join_rows,
        [shaped((rows, blocks[0].shape[1]), LOW)],
        (ids, *blocks),
        own_copies=len(blocks),
    )
    return whole


def sync(*values):
    return lax.optimization_barrier(values)


def gather_slots(block, ids, *beside):
    near = swap(block, 1)
    far, *beside = sync(swap(block, 2), *beside)
    whole = join(ids, block, far, near, swap(far, 1))
    return (whole, *beside) if beside else whole


def scatter_slots(left, right, right_dim, gate=None, beside=()):
    half = left.shape[0] // 2
    block = half // 2
    away = mm(left[half:], right, 1, right_dim).astype(LOW)
    near = swap(away, 1)
    far = (mm(left[block:half], right, 1, right_dim) + near[block:].astype(WIDE)).astype(LOW)
    if gate is not None:
        far = after(far, gate)
    far, *beside = sync(swap(far, 2), *beside)
    here = mm(left[:block], right, 1, right_dim) + near[:block].astype(WIDE)
    result = here + far.astype(WIDE)
    return (result, *beside) if beside else result


def gather_pair(block, ids):
    return join(ids, block, swap(block, 1))


def scatter_pair(left, right, right_dim):
    half = left.shape[0] // 2
    away = mm(left[half:], right, 1, right_dim).astype(LOW)
    return mm(left[:half], right, 1, right_dim) + swap(away, 1).astype(WIDE)


def norm_forward(values, gain, bias):
    average = jnp.mean(values, axis=-1, keepdims=True)
    centred = values - average
    spread = jnp.mean(centred * centred, axis=-1, keepdims=True)
    inverse = lax.rsqrt(spread + 1e-05)
    hat = centred * inverse
    return (hat * gain + bias).astype(LOW), hat, inverse


def norm_backward(grad, hat, inverse, gain):
    weighted = grad * gain
    first = jnp.mean(weighted, axis=-1, keepdims=True)
    second = jnp.mean(weighted * hat, axis=-1, keepdims=True)
    return (
        (weighted - first - hat * second) * inverse,
        jnp.sum(grad * hat, axis=0),
        jnp.sum(grad, axis=0),
    )


def slot_of(index, here):
    other = index ^ here
    return ((other & 1) << 1) | (other >> 1)


def half_lanes(values, head):
    lane = lax.broadcasted_iota(jnp.int32, values.shape, 1)
    keep = (lane < 64) if head == 0 else (lane >= 64)
    return jnp.where(keep, values, jnp.zeros_like(values))


def nt(left, right):
    return mm(left, right, 1, 1)


def rows_at(ref, slot, size, pair, offset):
    start = pl.multiple_of(slot * size, size)
    return ref[pl.ds(start, size), offset + pair * 128 : offset + (pair + 1) * 128]


def transposed(values):
    return values.astype(WIDE).T


def self_forward(here_ref, marks_ref, mixed_ref, out_ref, lse_ref):
    here = here_ref[0]
    size = mixed_ref.shape[0] // WAYS
    down = lax.broadcasted_iota(jnp.int32, (size, size), 0)
    across = lax.broadcasted_iota(jnp.int32, (size, size), 1)
    for pair in range(2):
        keys = [rows_at(mixed_ref, slot_of(j, here), size, pair, 256) for j in range(WAYS)]
        values_t = [
            transposed(rows_at(mixed_ref, slot_of(j, here), size, pair, 512)).astype(LOW)
            for j in range(WAYS)
        ]
        for i in range(WAYS):
            mine = slot_of(i, here)
            query = rows_at(mixed_ref, mine, size, pair, 0) * LOW(0.125)
            first = marks_ref[0:1, i * size : (i + 1) * size]
            outs = []
            for head in range(2):
                scores = []
                for j in range(i + 1):
                    s = nt(half_lanes(keys[j], head), query)
                    allowed = (down + j * size) >= first
                    if j == i:
                        allowed = allowed & (down <= across)
                    scores.append(jnp.where(allowed, s, NEVER))
                top = jnp.max(scores[0], axis=0, keepdims=True)
                for s in scores[1:]:
                    top = jnp.maximum(top, jnp.max(s, axis=0, keepdims=True))
                total = jnp.zeros_like(top)
                result = jnp.zeros((64, size), WIDE)
                for j, s in enumerate(scores):
                    probs = jnp.exp(s - top)
                    total = total + jnp.sum(probs, axis=0, keepdims=True)
                    part = values_t[j][head * 64 : (head + 1) * 64]
                    result = result + mm(part, probs.astype(LOW))
                outs.append(result / total)
                lse_ref[2 * pair + head : 2 * pair + head + 1, i * size : (i + 1) * size] = (
                    top + jnp.log(total)
                )
            start = pl.multiple_of(mine * size, size)
            out_ref[pl.ds(start, size), pair * 128 : (pair + 1) * 128] = (
                jnp.concatenate(outs, axis=0).T.astype(LOW)
            )


def self_backward(here_ref, marks_ref, mixed_ref, grad_ref, lse_ref, out_ref, dk_ref, dv_ref):
    here = here_ref[0]
    size = mixed_ref.shape[0] // WAYS
    down = lax.broadcasted_iota(jnp.int32, (size, size), 0)
    across = lax.broadcasted_iota(jnp.int32, (size, size), 1)
    for pair in range(2):
        keys = [rows_at(mixed_ref, slot_of(j, here), size, pair, 256) for j in range(WAYS)]
        values = [rows_at(mixed_ref, slot_of(j, here), size, pair, 512) for j in range(WAYS)]
        keys_t = [transposed(k).astype(LOW) for k in keys]
        for i in reversed(range(WAYS)):
            mine = slot_of(i, here)
            query = rows_at(mixed_ref, mine, size, pair, 0) * LOW(0.125)
            grad = rows_at(grad_ref, mine, size, pair, 0)
            first = marks_ref[0:1, i * size : (i + 1) * size]
            grads_q = []
            dk_parts = [None] * (i + 1)
            dv_parts = [None] * (i + 1)
            for head in range(2):
                mass = lse_ref[2 * pair + head : 2 * pair + head + 1, i * size : (i + 1) * size]
                grad_head = half_lanes(grad, head)
                query_head = half_lanes(query, head)
                probs, grad_probs = [], []
                delta = jnp.zeros((1, size), WIDE)
                for j in range(i + 1):
                    s = nt(half_lanes(keys[j], head), query)
                    allowed = (down + j * size) >= first
                    if j == i:
                        allowed = allowed & (down <= across)
                    p = jnp.exp(jnp.where(allowed, s, NEVER) - mass)
                    dp = nt(half_lanes(values[j], head), grad)
                    delta = delta + jnp.sum(p * dp, axis=0, keepdims=True)
                    probs.append(p)
                    grad_probs.append(dp)
                grad_q = jnp.zeros((64, size), WIDE)
                for j in range(i + 1):
                    ds = (probs[j] * (grad_probs[j] - delta)).astype(LOW)
                    dv = mm(probs[j].astype(LOW), grad_head)
                    dk = mm(ds, query_head)
                    dv_parts[j] = dv if head == 0 else dv_parts[j] + dv
                    dk_parts[j] = dk if head == 0 else dk_parts[j] + dk
                    grad_q = grad_q + mm(keys_t[j][head * 64 : (head + 1) * 64], ds)
                grads_q.append(grad_q)
            start = pl.multiple_of(mine * size, size)
            out_ref[pl.ds(start, size), pair * 128 : (pair + 1) * 128] = (
                (jnp.concatenate(grads_q, axis=0) * 0.125).T.astype(LOW)
            )
            for j in range(i + 1):
                rows = slice(j * size, (j + 1) * size)
                if i == WAYS - 1:
                    dk_ref[rows] = dk_parts[j]
                    dv_ref[rows] = dv_parts[j]
                else:
                    dk_ref[rows] = dk_ref[rows] + dk_parts[j]
                    dv_ref[rows] = dv_ref[rows] + dv_parts[j]
        for j in range(WAYS):
            rows = slice(j * size, (j + 1) * size)
            start = pl.multiple_of(slot_of(j, here) * size, size)
            out_ref[pl.ds(start, size), 256 + pair * 128 : 256 + (pair + 1) * 128] = dk_ref[
                rows
            ].astype(LOW)
            out_ref[pl.ds(start, size), 512 + pair * 128 : 512 + (pair + 1) * 128] = dv_ref[
                rows
            ].astype(LOW)


def token_places(here, count, width):
    row = lax.broadcasted_iota(jnp.int32, (count, width), 0)
    size = count // WAYS
    place = row
    for slot, mask in enumerate(SLOTS):
        inside = (row >= slot * size) & (row < (slot + 1) * size)
        place = jnp.where(inside, row - slot * size + (here ^ mask) * size, place)
    return place


def text_allowed(here, marks_ref, block, size, count):
    start = pl.multiple_of((here ^ block) * size, size)
    low = marks_ref[1:2, pl.ds(start, size)]
    high = marks_ref[2:3, pl.ds(start, size)]
    places = [token_places(here, count, size), token_places(here ^ 2, count, size)]
    return [(place >= low) & (place < high) for place in places]


def cross_forward(here_ref, marks_ref, query_ref, own_ref, other_ref, out_ref, lse_ref):
    here = here_ref[0]
    size = query_ref.shape[0] // 2
    allowed = [text_allowed(here, marks_ref, b, size, own_ref.shape[0]) for b in range(2)]
    for pair in range(4):
        ref = (own_ref, other_ref)[pair // 2]
        column = (pair % 2) * 128
        keys = ref[:, column : column + 128]
        values_t = transposed(ref[:, 256 + column : 384 + column]).astype(LOW)
        for block in range(2):
            rows = slice(block * size, (block + 1) * size)
            query = query_ref[rows, pair * 128 : (pair + 1) * 128] * LOW(0.125)
            outs = []
            for head in range(2):
                s = nt(half_lanes(keys, head), query)
                s = jnp.where(allowed[block][pair // 2], s, NEVER)
                top = jnp.max(s, axis=0, keepdims=True)
                probs = jnp.exp(s - top)
                total = jnp.sum(probs, axis=0, keepdims=True)
                result = mm(values_t[head * 64 : (head + 1) * 64], probs.astype(LOW))
                outs.append(result / total)
                lse_ref[2 * pair + head : 2 * pair + head + 1, rows] = top + jnp.log(total)
            out_ref[rows, pair * 128 : (pair + 1) * 128] = (
                jnp.concatenate(outs, axis=0).T.astype(LOW)
            )


def cross_backward(
    here_ref, marks_ref, query_ref, own_ref, other_ref, grad_ref, lse_ref, dq_ref, down_ref, dother_ref
):
    here = here_ref[0]
    size = query_ref.shape[0] // 2
    allowed = [text_allowed(here, marks_ref, b, size, own_ref.shape[0]) for b in range(2)]
    for pair in range(4):
        ref, out = ((own_ref, down_ref), (other_ref, dother_ref))[pair // 2]
        column = (pair % 2) * 128
        keys = ref[:, column : column + 128]
        values = ref[:, 256 + column : 384 + column]
        keys_t = transposed(keys).astype(LOW)
        sum_k = jnp.zeros(keys.shape, WIDE)
        sum_v = jnp.zeros(keys.shape, WIDE)
        for block in range(2):
            rows = slice(block * size, (block + 1) * size)
            query = query_ref[rows, pair * 128 : (pair + 1) * 128] * LOW(0.125)
            grad = grad_ref[rows, pair * 128 : (pair + 1) * 128]
            grads_q = []
            for head in range(2):
                mass = lse_ref[2 * pair + head : 2 * pair + head + 1, rows]
                s = nt(half_lanes(keys, head), query)
                p = jnp.exp(jnp.where(allowed[block][pair // 2], s, NEVER) - mass)
                dp = nt(half_lanes(values, head), grad)
                delta = jnp.sum(p * dp, axis=0, keepdims=True)
                ds = (p * (dp - delta)).astype(LOW)
                sum_v = sum_v + mm(p.astype(LOW), half_lanes(grad, head))
                sum_k = sum_k + mm(ds, half_lanes(query, head))
                grads_q.append(mm(keys_t[head * 64 : (head + 1) * 64], ds))
            dq_ref[rows, pair * 128 : (pair + 1) * 128] = (
                (jnp.concatenate(grads_q, axis=0) * 0.125).T.astype(LOW)
            )
        out[:, column : column + 128] = sum_k.astype(LOW)
        out[:, 256 + column : 384 + column] = sum_v.astype(LOW)


def bring_in(body, number, ids_ref, *refs):
    scratch, sem = refs[len(refs) - number - 1 : -1], refs[-1]
    copies = [
        pltpu.make_async_copy(refs[i], scratch[i], sem.at[i]) for i in range(number)
    ]
    for copy in copies:
        copy.start()
    for copy in copies:
        copy.wait()
    body(ids_ref, *scratch, *refs[number : len(refs) - number - 1])


def call(body, outs, operands, scratch=(), resident=False, own_copies=0):
    vmem = pl.BlockSpec(memory_space=pltpu.VMEM)
    spec = vmem if resident else pl.BlockSpec(memory_space=pl.ANY)
    scratch = list(scratch)
    if own_copies:
        scratch.append(pltpu.SemaphoreType.DMA((own_copies,)))
    elif not resident:
        scratch = [pltpu.VMEM(v.shape, v.dtype) for v in operands[1:]]
        scratch.append(pltpu.SemaphoreType.DMA((len(scratch),)))
        body = functools.partial(bring_in, body, len(operands) - 1)
    moved = sum(v.size * v.dtype.itemsize for v in (*operands, *outs))
    return pl.pallas_call(
        body,
        out_shape=outs,
        in_specs=[pl.BlockSpec(memory_space=pltpu.SMEM)] + [spec for v in operands[1:]],
        out_specs=[vmem for v in outs],
        scratch_shapes=scratch,
        cost_estimate=pl.CostEstimate(flops=0, bytes_accessed=moved, transcendentals=0),
        compiler_params=pltpu.CompilerParams(vmem_limit_bytes=48 << 20),
    )(*operands)


def weight_block(row_ref, left, right, last_ref, first_ref, kept_ref):
    step = pl.program_id(0)
    value = mm(left[...], right[...], 0, 0).astype(LOW)

    @pl.when(step < 2)
    def _():
        last_ref[0] = value

    @pl.when((step >= 2) & (step < 4))
    def _():
        first_ref[0] = value

    @pl.when(step >= 4)
    def _():
        kept_ref[0] = value


def weight_grad(row, left, right):
    count, rows = left.shape
    columns = right.shape[1]
    tile = rows // 8

    def owner(step, row_ref):
        k = jnp.where(step < 4, step ^ 2, step - 4)
        away = jnp.where(step < 4, 1, 0)
        return row_ref[0] ^ (2 * k) ^ away

    def parked(first, number):
        return pl.BlockSpec(
            (1, tile, columns), lambda s, r: (jnp.clip(s - first, 0, number - 1), 0, 0)
        )

    return pl.pallas_call(
        weight_block,
        grid_spec=pltpu.PrefetchScalarGridSpec(
            num_scalar_prefetch=1,
            grid=(8,),
            in_specs=[
                pl.BlockSpec((count, tile), lambda s, r: (0, owner(s, r))),
                pl.BlockSpec((count, columns), lambda s, r: (0, 0)),
            ],
            out_specs=[parked(0, 2), parked(2, 2), parked(4, 4)],
        ),
        out_shape=[shaped((n, tile, columns), LOW) for n in (2, 2, 4)],
        cost_estimate=pl.CostEstimate(
            flops=2 * count * rows * columns,
            bytes_accessed=2 * count * (rows + columns) + 2 * rows * columns,
            transcendentals=0,
        ),
        compiler_params=pltpu.CompilerParams(vmem_limit_bytes=48 << 20),
    )(row.astype(jnp.int32).reshape(1), left, right)


def shaped(shape, dtype):
    return jax.ShapeDtypeStruct(shape, dtype)


def deal(matrix, groups):
    depth, width = matrix.shape
    piece = width // (groups * WAYS)
    return jnp.moveaxis(matrix.reshape(depth, groups, WAYS, piece), 2, 0).reshape(
        WAYS, depth, groups * piece
    )


def undeal(dealt, groups):
    _, depth, width = dealt.shape
    return jnp.moveaxis(dealt.reshape(WAYS, depth, groups, width // groups), 0, 2).reshape(
        depth, WAYS * width
    )


def pick(values, index, axis):
    return lax.dynamic_index_in_dim(values, index, axis, keepdims=False)


def ordered(mine, other, bit, axis=0):
    return jnp.stack([jnp.where(bit == 0, mine, other), jnp.where(bit == 0, other, mine)], axis)


def exchange(dealt, here, *gates):
    core, far = here & 1, here >> 1
    tail = dealt.shape[1:]
    dealt = dealt.reshape((2, 2) + tail)
    stage = ordered(pick(dealt, core, 1), swap(pick(dealt, 1 - core, 1), 1), core, 1)
    sent = pick(stage, 1 - far, 0)
    if gates:
        sent = after(sent, *gates)
    return ordered(pick(stage, far, 0), swap(sent, 2), far).reshape((WAYS,) + tail)


def side_by_side(parts):
    return jnp.moveaxis(parts, 0, 1).reshape(parts.shape[1], -1)


def apart(columns):
    depth, width = columns.shape
    return jnp.moveaxis(columns.reshape(depth, WAYS, width // WAYS), 1, 0)


def row_swap(values, mask):
    size = lax.axis_size("rows")
    return lax.ppermute(values, "rows", [(i, i ^ mask) for i in range(size)])


def gather_rows(block):
    return lax.all_gather(block, "rows", axis=0, tiled=True)


def sum_rows(whole):
    return lax.psum_scatter(whole, "rows", scatter_dimension=0, tiled=True)


def place_pieces(depth, splits, ids_ref, *refs):
    row, outs, sem = ids_ref[1], refs[7:-1], refs[-1]
    pairs = []
    for k in range(4):
        for flip in range(2):
            owner = (row ^ flip) ^ (2 * k)
            start = pl.multiple_of(owner * depth, depth)
            column = 0
            for index, width in enumerate(splits):
                columns = slice(column, column + width)
                if not flip:
                    piece = refs[k].at[:, columns]
                elif k < 2:
                    piece = refs[4 + k].at[:, columns]
                else:
                    piece = refs[6].at[k - 2, :, columns]
                pairs.append((piece, outs[index].at[pl.ds(start, depth)]))
                column += width
    copy_all(pairs, sem)


def place(ids, splits, pieces, others):
    depth = pieces[0].shape[0]
    return call(
        functools.partial(place_pieces, depth, splits),
        [shaped((8 * depth, width), LOW) for width in splits],
        (ids, *pieces, *others),
        own_copies=8 * len(splits),
    )


def place_line_pieces(ids_ref, *refs):
    far = ids_ref[1] >> 1
    height = refs[0].shape[0]
    pairs = []
    for k in range(4):
        start = pl.multiple_of((far ^ k) * height, height)
        pairs.append((refs[k], refs[4].at[pl.ds(start, height)]))
    copy_all(pairs, refs[5])


def place_line(ids, *pieces):
    whole = shaped((4 * pieces[0].shape[0], pieces[0].shape[1]), LOW)
    return call(place_line_pieces, [whole], (ids, *pieces), own_copies=4)[0]


def three_ways(block):
    return [row_swap(block, 2 * k) for k in range(1, 4)]


def split_sums(row_ref, whole_ref, sent_ref, own_ref, *low_refs):
    row = row_ref[1]
    x, far = row & 1, row >> 1
    depth = own_ref.shape[0]
    for k in range(4):
        owner = far ^ k
        start = pl.multiple_of((owner * 2 + x) * depth, depth)
        value = whole_ref[pl.ds(start, depth)].astype(WIDE) + sent_ref[owner].astype(WIDE)
        if k == 0:
            own_ref[...] = value
        else:
            low_refs[k - 1][...] = value.astype(LOW)


def choose(bit, zero, one):
    return jnp.where(bit == 0, zero, one)


def put(ref, column, *values):
    for value in values:
        ref[:, column : column + value.shape[1]] = value.astype(ref.dtype)
        column += value.shape[1]


def total(refs):
    value = refs[0][...]
    for ref in refs[1:]:
        value = value + ref[...].astype(WIDE)
    return value


def device_bits(ids_ref):
    here, row = ids_ref[0], ids_ref[1]
    return here & 1, here >> 1, row & 1, row >> 1


def keep_and_send(kept, sent, column, bit, zero, one):
    put(kept, column, choose(bit, zero, one))
    put(sent, column, choose(bit, one, zero))
    return column + zero.shape[1]


def deal_first_core(ids, self_in, self_out, cross_out, kept, sent):
    core, _, _, _ = device_bits(ids)
    column = 0
    for y in range(2):
        for j in range(3):
            first = (4 * j + 2 * y) * 64
            zero, one = self_in[:, first : first + 64], self_in[:, first + 64 : first + 128]
            column = keep_and_send(kept, sent, column, core, zero, one)
    for index, ref in enumerate((self_out, cross_out)):
        rows = slice(64 * index, 64 * (index + 1))
        kept[rows, column:] = choose(core, ref[:64], ref[64:])
        sent[rows, column:] = choose(core, ref[64:], ref[:64])


def deal_first_far(ids, kept, came, far_kept, far_sent):
    core, y, _, _ = device_bits(ids)
    column = 0
    sources = [choose(core, kept[...], came[...]), choose(core, came[...], kept[...])]
    for source in sources:
        column = keep_and_send(far_kept, far_sent, column, y, source[:, :192], source[:, 192:384])
    for source in sources:
        put(far_kept, column, source[:, 384:])
        put(far_sent, column, source[:, 384:])
        column += 256


def deal_first_last(ids, kept, came, mixed, lines):
    _, y, _, _ = device_bits(ids)
    zero, one = choose(y, kept[...], came[...]), choose(y, came[...], kept[...])
    put(mixed, 0, zero[:, :384], one[:, :384])
    put(lines, 0, zero[:, 384:], one[:, 384:])


def deal_rest_core(ids, query, pairs, up, down, kept, sent):
    core, _, _, _ = device_bits(ids)
    column = 0
    for y in range(2):
        for r in range(2):
            first = (4 * r + 2 * y) * 128
            zero, one = up[:, first : first + 128], up[:, first + 128 : first + 256]
            column = keep_and_send(kept, sent, column, core, zero, one)
    for y in range(2):
        zero, one = [down[(2 * y + c) * 128 : (2 * y + c + 1) * 128] for c in range(2)]
        column = keep_and_send(kept, sent, column, core, zero, one)
    for y in range(2):
        for j in range(2):
            first = (4 * j + 2 * y) * 64
            zero, one = pairs[:, first : first + 64], pairs[:, first + 64 : first + 128]
            column = keep_and_send(kept, sent, column, core, zero, one)
    for y in range(2):
        zero, one = query[:, 128 * y : 128 * y + 64], query[:, 128 * y + 64 : 128 * y + 128]
        column = keep_and_send(kept, sent, column, core, zero, one)


def deal_rest_far(ids, kept, came, far_kept, far_sent):
    core, y, _, _ = device_bits(ids)
    sources = [choose(core, kept[...], came[...]), choose(core, came[...], kept[...])]
    column = 0
    for first, width in ((0, 256), (512, 256), (1024, 128)):
        for source in sources:
            zero = source[:, first : first + width]
            one = source[:, first + width : first + 2 * width]
            column = keep_and_send(far_kept, far_sent, column, y, zero, one)
    for source in sources:
        put(far_kept, column, source[:, 1280:])
        put(far_sent, column, source[:, 1280:])
        column += 128


def deal_rest_last(ids, kept, came, attend, up, down):
    _, y, _, _ = device_bits(ids)
    sources = [choose(y, kept[...], came[...]), choose(y, came[...], kept[...])]
    put(up, 0, *[s[:, :512] for s in sources])
    put(down, 0, *[s[:, 512:1024] for s in sources])
    put(attend, 512, *[s[:, 1024:1280] for s in sources])
    for group in range(2):
        for place, source in enumerate(sources):
            for c in range(2):
                first = 1280 + c * 128
                zero = source[:, first + group * 64 : first + group * 64 + 64]
                one = source[:, first + (1 - group) * 64 : first + (1 - group) * 64 + 64]
                put(attend, group * 256 + (2 * place + c) * 64, choose(y, zero, one))


def ffn_far(ids, *refs):
    _, y, _, _ = device_bits(ids)
    kept, sent = refs[8:]
    for half in range(2):
        value = total(refs[4 * half : 4 * half + 4])
        put(kept, half * 512, choose(y, value[:, :512], value[:, 512:]))
        put(sent, half * 512, choose(y, value[:, 512:], value[:, :512]))


def ffn_core(ids, kept, came, core_kept, core_sent):
    core, y, _, _ = device_bits(ids)
    mine, other = kept[...], came[...].astype(WIDE)
    column = 0
    for source in (choose(y, mine, other), choose(y, other, mine)):
        for half in range(2):
            zero = source[:, half * 512 : half * 512 + 256]
            one = source[:, half * 512 + 256 : half * 512 + 512]
            put(core_kept, column, choose(core, zero, one))
            put(core_sent, column, choose(core, one, zero))
            column += 256


def ffn_last(ids, kept, came, up, down):
    core, _, _, _ = device_bits(ids)
    mine, other = kept[...], came[...].astype(WIDE)
    for c, source in enumerate((choose(core, mine, other), choose(core, other, mine))):
        for y in range(2):
            sender = 2 * y + c
            for r in range(2):
                first = 512 * y + 128 * r
                put(up, (4 * r + sender) * 128, source[:, first : first + 128])
            down[sender * 128 : (sender + 1) * 128] = source[:, 512 * y + 256 : 512 * y + 512]


def mixed_far(ids, own, a, b, c, kept, sent):
    _, y, _, _ = device_bits(ids)
    value = total((own, a, b, c))
    put(kept, 0, choose(y, value[:, :384], value[:, 384:]))
    put(sent, 0, choose(y, value[:, 384:], value[:, :384]))


def mixed_core(ids, kept, came, core_kept, core_sent):
    core, y, _, _ = device_bits(ids)
    mine, other = kept[...], came[...].astype(WIDE)
    for index, source in enumerate((choose(y, mine, other), choose(y, other, mine))):
        put(core_kept, 192 * index, choose(core, source[:, :192], source[:, 192:]))
        put(core_sent, 192 * index, choose(core, source[:, 192:], source[:, :192]))


def mixed_last(ids, kept, came, mixed):
    core, _, _, _ = device_bits(ids)
    mine, other = kept[...], came[...].astype(WIDE)
    for c, source in enumerate((choose(core, mine, other), choose(core, other, mine))):
        for y in range(2):
            for j in range(3):
                first = 192 * y + 64 * j
                put(mixed, (4 * j + 2 * y + c) * 64, source[:, first : first + 64])


def attend_x(ids, query, pairs, cross, sent):
    _, y, x, _ = device_bits(ids)
    for z in range(4):
        start = pl.multiple_of((2 * z + 1 - x) * 128, 128)
        line = pl.multiple_of(((y ^ x ^ 1) * 4 + z) * 64, 64)
        sent[z, :128, :512] = query[pl.ds(start, 128)]
        sent[z, :128, 512:] = pairs[pl.ds(start, 128)]
        sent[z, 128:] = cross[pl.ds(line, 64)]


def attend_z(ids, query, pairs, cross, self_out, came, own, a, b, c):
    _, y, x, z = device_bits(ids)
    for k, ref in enumerate((own, a, b, c)):
        owner = z ^ k
        start = pl.multiple_of((2 * owner + x) * 128, 128)
        line = pl.multiple_of(((y ^ x) * 4 + owner) * 64, 64)
        below = pl.multiple_of(owner * 64, 64)
        moved = came[owner].astype(WIDE)
        value = query[pl.ds(start, 128)].astype(WIDE) + moved[:128, :512]
        ref[:128, :512] = value.astype(ref.dtype)
        value = pairs[pl.ds(start, 128)].astype(WIDE) + moved[:128, 512:]
        ref[:128, 512:] = value.astype(ref.dtype)
        value = cross[pl.ds(line, 64)].astype(WIDE) + moved[128:]
        ref[128:192] = value.astype(ref.dtype)
        ref[192:] = self_out[pl.ds(below, 64)].astype(ref.dtype)


def attend_total(ids, own, a, b, c, value, line):
    value[...] = total((own, a, b, c))
    line[...] = value[192:].astype(LOW)


def attend_far(ids, value, line, kept, sent):
    _, y, _, _ = device_bits(ids)
    lines = jnp.concatenate([value[192:] + line[...].astype(WIDE), value[128:192]], axis=0)
    put(kept, 0, choose(y, lines[:, :512], lines[:, 512:]))
    put(sent, 0, choose(y, lines[:, 512:], lines[:, :512]))
    mine, other = value[:128, :256], value[:128, 256:512]
    for index, group in enumerate((choose(y, mine, other), choose(y, other, mine))):
        put(kept, 512 + 128 * index, choose(y, group[:, :128], group[:, 128:]))
        put(sent, 512 + 128 * index, choose(y, group[:, 128:], group[:, :128]))
    pairs = value[:128, 512:]
    put(kept, 768, choose(y, pairs[:, :256], pairs[:, 256:]))
    put(sent, 768, choose(y, pairs[:, 256:], pairs[:, :256]))


def attend_core(ids, kept, came, core_kept, core_sent):
    core, y, x, _ = device_bits(ids)
    mine, other = kept[...], came[...].astype(WIDE)
    owner = jnp.where(x == y, mine[:64, :512], other[:64, :512])
    lines = jnp.concatenate([owner, mine[64:, :512] + other[64:, :512]], axis=0)
    put(core_kept, 0, choose(core, lines[:, :256], lines[:, 256:]))
    put(core_sent, 0, choose(core, lines[:, 256:], lines[:, :256]))
    query = mine[:, 512:768] + other[:, 512:768]
    for group in range(2):
        zero, one = [query[:, 128 * group + 64 * c : 128 * group + 64 * c + 64] for c in range(2)]
        put(core_kept, 256 + 64 * group, choose(core, zero, one))
        put(core_sent, 256 + 64 * group, choose(core, one, zero))
    mine, other = mine[:, 768:], other[:, 768:]
    for index, source in enumerate((choose(y, mine, other), choose(y, other, mine))):
        put(core_kept, 384 + 128 * index, choose(core, source[:, :128], source[:, 128:]))
        put(core_sent, 384 + 128 * index, choose(core, source[:, 128:], source[:, :128]))


def attend_last(ids, kept, came, self_out, query, pairs, cross):
    core, _, _, _ = device_bits(ids)
    mine, other = kept[...], came[...].astype(WIDE)
    for c, source in enumerate((choose(core, mine, other), choose(core, other, mine))):
        self_out[64 * c : 64 * c + 64] = source[:64, :256]
        cross[64 * c : 64 * c + 64] = source[64:, :256]
        for y in range(2):
            put(query, 64 * (2 * y + c), source[:, 256 + 64 * y : 320 + 64 * y])
            for j in range(2):
                first = 384 + 128 * y + 64 * j
                put(pairs, 64 * (4 * j + 2 * y + c), source[:, first : first + 64])


def along_z(values):
    return [row_swap(v, 2 * (k + 1)) for k, v in enumerate(values)]


def add_parts(first, ids, kept, came, *outs):
    for index, out in enumerate(outs):
        value = kept[first + index].astype(WIDE) + came[index].astype(WIDE)
        out[...] = value.astype(out.dtype)


def return_ffn(ids, up, down):
    low = lambda *shape: shaped(shape, LOW)
    wide = lambda *shape: shaped(shape, WIDE)
    kept, sent = call(ffn_far, [wide(128, 1024), low(128, 1024)], (ids, *up, *down))
    kept, sent = call(ffn_core, [wide(128, 1024), low(128, 1024)], (ids, kept, swap(sent, 2)))
    return call(ffn_last, [wide(128, 1024), wide(512, 256)], (ids, kept, swap(sent, 1)))


def send_last(ids, kept, came):
    second, third = call(
        lambda *refs: add_parts(2, *refs), [shaped((128, 1024), LOW)] * 2, (ids, kept, came)
    )
    return row_swap(second, 4), row_swap(third, 6)


def send_first(ids, kept, came):
    own, part = call(
        lambda *refs: add_parts(0, *refs),
        [shaped((128, 1024), WIDE), shaped((128, 1024), LOW)],
        (ids, kept, came),
    )
    return own, row_swap(part, 2)


def return_mixed(ids, own, parts):
    low = lambda *shape: shaped(shape, LOW)
    wide = lambda *shape: shaped(shape, WIDE)
    kept, sent = call(mixed_far, [wide(128, 384), low(128, 384)], (ids, own, *parts))
    kept, sent = call(mixed_core, [wide(128, 384), low(128, 384)], (ids, kept, swap(sent, 2)))
    (mixed,) = call(mixed_last, [wide(128, 768)], (ids, kept, swap(sent, 1)))
    return mixed


def return_attend(ids, own, parts):
    low = lambda *shape: shaped(shape, LOW)
    wide = lambda *shape: shaped(shape, WIDE)
    value, line = call(attend_total, [wide(256, 1024), low(64, 1024)], (ids, own, *parts))
    kept, sent = call(
        attend_far, [wide(128, 1024), low(128, 1024)], (ids, value, row_swap(line, 1))
    )
    kept, sent = call(attend_core, [wide(128, 640), low(128, 640)], (ids, kept, swap(sent, 2)))
    return call(
        attend_last,
        [wide(128, 256), wide(128, 256), wide(128, 512), wide(128, 256)],
        (ids, kept, swap(sent, 1)),
    )


def own_heads(matrix, here):
    rows = gather_rows(lax.all_gather(matrix, "text", axis=1, tiled=True))
    width = rows.shape[1]
    grouped = rows.reshape(HEADS // WAYS, WAYS, -1, width)
    return pick(grouped, here, 1).reshape(-1, width)


def return_heads(grad, here):
    count, width = grad.shape
    spread = jnp.zeros((HEADS // WAYS, WAYS, count * WAYS // HEADS, width), grad.dtype)
    spread = lax.dynamic_update_index_in_dim(
        spread, grad.reshape(HEADS // WAYS, 1, -1, width), here, 1
    )
    columns = lax.psum_scatter(
        spread.reshape(count * WAYS, width), "text", scatter_dimension=1, tiled=True
    )
    return sum_rows(columns)


def mask_marks(segments, lengths):
    clip = jnp.arange(lengths.shape[0], dtype=jnp.int32)
    ends = jnp.sum(jnp.where(clip[None, :] <= clip[:, None], lengths[None, :], 0), axis=1)
    begins = jnp.sum((segments[None, :] < clip[:, None]).astype(jnp.int32), axis=1)
    same = (segments[None, :] == clip[:, None]).astype(jnp.int32)
    rows = [begins, ends - lengths, ends] + [jnp.zeros_like(ends)] * 5
    return jnp.stack([jnp.sum(same * values[:, None], axis=0) for values in rows])


def gelu_parts(up):
    phi = 0.5 * (1.0 + lax.erf(up * math.sqrt(0.5)))
    slope = phi + up * (jnp.exp(-0.5 * up * up) * (1.0 / math.sqrt(2.0 * math.pi)))
    return lax.optimization_barrier(((up * phi).astype(LOW), slope))


def reduce_norms(sums, here):
    split = sums.reshape(6, 2, 2, -1)
    split = pick(split, here & 1, 2) + swap(pick(split, 1 - (here & 1), 2), 1)
    sums = pick(split, here >> 1, 1) + swap(pick(split, 1 - (here >> 1), 1), 2)
    mask = 1
    while mask < lax.axis_size("rows"):
        sums = sums + row_swap(sums, mask)
        mask = 2 * mask
    return sums


def local_grid(
    frames,
    text_states,
    frame_segments,
    text_lengths,
    self_in,
    self_out,
    cross_query,
    cross_kv,
    cross_out,
    ffn_in,
    ffn_out,
    norm_gains,
    norm_biases,
    out_grad,
):
    here, row = lax.axis_index("text"), lax.axis_index("rows")
    ids = jnp.stack([here, row]).astype(jnp.int32)
    width = frames.shape[2]
    count = frames.shape[1] * WAYS
    inner = width // WAYS
    low = lambda *shape: shaped(shape, LOW)
    wide = lambda *shape: shaped(shape, WIDE)
    frames_wide = frames[0].astype(WIDE)
    marks = mask_marks(frame_segments[0], text_lengths[0])

    kept, sent = call(deal_first_core, [low(128, 640)] * 2, (ids, self_in, self_out, cross_out))
    norms = jnp.concatenate([norm_gains, norm_biases], axis=0)
    norms_far = swap(norms, 2)
    kept, sent = call(deal_first_far, [low(128, 896)] * 2, (ids, kept, swap(sent, 1)))
    norms = ordered(norms, norms_far, here >> 1)
    norms = ordered(norms, swap(norms, 1), here & 1, 1)
    norms = jnp.moveaxis(norms, 2, 0).reshape(6, width).astype(WIDE)
    gains, biases = norms[:3], norms[3:]
    one, hat_one, inverse_one = norm_forward(frames_wide, gains[0], biases[0])
    came = swap(sent, 2)
    rest = sync(cross_query, cross_kv, ffn_in, ffn_out, sent)[:4]
    rest_kept, rest_sent = call(deal_rest_core, [low(128, 1408)] * 2, (ids, *rest))
    rest_kept, rest_sent = call(
        deal_rest_far, [low(128, 1536)] * 2, (ids, rest_kept, swap(rest_sent, 1))
    )
    mixed, lines = call(deal_first_last, [low(128, 768), low(128, 1024)], (ids, kept, came))
    mixed, lines, rest_sent, one = sync(mixed, lines, rest_sent, one)
    mixed_z = three_ways(mixed)
    mixed_x = row_swap(mixed, 1)
    lines_x = row_swap(lines, 1)
    rest_came = swap(rest_sent, 2)
    one_far, one_near = swap(one, 2), swap(one, 1)
    attend, up_block, down_block = call(
        deal_rest_last, [low(128, 1024)] * 3, (ids, rest_kept, rest_came)
    )
    lines = jnp.where((row & 1) == (here >> 1), lines, lines_x)
    *mixed_z, mixed_x, attend, lines, text, grad = sync(
        *mixed_z, mixed_x, attend, lines, text_states[0], out_grad[0]
    )
    mixed_x1 = row_swap(mixed_z[0], 1)
    mixed_x2 = row_swap(jnp.stack(mixed_z[1:]), 1)
    self_line, cross_line = lines[:64], lines[64:]
    self_z = three_ways(sync(self_line, mixed_x1)[0])
    attend_z1 = row_swap(sync(attend, mixed_x1)[0], 2)
    one_all = join(ids, one, one_far, one_near, swap(one_far, 1))
    text_far, text_near = swap(text, 2), swap(text, 1)
    mixed_x1, mixed_x2, one_all, text_far, attend_z1, *self_z = sync(
        mixed_x1, mixed_x2, one_all, text_far, attend_z1, *self_z
    )
    (w_mixed,) = place(ids, (768,), [mixed, *mixed_z], [mixed_x, mixed_x1, mixed_x2])
    attend, grad, cross_line = sync(attend, grad, cross_line, mixed_x2)[:3]
    attend_z2, attend_z3 = row_swap(attend, 4), row_swap(attend, 6)
    attend_x0, attend_x1 = row_swap(attend, 1), row_swap(attend_z1, 1)
    grad_far, grad_near = swap(grad, 2), swap(grad, 1)
    mixed_low = mm(one_all, w_mixed).astype(LOW)
    w_self = place_line(ids, self_line, *self_z)
    text_all = join(ids, text, text_far, text_near, swap(text_far, 1))
    self_att, self_lse = call(
        self_forward, [low(count, inner), wide(4, count)], (ids, marks, mixed_low), resident=True
    )
    self_att, w_self, text_all, attend_x1, grad_far, attend_z2, attend_z3, cross_line = sync(
        self_att, w_self, text_all, attend_x1, grad_far, attend_z2, attend_z3, cross_line
    )
    attend_x2 = row_swap(jnp.stack([attend_z2, attend_z3]), 1)
    cross_z = three_ways(cross_line)
    received, attend_x2, *cross_z = scatter_slots(self_att, w_self, 0, None, (attend_x2, *cross_z))
    hidden = frames_wide + received
    w_query, w_pairs = place(
        ids,
        (512, 512),
        [attend, attend_z1, attend_z2, attend_z3],
        [attend_x0, attend_x1, attend_x2],
    )
    grad_all = join(ids, grad, grad_far, grad_near, swap(grad_far, 1))
    (up_block,) = sync(up_block, attend_x2)[:1]
    up_z = three_ways(up_block)
    up_x = row_swap(up_block, 1)
    two, hat_two, inverse_two = norm_forward(hidden, gains[1], biases[1])
    two_pair = gather_pair(two, ids)
    pair_count = two_pair.shape[0]
    text_count = text_all.shape[0]
    pairs_own = mm(text_all, w_pairs).astype(LOW)
    pairs_other = swap(pairs_own, 2)
    w_cross = place_line(ids, cross_line, *cross_z)
    w_cross_far = swap(sync(w_cross, pairs_own)[0], 2)
    query = mm(two_pair, w_query).astype(LOW)
    cross_att, cross_lse = call(
        cross_forward,
        [low(pair_count, 2 * inner), wide(8, pair_count)],
        (ids, marks, query, pairs_own, pairs_other),
        resident=True,
    )
    cross_att, *up_z = sync(cross_att, *up_z)
    (down_block,) = sync(down_block, up_z[2])[:1]
    up_x1 = row_swap(up_z[0], 1)
    up_x2 = row_swap(jnp.stack(up_z[1:]), 1)
    down_z = three_ways(down_block)
    down_x = row_swap(down_block, 1)
    w_cross_both = join(ids, w_cross, w_cross_far)
    hidden_two = hidden + scatter_pair(cross_att, w_cross_both, 0)
    three, hat_three, inverse_three = norm_forward(hidden_two, gains[2], biases[2])
    three_all, up_x1, up_x2 = gather_slots(three, ids, up_x1, up_x2)
    (w_up,) = place(ids, (1024,), [up_block, *up_z], [up_x, up_x1, up_x2])
    three_all, *down_z = sync(three_all, *down_z)
    down_x1 = row_swap(down_z[0], 1)
    down_x2 = row_swap(jnp.stack(down_z[1:]), 1)
    activ, slope = gelu_parts(mm(three_all, w_up))
    (w_down,) = place(ids, (1024,), [down_block, *down_z], [down_x, down_x1, down_x2])

    last_down, first_down, kept_down = weight_grad(row, activ, grad_all)
    last_down = row_swap(last_down, 1)
    first_down = row_swap(first_down, 1)
    grad_up = (mm(grad_all, w_down, 1, 1) * slope).astype(LOW)
    last_up, first_up, kept_up = weight_grad(row, three_all, grad_up)
    grad_three, last_down, last_up, first_up = scatter_slots(
        grad_up, w_up, 1, None, (last_down, last_up, first_up)
    )
    last_up = row_swap(last_up, 1)
    down_two, down_three = send_last(ids, kept_down, last_down)
    output = (hidden_two + scatter_slots(activ, w_down, 0, grad_three)).astype(LOW)
    part, gain_three, bias_three = norm_backward(grad_three, hat_three, inverse_three, gains[2])
    grad_two = out_grad[0].astype(WIDE) + part
    branch_two = gather_pair(grad_two.astype(LOW), ids)
    grad_cross = mm(branch_two, w_cross_both, 1, 1).astype(LOW)
    grad_cross, first_down, first_up, down_two, down_three = sync(
        grad_cross, first_down, first_up, down_two, down_three
    )
    first_up = row_swap(first_up, 1)
    down_own, down_one = send_first(ids, kept_down, first_down)
    grad_query, pairs_mine, pairs_away = call(
        cross_backward,
        [low(pair_count, 2 * inner)] + [low(text_count, 2 * inner)] * 2,
        (ids, marks, query, pairs_own, pairs_other, grad_cross, cross_lse),
        resident=True,
    )
    grad_query, pairs_away, last_up = sync(grad_query, pairs_away, last_up)
    pairs_came = swap(pairs_away, 2)
    up_two, up_three = send_last(ids, kept_up, last_up)
    g_cross = mm(cross_att, branch_two, 0, 0).astype(LOW)
    g_query = mm(two_pair, grad_query, 0, 0).astype(LOW)
    part, gain_two, bias_two = norm_backward(
        scatter_pair(grad_query, w_query, 1), hat_two, inverse_two, gains[1]
    )
    grad_hidden = grad_two + part
    grad_low, pairs_came, g_cross, g_query = sync(
        grad_hidden.astype(LOW), pairs_came, g_cross, g_query
    )
    grad_pairs = (pairs_mine.astype(WIDE) + pairs_came.astype(WIDE)).astype(LOW)
    g_pairs = mm(text_all, grad_pairs, 0, 0).astype(LOW)
    (attend_sent,) = call(attend_x, [low(4, 192, 1024)], (ids, g_query, g_pairs, g_cross))
    attend_came = row_swap(attend_sent, 1)
    branch, first_up, up_two, up_three, down_one = gather_slots(
        grad_low, ids, first_up, up_two, up_three, down_one
    )
    up_own, up_one = send_first(ids, kept_up, first_up)
    text_grad = scatter_slots(grad_pairs, w_pairs, 1, branch)
    grad_self = mm(branch, w_self, 1, 1).astype(LOW)
    g_self = mm(self_att, branch, 0, 0).astype(LOW)
    (grad_mixed,) = call(
        self_backward,
        [low(count, 3 * inner)],
        (ids, marks, mixed_low, grad_self, self_lse),
        scratch=[pltpu.VMEM((count, 128), WIDE), pltpu.VMEM((count, 128), WIDE)],
        resident=True,
    )
    grad_mixed, up_one = sync(grad_mixed, up_one)
    g_mixed = mm(one_all, grad_mixed, 0, 0).astype(LOW)
    mixed_sent = pick(g_mixed.reshape(4, 2, 128, 768), 1 - (row & 1), 1)
    mixed_sent, grad_mixed, attend_came = sync(mixed_sent, grad_mixed, attend_came)
    mixed_came = row_swap(mixed_sent, 1)
    attend_own, *attend_parts = call(
        attend_z,
        [wide(256, 1024)] + [low(256, 1024)] * 3,
        (ids, g_query, g_pairs, g_cross, g_self, attend_came),
    )
    attend_parts = along_z(attend_parts)
    grad_one, mixed_came = scatter_slots(grad_mixed, w_mixed, 1, None, (mixed_came,))
    mixed_own, *mixed_parts = call(
        split_sums, [wide(128, 768)] + [low(128, 768)] * 3, (ids, g_mixed, mixed_came)
    )
    attend_own, *attend_parts, _ = sync(attend_own, *attend_parts, mixed_own)
    mixed_parts = along_z(mixed_parts)
    part, gain_one, bias_one = norm_backward(grad_one, hat_one, inverse_one, gains[0])
    frame_grad = grad_hidden + part
    d_up, d_down = return_ffn(
        ids, (up_own, up_one, up_two, up_three), (down_own, down_one, down_two, down_three)
    )
    norm_sums = reduce_norms(
        jnp.stack([gain_one, gain_two, gain_three, bias_one, bias_two, bias_three]), here
    )
    d_self, d_query, d_pairs, d_cross = return_attend(ids, attend_own, attend_parts)
    d_mixed = return_mixed(ids, mixed_own, mixed_parts)
    return (
        output[None],
        frame_grad[None],
        text_grad[None],
        d_mixed,
        d_self,
        d_query,
        d_pairs,
        d_cross,
        d_up,
        d_down,
        norm_sums[:3],
        norm_sums[3:],
    )


def local_general(
    frames,
    text_states,
    frame_segments,
    text_lengths,
    self_in,
    self_out,
    cross_query,
    cross_kv,
    cross_out,
    ffn_in,
    ffn_out,
    norm_gains,
    norm_biases,
    out_grad,
):
    here = lax.axis_index("text")
    row = lax.axis_index("rows")
    ids = jnp.stack([here, row]).astype(jnp.int32)
    row_count = lax.axis_size("rows")
    width = frames.shape[2]
    count = frames.shape[1] * WAYS
    inner = width // WAYS

    chunk = ffn_out.shape[0] // WAYS
    norms = jnp.concatenate([norm_gains, norm_biases], axis=0)
    norms = ordered(norms, swap(norms, 2), here >> 1)
    norms = ordered(norms, swap(norms, 1), here & 1, 1)
    norms = jnp.moveaxis(norms, 2, 0).reshape(6, width).astype(WIDE)
    gains, biases = norms[:3], norms[3:]
    depth = ffn_in.shape[0]
    gate = norms
    w_mixed = gather_rows(side_by_side(exchange(deal(self_in, 3), here)))
    w_query = gather_rows(side_by_side(exchange(deal(cross_query, 1), here)))
    w_query = jnp.concatenate([w_query, swap(w_query, 2)], axis=1)
    w_pairs = gather_rows(side_by_side(exchange(deal(cross_kv, 2), here)))
    w_self = own_heads(self_out, here)
    w_cross = own_heads(cross_out, here)
    w_up = gather_rows(side_by_side(exchange(deal(ffn_in, row_count // WAYS), here)))
    w_down = ffn_out.reshape(WAYS, chunk, inner)
    w_down = gather_rows(side_by_side(exchange(w_down, here)))

    marks = mask_marks(frame_segments[0], text_lengths[0])

    frames_wide = frames[0].astype(WIDE)
    one, hat_one, inverse_one = norm_forward(frames_wide, gains[0], biases[0])
    one_all = gather_slots(after(one, gate), ids)
    text_all = gather_slots(after(text_states[0], one_all), ids)
    grad_all = gather_slots(after(out_grad[0], text_all), ids)
    one_all = after(one_all, text_all, grad_all)
    mixed = mm(one_all, w_mixed).astype(LOW)
    self_att, self_lse = call(
        self_forward,
        [shaped((count, inner), LOW), shaped((4, count), WIDE)],
        (ids, marks, mixed),
        resident=True,
    )
    hidden = frames_wide + scatter_slots(self_att, w_self, 0)
    two, hat_two, inverse_two = norm_forward(hidden, gains[1], biases[1])
    two_pair = gather_pair(two, ids)
    pair_count = two_pair.shape[0]
    text_count = text_all.shape[0]
    pairs_own = mm(text_all, w_pairs).astype(LOW)
    pairs_other = swap(pairs_own, 2)
    w_cross_both = join(ids, w_cross, swap(after(w_cross, pairs_other), 2))
    query = mm(two_pair, w_query).astype(LOW)
    cross_att, cross_lse = call(
        cross_forward,
        [shaped((pair_count, 2 * inner), LOW), shaped((8, pair_count), WIDE)],
        (ids, marks, query, pairs_own, pairs_other),
        resident=True,
    )
    hidden_two = hidden + scatter_pair(cross_att, w_cross_both, 0)
    three, hat_three, inverse_three = norm_forward(hidden_two, gains[2], biases[2])
    three_all = gather_slots(three, ids)
    up = mm(three_all, w_up)
    activ, slope = gelu_parts(up)

    grad_up = (mm(grad_all, w_down, 1, 1) * slope).astype(LOW)
    grad_three = scatter_slots(grad_up, w_up, 1)
    g_up = mm(three_all, grad_up, 0, 0).astype(LOW)
    g_down = mm(activ, grad_all, 0, 0).astype(LOW)
    output = (hidden_two + scatter_slots(activ, w_down, 0, grad_three)).astype(LOW)
    part, gain_three, bias_three = norm_backward(grad_three, hat_three, inverse_three, gains[2])
    grad_two = out_grad[0].astype(WIDE) + part
    branch_two = gather_pair(grad_two.astype(LOW), ids)
    grad_cross = mm(branch_two, w_cross_both, 1, 1).astype(LOW)
    g_cross = mm(cross_att, branch_two, 0, 0).astype(LOW)
    grad_query, pairs_mine, pairs_away = call(
        cross_backward,
        [shaped((pair_count, 2 * inner), LOW)] + [shaped((text_count, 2 * inner), LOW)] * 2,
        (ids, marks, query, pairs_own, pairs_other, grad_cross, cross_lse),
        resident=True,
    )
    part, gain_two, bias_two = norm_backward(
        scatter_pair(grad_query, w_query, 1), hat_two, inverse_two, gains[1]
    )
    grad_pairs = (pairs_mine.astype(WIDE) + swap(pairs_away, 2).astype(WIDE)).astype(LOW)
    g_query = mm(two_pair, grad_query, 0, 0).astype(LOW)
    g_pairs = mm(text_all, grad_pairs, 0, 0).astype(LOW)
    grad_hidden = grad_two + part
    grad_low = grad_hidden.astype(LOW)
    branch = gather_slots(grad_low, ids)
    text_grad = scatter_slots(grad_pairs, w_pairs, 1, branch)
    grad_self = mm(branch, w_self, 1, 1).astype(LOW)
    g_self = mm(self_att, branch, 0, 0).astype(LOW)
    (grad_mixed,) = call(
        self_backward,
        [shaped((count, 3 * inner), LOW)],
        (ids, marks, mixed, grad_self, self_lse),
        scratch=[pltpu.VMEM((count, 128), WIDE), pltpu.VMEM((count, 128), WIDE)],
        resident=True,
    )
    g_mixed = mm(one_all, grad_mixed, 0, 0).astype(LOW)
    part, gain_one, bias_one = norm_backward(
        scatter_slots(grad_mixed, w_mixed, 1), hat_one, inverse_one, gains[0]
    )
    frame_grad = grad_hidden + part

    norm_sums = reduce_norms(
        jnp.stack([gain_one, gain_two, gain_three, bias_one, bias_two, bias_three]), here
    )
    parts = jnp.concatenate([apart(sum_rows(g_up)), apart(sum_rows(g_down))], axis=1)
    parts = exchange(parts, here)
    d_up = undeal(parts[:, :depth], row_count // WAYS).astype(WIDE)
    d_down = parts[:, depth:].reshape(ffn_out.shape).astype(WIDE)
    g_query = g_query[:, :inner] + swap(g_query[:, inner:], 2)
    g_cross = g_cross[:inner] + swap(g_cross[inner:], 2)
    d_cross = return_heads(g_cross, here).astype(WIDE)
    d_self = return_heads(g_self, here).astype(WIDE)
    d_query = undeal(exchange(apart(sum_rows(g_query)), here), 1).astype(WIDE)
    d_pairs = undeal(exchange(apart(sum_rows(g_pairs)), here), 2).astype(WIDE)
    d_mixed = undeal(exchange(apart(sum_rows(g_mixed)), here), 3).astype(WIDE)
    return (
        output[None],
        frame_grad[None],
        text_grad[None],
        d_mixed,
        d_self,
        d_query,
        d_pairs,
        d_cross,
        d_up,
        d_down,
        norm_sums[:3],
        norm_sums[3:],
    )


def solution(mesh):
    in_specs = (
        P("rows", "text", None),
        P("rows", "text", None),
        P("rows", None),
        P("rows", None),
        P("rows", "text"),
        P("rows", "text"),
        P("rows", "text"),
        P("rows", "text"),
        P("rows", "text"),
        P("rows", "text"),
        P("rows", "text"),
        P(None, "text"),
        P(None, "text"),
        P("rows", "text", None),
    )
    out_specs = (
        P("rows", "text", None),
        P("rows", "text", None),
        P("rows", "text", None),
        P("rows", "text"),
        P("rows", "text"),
        P("rows", "text"),
        P("rows", "text"),
        P("rows", "text"),
        P("rows", "text"),
        P("rows", "text"),
        P(None, "text"),
        P(None, "text"),
    )
    local = local_grid if mesh.shape["rows"] == 8 else local_general
    return jax.shard_map(local, mesh=mesh, in_specs=in_specs, out_specs=out_specs, check_vma=False)
```

```python
import functools
import math

import jax
import jax.numpy as jnp
from jax import lax
from jax.experimental import pallas as pl
from jax.experimental.pallas import tpu as pltpu
from jax.sharding import PartitionSpec as P

HEADS = 16
WAYS = 4
SLOTS = (0, 2, 1, 3)
LOW = jnp.bfloat16
WIDE = jnp.float32
NEVER = -1e30


def mm(left, right, left_dim=1, right_dim=0):
    return lax.dot_general(
        left, right, (((left_dim,), (right_dim,)), ((), ())), preferred_element_type=WIDE
    )


def swap(values, mask):
    return lax.ppermute(values, "text", [(i, i ^ mask) for i in range(WAYS)])


def after(value, *events):
    return lax.optimization_barrier((value,) + events)[0]


def copy_all(pairs, sem):
    copies = [pltpu.make_async_copy(*pair, sem.at[i]) for i, pair in enumerate(pairs)]
    for copy in copies:
        copy.start()
    for copy in copies:
        copy.wait()


def join_rows(_, *refs):
    *blocks, whole, sem = refs
    size = whole.shape[0] // len(blocks)
    copy_all(
        [(block, whole.at[i * size : (i + 1) * size]) for i, block in enumerate(blocks)], sem
    )


def join(ids, *blocks):
    rows = sum(b.shape[0] for b in blocks)
    (whole,) = call(
        join_rows,
        [shaped((rows, blocks[0].shape[1]), LOW)],
        (ids, *blocks),
        own_copies=len(blocks),
    )
    return whole


def sync(*values):
    return lax.optimization_barrier(values)


def gather_slots(block, ids, *beside):
    near = swap(block, 1)
    far, *beside = sync(swap(block, 2), *beside)
    whole = join(ids, block, far, near, swap(far, 1))
    return (whole, *beside) if beside else whole


def scatter_slots(left, right, right_dim, gate=None, beside=()):
    half = left.shape[0] // 2
    block = half // 2
    away = mm(left[half:], right, 1, right_dim).astype(LOW)
    near = swap(away, 1)
    far = (mm(left[block:half], right, 1, right_dim) + near[block:].astype(WIDE)).astype(LOW)
    if gate is not None:
        far = after(far, gate)
    far, *beside = sync(swap(far, 2), *beside)
    here = mm(left[:block], right, 1, right_dim) + near[:block].astype(WIDE)
    result = here + far.astype(WIDE)
    return (result, *beside) if beside else result


def gather_pair(block, ids):
    return join(ids, block, swap(block, 1))


def scatter_pair(left, right, right_dim):
    half = left.shape[0] // 2
    away = mm(left[half:], right, 1, right_dim).astype(LOW)
    return mm(left[:half], right, 1, right_dim) + swap(away, 1).astype(WIDE)


def norm_forward(values, gain, bias):
    average = jnp.mean(values, axis=-1, keepdims=True)
    centred = values - average
    spread = jnp.mean(centred * centred, axis=-1, keepdims=True)
    inverse = lax.rsqrt(spread + 1e-05)
    hat = centred * inverse
    return (hat * gain + bias).astype(LOW), hat, inverse


def norm_backward(grad, hat, inverse, gain):
    weighted = grad * gain
    first = jnp.mean(weighted, axis=-1, keepdims=True)
    second = jnp.mean(weighted * hat, axis=-1, keepdims=True)
    return (
        (weighted - first - hat * second) * inverse,
        jnp.sum(grad * hat, axis=0),
        jnp.sum(grad, axis=0),
    )


def slot_of(index, here):
    other = index ^ here
    return ((other & 1) << 1) | (other >> 1)


def half_lanes(values, head):
    lane = lax.broadcasted_iota(jnp.int32, values.shape, 1)
    keep = (lane < 64) if head == 0 else (lane >= 64)
    return jnp.where(keep, values, jnp.zeros_like(values))


def nt(left, right):
    return mm(left, right, 1, 1)


def rows_at(ref, slot, size, pair, offset):
    start = pl.multiple_of(slot * size, size)
    return ref[pl.ds(start, size), offset + pair * 128 : offset + (pair + 1) * 128]


def transposed(values):
    return values.astype(WIDE).T


def self_forward(here_ref, marks_ref, mixed_ref, out_ref, lse_ref):
    here = here_ref[0]
    size = mixed_ref.shape[0] // WAYS
    down = lax.broadcasted_iota(jnp.int32, (size, size), 0)
    across = lax.broadcasted_iota(jnp.int32, (size, size), 1)
    for pair in range(2):
        keys = [rows_at(mixed_ref, slot_of(j, here), size, pair, 256) for j in range(WAYS)]
        values_t = [
            transposed(rows_at(mixed_ref, slot_of(j, here), size, pair, 512)).astype(LOW)
            for j in range(WAYS)
        ]
        for i in range(WAYS):
            mine = slot_of(i, here)
            query = rows_at(mixed_ref, mine, size, pair, 0) * LOW(0.125)
            first = marks_ref[0:1, i * size : (i + 1) * size]
            outs = []
            for head in range(2):
                scores = []
                for j in range(i + 1):
                    s = nt(half_lanes(keys[j], head), query)
                    allowed = (down + j * size) >= first
                    if j == i:
                        allowed = allowed & (down <= across)
                    scores.append(jnp.where(allowed, s, NEVER))
                top = jnp.max(scores[0], axis=0, keepdims=True)
                for s in scores[1:]:
                    top = jnp.maximum(top, jnp.max(s, axis=0, keepdims=True))
                total = jnp.zeros_like(top)
                result = jnp.zeros((64, size), WIDE)
                for j, s in enumerate(scores):
                    probs = jnp.exp(s - top)
                    total = total + jnp.sum(probs, axis=0, keepdims=True)
                    part = values_t[j][head * 64 : (head + 1) * 64]
                    result = result + mm(part, probs.astype(LOW))
                outs.append(result / total)
                lse_ref[2 * pair + head : 2 * pair + head + 1, i * size : (i + 1) * size] = (
                    top + jnp.log(total)
                )
            start = pl.multiple_of(mine * size, size)
            out_ref[pl.ds(start, size), pair * 128 : (pair + 1) * 128] = (
                jnp.concatenate(outs, axis=0).T.astype(LOW)
            )


def self_backward(here_ref, marks_ref, mixed_ref, grad_ref, lse_ref, out_ref, dk_ref, dv_ref):
    here = here_ref[0]
    size = mixed_ref.shape[0] // WAYS
    down = lax.broadcasted_iota(jnp.int32, (size, size), 0)
    across = lax.broadcasted_iota(jnp.int32, (size, size), 1)
    for pair in range(2):
        keys = [rows_at(mixed_ref, slot_of(j, here), size, pair, 256) for j in range(WAYS)]
        values = [rows_at(mixed_ref, slot_of(j, here), size, pair, 512) for j in range(WAYS)]
        keys_t = [transposed(k).astype(LOW) for k in keys]
        for i in reversed(range(WAYS)):
            mine = slot_of(i, here)
            query = rows_at(mixed_ref, mine, size, pair, 0) * LOW(0.125)
            grad = rows_at(grad_ref, mine, size, pair, 0)
            first = marks_ref[0:1, i * size : (i + 1) * size]
            grads_q = []
            dk_parts = [None] * (i + 1)
            dv_parts = [None] * (i + 1)
            for head in range(2):
                mass = lse_ref[2 * pair + head : 2 * pair + head + 1, i * size : (i + 1) * size]
                grad_head = half_lanes(grad, head)
                query_head = half_lanes(query, head)
                probs, grad_probs = [], []
                delta = jnp.zeros((1, size), WIDE)
                for j in range(i + 1):
                    s = nt(half_lanes(keys[j], head), query)
                    allowed = (down + j * size) >= first
                    if j == i:
                        allowed = allowed & (down <= across)
                    p = jnp.exp(jnp.where(allowed, s, NEVER) - mass)
                    dp = nt(half_lanes(values[j], head), grad)
                    delta = delta + jnp.sum(p * dp, axis=0, keepdims=True)
                    probs.append(p)
                    grad_probs.append(dp)
                grad_q = jnp.zeros((64, size), WIDE)
                for j in range(i + 1):
                    ds = (probs[j] * (grad_probs[j] - delta)).astype(LOW)
                    dv = mm(probs[j].astype(LOW), grad_head)
                    dk = mm(ds, query_head)
                    dv_parts[j] = dv if head == 0 else dv_parts[j] + dv
                    dk_parts[j] = dk if head == 0 else dk_parts[j] + dk
                    grad_q = grad_q + mm(keys_t[j][head * 64 : (head + 1) * 64], ds)
                grads_q.append(grad_q)
            start = pl.multiple_of(mine * size, size)
            out_ref[pl.ds(start, size), pair * 128 : (pair + 1) * 128] = (
                (jnp.concatenate(grads_q, axis=0) * 0.125).T.astype(LOW)
            )
            for j in range(i + 1):
                rows = slice(j * size, (j + 1) * size)
                if i == WAYS - 1:
                    dk_ref[rows] = dk_parts[j]
                    dv_ref[rows] = dv_parts[j]
                else:
                    dk_ref[rows] = dk_ref[rows] + dk_parts[j]
                    dv_ref[rows] = dv_ref[rows] + dv_parts[j]
        for j in range(WAYS):
            rows = slice(j * size, (j + 1) * size)
            start = pl.multiple_of(slot_of(j, here) * size, size)
            out_ref[pl.ds(start, size), 256 + pair * 128 : 256 + (pair + 1) * 128] = dk_ref[
                rows
            ].astype(LOW)
            out_ref[pl.ds(start, size), 512 + pair * 128 : 512 + (pair + 1) * 128] = dv_ref[
                rows
            ].astype(LOW)


def token_places(here, count, width):
    row = lax.broadcasted_iota(jnp.int32, (count, width), 0)
    size = count // WAYS
    place = row
    for slot, mask in enumerate(SLOTS):
        inside = (row >= slot * size) & (row < (slot + 1) * size)
        place = jnp.where(inside, row - slot * size + (here ^ mask) * size, place)
    return place


def text_allowed(here, marks_ref, block, size, count):
    start = pl.multiple_of((here ^ block) * size, size)
    low = marks_ref[1:2, pl.ds(start, size)]
    high = marks_ref[2:3, pl.ds(start, size)]
    places = [token_places(here, count, size), token_places(here ^ 2, count, size)]
    return [(place >= low) & (place < high) for place in places]


def cross_forward(here_ref, marks_ref, query_ref, own_ref, other_ref, out_ref, lse_ref):
    here = here_ref[0]
    size = query_ref.shape[0] // 2
    allowed = [text_allowed(here, marks_ref, b, size, own_ref.shape[0]) for b in range(2)]
    for pair in range(4):
        ref = (own_ref, other_ref)[pair // 2]
        column = (pair % 2) * 128
        keys = ref[:, column : column + 128]
        values_t = transposed(ref[:, 256 + column : 384 + column]).astype(LOW)
        for block in range(2):
            rows = slice(block * size, (block + 1) * size)
            query = query_ref[rows, pair * 128 : (pair + 1) * 128] * LOW(0.125)
            outs = []
            for head in range(2):
                s = nt(half_lanes(keys, head), query)
                s = jnp.where(allowed[block][pair // 2], s, NEVER)
                top = jnp.max(s, axis=0, keepdims=True)
                probs = jnp.exp(s - top)
                total = jnp.sum(probs, axis=0, keepdims=True)
                result = mm(values_t[head * 64 : (head + 1) * 64], probs.astype(LOW))
                outs.append(result / total)
                lse_ref[2 * pair + head : 2 * pair + head + 1, rows] = top + jnp.log(total)
            out_ref[rows, pair * 128 : (pair + 1) * 128] = (
                jnp.concatenate(outs, axis=0).T.astype(LOW)
            )


def cross_backward(
    here_ref, marks_ref, query_ref, own_ref, other_ref, grad_ref, lse_ref, dq_ref, down_ref, dother_ref
):
    here = here_ref[0]
    size = query_ref.shape[0] // 2
    allowed = [text_allowed(here, marks_ref, b, size, own_ref.shape[0]) for b in range(2)]
    for pair in range(4):
        ref, out = ((own_ref, down_ref), (other_ref, dother_ref))[pair // 2]
        column = (pair % 2) * 128
        keys = ref[:, column : column + 128]
        values = ref[:, 256 + column : 384 + column]
        keys_t = transposed(keys).astype(LOW)
        sum_k = jnp.zeros(keys.shape, WIDE)
        sum_v = jnp.zeros(keys.shape, WIDE)
        for block in range(2):
            rows = slice(block * size, (block + 1) * size)
            query = query_ref[rows, pair * 128 : (pair + 1) * 128] * LOW(0.125)
            grad = grad_ref[rows, pair * 128 : (pair + 1) * 128]
            grads_q = []
            for head in range(2):
                mass = lse_ref[2 * pair + head : 2 * pair + head + 1, rows]
                s = nt(half_lanes(keys, head), query)
                p = jnp.exp(jnp.where(allowed[block][pair // 2], s, NEVER) - mass)
                dp = nt(half_lanes(values, head), grad)
                delta = jnp.sum(p * dp, axis=0, keepdims=True)
                ds = (p * (dp - delta)).astype(LOW)
                sum_v = sum_v + mm(p.astype(LOW), half_lanes(grad, head))
                sum_k = sum_k + mm(ds, half_lanes(query, head))
                grads_q.append(mm(keys_t[head * 64 : (head + 1) * 64], ds))
            dq_ref[rows, pair * 128 : (pair + 1) * 128] = (
                (jnp.concatenate(grads_q, axis=0) * 0.125).T.astype(LOW)
            )
        out[:, column : column + 128] = sum_k.astype(LOW)
        out[:, 256 + column : 384 + column] = sum_v.astype(LOW)


def bring_in(body, number, ids_ref, *refs):
    scratch, sem = refs[len(refs) - number - 1 : -1], refs[-1]
    copies = [
        pltpu.make_async_copy(refs[i], scratch[i], sem.at[i]) for i in range(number)
    ]
    for copy in copies:
        copy.start()
    for copy in copies:
        copy.wait()
    body(ids_ref, *scratch, *refs[number : len(refs) - number - 1])


def call(body, outs, operands, scratch=(), resident=False, own_copies=0):
    vmem = pl.BlockSpec(memory_space=pltpu.VMEM)
    spec = vmem if resident else pl.BlockSpec(memory_space=pltpu.HBM)
    scratch = list(scratch)
    if own_copies:
        scratch.append(pltpu.SemaphoreType.DMA((own_copies,)))
    elif not resident:
        scratch = [pltpu.VMEM(v.shape, v.dtype) for v in operands[1:]]
        scratch.append(pltpu.SemaphoreType.DMA((len(scratch),)))
        body = functools.partial(bring_in, body, len(operands) - 1)
    moved = sum(v.size * v.dtype.itemsize for v in (*operands, *outs))
    return pl.pallas_call(
        body,
        out_shape=outs,
        in_specs=[pl.BlockSpec(memory_space=pltpu.SMEM)] + [spec for v in operands[1:]],
        out_specs=[vmem for v in outs],
        scratch_shapes=scratch,
        cost_estimate=pl.CostEstimate(flops=0, bytes_accessed=moved, transcendentals=0),
        compiler_params=pltpu.CompilerParams(vmem_limit_bytes=48 << 20),
    )(*operands)


def weight_block(left_a, right_a, left_b, right_b, out_ref):
    @pl.when(pl.program_id(0) == 0)
    def _():
        out_ref[...] = mm(left_a[...], right_a[...], 0, 0).astype(LOW)

    @pl.when(pl.program_id(0) == 1)
    def _():
        out_ref[...] = mm(left_b[...], right_b[...], 0, 0).astype(LOW)


def weight_grads(left_a, right_a, left_b, right_b):
    count, rows = left_a.shape
    columns = right_a.shape[1]
    tile = 256
    last = rows // tile - 1
    return pl.pallas_call(
        weight_block,
        grid=(2, rows // tile),
        out_shape=shaped((rows, 2 * columns), LOW),
        in_specs=[
            pl.BlockSpec((count, tile), lambda w, i: (0, jnp.where(w == 0, i, last))),
            pl.BlockSpec((count, columns), lambda w, i: (0, 0)),
            pl.BlockSpec((count, tile), lambda w, i: (0, jnp.where(w == 0, 0, i))),
            pl.BlockSpec((count, columns), lambda w, i: (0, 0)),
        ],
        out_specs=pl.BlockSpec((tile, columns), lambda w, i: (i, w)),
        cost_estimate=pl.CostEstimate(
            flops=4 * count * rows * columns,
            bytes_accessed=4 * count * (rows + columns) + 4 * rows * columns,
            transcendentals=0,
        ),
        compiler_params=pltpu.CompilerParams(vmem_limit_bytes=48 << 20),
    )(left_a, right_a, left_b, right_b)


def shaped(shape, dtype):
    return jax.ShapeDtypeStruct(shape, dtype)


def deal(matrix, groups):
    depth, width = matrix.shape
    piece = width // (groups * WAYS)
    return jnp.moveaxis(matrix.reshape(depth, groups, WAYS, piece), 2, 0).reshape(
        WAYS, depth, groups * piece
    )


def undeal(dealt, groups):
    _, depth, width = dealt.shape
    return jnp.moveaxis(dealt.reshape(WAYS, depth, groups, width // groups), 0, 2).reshape(
        depth, WAYS * width
    )


def pick(values, index, axis):
    return lax.dynamic_index_in_dim(values, index, axis, keepdims=False)


def ordered(mine, other, bit, axis=0):
    return jnp.stack([jnp.where(bit == 0, mine, other), jnp.where(bit == 0, other, mine)], axis)


def exchange(dealt, here, *gates):
    core, far = here & 1, here >> 1
    tail = dealt.shape[1:]
    dealt = dealt.reshape((2, 2) + tail)
    stage = ordered(pick(dealt, core, 1), swap(pick(dealt, 1 - core, 1), 1), core, 1)
    sent = pick(stage, 1 - far, 0)
    if gates:
        sent = after(sent, *gates)
    return ordered(pick(stage, far, 0), swap(sent, 2), far).reshape((WAYS,) + tail)


def side_by_side(parts):
    return jnp.moveaxis(parts, 0, 1).reshape(parts.shape[1], -1)


def apart(columns):
    depth, width = columns.shape
    return jnp.moveaxis(columns.reshape(depth, WAYS, width // WAYS), 1, 0)


def row_swap(values, mask):
    size = lax.axis_size("rows")
    return lax.ppermute(values, "rows", [(i, i ^ mask) for i in range(size)])


def gather_rows(block):
    return lax.all_gather(block, "rows", axis=0, tiled=True)


def sum_rows(whole):
    return lax.psum_scatter(whole, "rows", scatter_dimension=0, tiled=True)


def place_pieces(depth, splits, ids_ref, *refs):
    row, outs, sem = ids_ref[1], refs[7:-1], refs[-1]
    pairs = []
    for k in range(4):
        for flip in range(2):
            owner = (row ^ flip) ^ (2 * k)
            start = pl.multiple_of(owner * depth, depth)
            column = 0
            for index, width in enumerate(splits):
                columns = slice(column, column + width)
                if not flip:
                    piece = refs[k].at[:, columns]
                elif k < 2:
                    piece = refs[4 + k].at[:, columns]
                else:
                    piece = refs[6].at[k - 2, :, columns]
                pairs.append((piece, outs[index].at[pl.ds(start, depth)]))
                column += width
    copy_all(pairs, sem)


def place(ids, splits, pieces, others):
    depth = pieces[0].shape[0]
    return call(
        functools.partial(place_pieces, depth, splits),
        [shaped((8 * depth, width), LOW) for width in splits],
        (ids, *pieces, *others),
        own_copies=8 * len(splits),
    )


def place_line_pieces(ids_ref, *refs):
    far = ids_ref[1] >> 1
    height = refs[0].shape[0] // 2
    pairs = []
    for k in range(4):
        start = pl.multiple_of((far ^ k) * height, height)
        for index in range(2):
            piece = refs[k].at[index * height : (index + 1) * height]
            pairs.append((piece, refs[4 + index].at[pl.ds(start, height)]))
    copy_all(pairs, refs[6])


def place_lines(ids, *pieces):
    whole = shaped((2 * pieces[0].shape[0], pieces[0].shape[1]), LOW)
    return call(place_line_pieces, [whole] * 2, (ids, *pieces), own_copies=8)


def three_ways(block):
    return [row_swap(block, 2 * k) for k in range(1, 4)]


def split_sums(row_ref, whole_ref, sent_ref, own_ref, *low_refs):
    row = row_ref[1]
    x, far = row & 1, row >> 1
    depth = own_ref.shape[0]
    for k in range(4):
        owner = far ^ k
        start = pl.multiple_of((owner * 2 + x) * depth, depth)
        value = whole_ref[pl.ds(start, depth)].astype(WIDE) + sent_ref[owner].astype(WIDE)
        if k == 0:
            own_ref[...] = value
        else:
            low_refs[k - 1][...] = value.astype(LOW)


def choose(bit, zero, one):
    return jnp.where(bit == 0, zero, one)


def put(ref, column, *values):
    for value in values:
        ref[:, column : column + value.shape[1]] = value.astype(ref.dtype)
        column += value.shape[1]


def total(refs):
    value = refs[0][...]
    for ref in refs[1:]:
        value = value + ref[...].astype(WIDE)
    return value


def device_bits(ids_ref):
    here, row = ids_ref[0], ids_ref[1]
    return here & 1, here >> 1, row & 1, row >> 1


def keep_and_send(kept, sent, column, bit, zero, one):
    put(kept, column, choose(bit, zero, one))
    put(sent, column, choose(bit, one, zero))
    return column + zero.shape[1]


def deal_first_core(ids, self_in, self_out, cross_out, norms, kept, sent):
    core, _, _, _ = device_bits(ids)
    depth = self_in.shape[0]
    for y in range(2):
        for j in range(3):
            first, column = (4 * j + 2 * y) * 64, (3 * y + j) * 64
            zero, one = self_in[:, first : first + 64], self_in[:, first + 64 : first + 128]
            kept[:depth, column : column + 64] = choose(core, zero, one)
            sent[:depth, column : column + 64] = choose(core, one, zero)
    for index, ref in enumerate((self_out, cross_out)):
        rows = slice(64 * index, 64 * (index + 1))
        kept[rows, 384:] = choose(core, ref[:64], ref[64:])
        sent[rows, 384:] = choose(core, ref[64:], ref[:64])
    for ref in (kept, sent):
        ref[depth:] = jnp.zeros_like(ref[depth:])
        ref[depth : depth + norms.shape[0], :256] = norms[...]


def deal_first_far(ids, kept, came, far_kept, far_sent):
    core, y, _, _ = device_bits(ids)
    depth = 128
    column = 0
    sources = [choose(core, kept[...], came[...]), choose(core, came[...], kept[...])]
    for source in sources:
        columns = slice(column, column + 192)
        zero, one = source[:depth, :192], source[:depth, 192:384]
        far_kept[:depth, columns] = choose(y, zero, one)
        far_sent[:depth, columns] = choose(y, one, zero)
        column += 192
    for index, source in enumerate(sources):
        for ref in (far_kept, far_sent):
            ref[:depth, column : column + 256] = source[:depth, 384:]
            ref[depth:, index * 256 : (index + 1) * 256] = source[depth:, :256]
        column += 256
    for ref in (far_kept, far_sent):
        ref[depth:, 512:] = jnp.zeros_like(ref[depth:, 512:])


def deal_first_last(ids, kept, came, mixed, lines, norms):
    _, y, _, _ = device_bits(ids)
    zero, one = choose(y, kept[...], came[...]), choose(y, came[...], kept[...])
    put(mixed, 0, zero[:128, :384], one[:128, :384])
    put(lines, 0, zero[:128, 384:], one[:128, 384:])
    put(norms, 0, zero[128:, :512], one[128:, :512])


def deal_rest_core(ids, query, pairs, up, down, kept, sent):
    core, _, _, _ = device_bits(ids)
    column = 0
    for y in range(2):
        for r in range(2):
            first = (4 * r + 2 * y) * 128
            zero, one = up[:, first : first + 128], up[:, first + 128 : first + 256]
            column = keep_and_send(kept, sent, column, core, zero, one)
    for y in range(2):
        zero, one = [down[(2 * y + c) * 128 : (2 * y + c + 1) * 128] for c in range(2)]
        column = keep_and_send(kept, sent, column, core, zero, one)
    for y in range(2):
        for j in range(2):
            first = (4 * j + 2 * y) * 64
            zero, one = pairs[:, first : first + 64], pairs[:, first + 64 : first + 128]
            column = keep_and_send(kept, sent, column, core, zero, one)
    for y in range(2):
        zero, one = query[:, 128 * y : 128 * y + 64], query[:, 128 * y + 64 : 128 * y + 128]
        column = keep_and_send(kept, sent, column, core, zero, one)


def deal_rest_far(ids, kept, came, far_kept, far_sent):
    core, y, _, _ = device_bits(ids)
    sources = [choose(core, kept[...], came[...]), choose(core, came[...], kept[...])]
    column = 0
    for first, width in ((0, 256), (512, 256), (1024, 128)):
        for source in sources:
            zero = source[:, first : first + width]
            one = source[:, first + width : first + 2 * width]
            column = keep_and_send(far_kept, far_sent, column, y, zero, one)
    for source in sources:
        put(far_kept, column, source[:, 1280:])
        put(far_sent, column, source[:, 1280:])
        column += 128


def deal_rest_last(ids, kept, came, attend, ffn):
    _, y, _, _ = device_bits(ids)
    sources = [choose(y, kept[...], came[...]), choose(y, came[...], kept[...])]
    put(ffn, 0, *[s[:, :512] for s in sources], *[s[:, 512:1024] for s in sources])
    put(attend, 512, *[s[:, 1024:1280] for s in sources])
    for group in range(2):
        for place, source in enumerate(sources):
            for c in range(2):
                first = 1280 + c * 128
                zero = source[:, first + group * 64 : first + group * 64 + 64]
                one = source[:, first + (1 - group) * 64 : first + (1 - group) * 64 + 64]
                put(attend, group * 256 + (2 * place + c) * 64, choose(y, zero, one))


def ffn_far(ids, value, kept, sent):
    _, y, _, _ = device_bits(ids)
    for half in range(2):
        zero = value[:, half * 1024 : half * 1024 + 512]
        one = value[:, half * 1024 + 512 : half * 1024 + 1024]
        put(kept, half * 512, choose(y, zero, one))
        put(sent, half * 512, choose(y, one, zero))


def ffn_core(ids, kept, came, core_kept, core_sent):
    core, y, _, _ = device_bits(ids)
    mine, other = kept[...], came[...]
    column = 0
    for source in (choose(y, mine, other), choose(y, other, mine)):
        for half in range(2):
            zero = source[:, half * 512 : half * 512 + 256]
            one = source[:, half * 512 + 256 : half * 512 + 512]
            put(core_kept, column, choose(core, zero, one))
            put(core_sent, column, choose(core, one, zero))
            column += 256


def ffn_last(ids, kept, came, up, down):
    core, _, _, _ = device_bits(ids)
    mine, other = kept[...], came[...]
    for c, source in enumerate((choose(core, mine, other), choose(core, other, mine))):
        for y in range(2):
            sender = 2 * y + c
            for r in range(2):
                first = 512 * y + 128 * r
                put(up, (4 * r + sender) * 128, source[:, first : first + 128])
            rows = slice(sender * 128, (sender + 1) * 128)
            down[rows] = source[:, 512 * y + 256 : 512 * y + 512].astype(WIDE)


def mixed_far(ids, own, a, b, c, kept, sent):
    _, y, _, _ = device_bits(ids)
    value = total((own, a, b, c))
    put(kept, 0, choose(y, value[:, :384], value[:, 384:]))
    put(sent, 0, choose(y, value[:, 384:], value[:, :384]))


def mixed_core(ids, kept, came, core_kept, core_sent):
    core, y, _, _ = device_bits(ids)
    mine, other = kept[...], came[...].astype(WIDE)
    for index, source in enumerate((choose(y, mine, other), choose(y, other, mine))):
        put(core_kept, 192 * index, choose(core, source[:, :192], source[:, 192:]))
        put(core_sent, 192 * index, choose(core, source[:, 192:], source[:, :192]))


def mixed_last(ids, kept, came, mixed):
    core, _, _, _ = device_bits(ids)
    mine, other = kept[...], came[...].astype(WIDE)
    for c, source in enumerate((choose(core, mine, other), choose(core, other, mine))):
        for y in range(2):
            for j in range(3):
                first = 192 * y + 64 * j
                put(mixed, (4 * j + 2 * y + c) * 64, source[:, first : first + 64])


def attend_x(ids, query, cross, sent):
    _, y, x, _ = device_bits(ids)
    for z in range(4):
        start = pl.multiple_of((2 * z + 1 - x) * 128, 128)
        line = pl.multiple_of(((y ^ x ^ 1) * 4 + z) * 64, 64)
        sent[z, :, :512] = query[pl.ds(start, 128)]
        sent[z, :64, 512:] = cross[pl.ds(line, 64), :512]
        sent[z, 64:, 512:] = cross[pl.ds(line, 64), 512:]


def pairs_x(ids, pairs, sent):
    _, _, x, _ = device_bits(ids)
    for z in range(4):
        sent[z] = pairs[pl.ds(pl.multiple_of((2 * z + 1 - x) * 128, 128), 128)]


def attend_along_z(ids, query, cross, came, own, a, b, c):
    _, y, x, z = device_bits(ids)
    for k, ref in enumerate((own, a, b, c)):
        owner = z ^ k
        start = pl.multiple_of((2 * owner + x) * 128, 128)
        line = pl.multiple_of(((y ^ x) * 4 + owner) * 64, 64)
        moved = came[owner].astype(WIDE)
        value = query[pl.ds(start, 128)].astype(WIDE) + moved[:, :512]
        ref[:, :512] = value.astype(ref.dtype)
        value = cross[pl.ds(line, 64)].astype(WIDE)
        ref[:64, 512:] = (value[:, :512] + moved[:64, 512:]).astype(ref.dtype)
        ref[64:, 512:] = (value[:, 512:] + moved[64:, 512:]).astype(ref.dtype)


def pairs_along_z(ids, pairs, self_out, came, own, a, b, c):
    _, _, x, z = device_bits(ids)
    for k, ref in enumerate((own, a, b, c)):
        owner = z ^ k
        start = pl.multiple_of((2 * owner + x) * 128, 128)
        below = pl.multiple_of(owner * 64, 64)
        value = pairs[pl.ds(start, 128)].astype(WIDE) + came[owner].astype(WIDE)
        ref[:, :512] = value.astype(ref.dtype)
        ref[:64, 512:] = self_out[pl.ds(below, 64), :512].astype(ref.dtype)
        ref[64:, 512:] = self_out[pl.ds(below, 64), 512:].astype(ref.dtype)


def attend_total(ids, *refs):
    value, line = refs[8:]
    value[:, :1024] = total(refs[:4])
    value[:, 1024:] = total(refs[4:8])
    line[...] = value[:, 1536:].astype(LOW)


def attend_far(ids, value, line, kept, sent):
    _, y, _, _ = device_bits(ids)
    own = value[:, 1536:] + line[...].astype(WIDE)
    low_half = jnp.concatenate([own[:64], value[:64, 512:1024]], axis=0)
    high_half = jnp.concatenate([own[64:], value[64:, 512:1024]], axis=0)
    put(kept, 0, choose(y, low_half, high_half))
    put(sent, 0, choose(y, high_half, low_half))
    mine, other = value[:, :256], value[:, 256:512]
    for index, group in enumerate((choose(y, mine, other), choose(y, other, mine))):
        put(kept, 512 + 128 * index, choose(y, group[:, :128], group[:, 128:]))
        put(sent, 512 + 128 * index, choose(y, group[:, 128:], group[:, :128]))
    pairs = value[:, 1024:1536]
    put(kept, 768, choose(y, pairs[:, :256], pairs[:, 256:]))
    put(sent, 768, choose(y, pairs[:, 256:], pairs[:, :256]))


def attend_core(ids, kept, came, core_kept, core_sent):
    core, y, x, _ = device_bits(ids)
    mine, other = kept[...], came[...].astype(WIDE)
    owner = jnp.where(x == y, mine[:64, :512], other[:64, :512])
    lines = jnp.concatenate([owner, mine[64:, :512] + other[64:, :512]], axis=0)
    put(core_kept, 0, choose(core, lines[:, :256], lines[:, 256:]))
    put(core_sent, 0, choose(core, lines[:, 256:], lines[:, :256]))
    query = mine[:, 512:768] + other[:, 512:768]
    for group in range(2):
        zero, one = [query[:, 128 * group + 64 * c : 128 * group + 64 * c + 64] for c in range(2)]
        put(core_kept, 256 + 64 * group, choose(core, zero, one))
        put(core_sent, 256 + 64 * group, choose(core, one, zero))
    mine, other = mine[:, 768:], other[:, 768:]
    for index, source in enumerate((choose(y, mine, other), choose(y, other, mine))):
        put(core_kept, 384 + 128 * index, choose(core, source[:, :128], source[:, 128:]))
        put(core_sent, 384 + 128 * index, choose(core, source[:, 128:], source[:, :128]))


def attend_last(ids, kept, came, self_out, query, pairs, cross):
    core, _, _, _ = device_bits(ids)
    mine, other = kept[...], came[...].astype(WIDE)
    for c, source in enumerate((choose(core, mine, other), choose(core, other, mine))):
        self_out[64 * c : 64 * c + 64] = source[:64, :256]
        cross[64 * c : 64 * c + 64] = source[64:, :256]
        for y in range(2):
            put(query, 64 * (2 * y + c), source[:, 256 + 64 * y : 320 + 64 * y])
            for j in range(2):
                first = 384 + 128 * y + 64 * j
                put(pairs, 64 * (4 * j + 2 * y + c), source[:, first : first + 64])


def along_z(values):
    return [row_swap(v, 2 * (k + 1)) for k, v in enumerate(values)]


def return_ffn(ids, sums):
    low = lambda *shape: shaped(shape, LOW)
    wide = lambda *shape: shaped(shape, WIDE)
    kept, sent = call(ffn_far, [low(128, 1024)] * 2, (ids, sums))
    kept, sent = call(ffn_core, [low(128, 1024)] * 2, (ids, kept, swap(sent, 2)))
    return call(ffn_last, [wide(128, 1024), wide(512, 256)], (ids, kept, swap(sent, 1)))


def return_mixed(ids, own, parts):
    low = lambda *shape: shaped(shape, LOW)
    wide = lambda *shape: shaped(shape, WIDE)
    kept, sent = call(mixed_far, [wide(128, 384), low(128, 384)], (ids, own, *parts))
    kept, sent = call(mixed_core, [wide(128, 384), low(128, 384)], (ids, kept, swap(sent, 2)))
    (mixed,) = call(mixed_last, [wide(128, 768)], (ids, kept, swap(sent, 1)))
    return mixed


def return_attend(ids, *parts):
    low = lambda *shape: shaped(shape, LOW)
    wide = lambda *shape: shaped(shape, WIDE)
    value, line = call(attend_total, [wide(128, 2048), low(128, 512)], (ids, *parts))
    kept, sent = call(
        attend_far, [wide(128, 1024), low(128, 1024)], (ids, value, row_swap(line, 1))
    )
    kept, sent = call(attend_core, [wide(128, 640), low(128, 640)], (ids, kept, swap(sent, 2)))
    return call(
        attend_last,
        [wide(128, 256), wide(128, 256), wide(128, 512), wide(128, 256)],
        (ids, kept, swap(sent, 1)),
    )


def own_heads(matrix, here):
    rows = gather_rows(lax.all_gather(matrix, "text", axis=1, tiled=True))
    width = rows.shape[1]
    grouped = rows.reshape(HEADS // WAYS, WAYS, -1, width)
    return pick(grouped, here, 1).reshape(-1, width)


def return_heads(grad, here):
    count, width = grad.shape
    spread = jnp.zeros((HEADS // WAYS, WAYS, count * WAYS // HEADS, width), grad.dtype)
    spread = lax.dynamic_update_index_in_dim(
        spread, grad.reshape(HEADS // WAYS, 1, -1, width), here, 1
    )
    columns = lax.psum_scatter(
        spread.reshape(count * WAYS, width), "text", scatter_dimension=1, tiled=True
    )
    return sum_rows(columns)


def mask_marks(segments, lengths):
    clip = jnp.arange(lengths.shape[0], dtype=jnp.int32)
    ends = jnp.sum(jnp.where(clip[None, :] <= clip[:, None], lengths[None, :], 0), axis=1)
    begins = jnp.sum((segments[None, :] < clip[:, None]).astype(jnp.int32), axis=1)
    same = (segments[None, :] == clip[:, None]).astype(jnp.int32)
    rows = [begins, ends - lengths, ends] + [jnp.zeros_like(ends)] * 5
    return jnp.stack([jnp.sum(same * values[:, None], axis=0) for values in rows])


def gelu_parts(up):
    phi = 0.5 * (1.0 + lax.erf(up * math.sqrt(0.5)))
    slope = phi + up * (jnp.exp(-0.5 * up * up) * (1.0 / math.sqrt(2.0 * math.pi)))
    return lax.optimization_barrier(((up * phi).astype(LOW), slope))


def reduce_norms(sums, here):
    split = sums.reshape(6, 2, 2, -1)
    split = pick(split, here & 1, 2) + swap(pick(split, 1 - (here & 1), 2), 1)
    sums = pick(split, here >> 1, 1) + swap(pick(split, 1 - (here >> 1), 1), 2)
    mask = 1
    while mask < lax.axis_size("rows"):
        sums = sums + row_swap(sums, mask)
        mask = 2 * mask
    return sums


def local_grid(
    frames,
    text_states,
    frame_segments,
    text_lengths,
    self_in,
    self_out,
    cross_query,
    cross_kv,
    cross_out,
    ffn_in,
    ffn_out,
    norm_gains,
    norm_biases,
    out_grad,
):
    here, row = lax.axis_index("text"), lax.axis_index("rows")
    ids = jnp.stack([here, row]).astype(jnp.int32)
    width = frames.shape[2]
    count = frames.shape[1] * WAYS
    inner = width // WAYS
    low = lambda *shape: shaped(shape, LOW)
    wide = lambda *shape: shaped(shape, WIDE)
    marks = mask_marks(frame_segments[0], text_lengths[0])

    norms = jnp.concatenate([norm_gains, norm_biases], axis=0)
    kept, sent = call(
        deal_first_core, [low(144, 640)] * 2, (ids, self_in, self_out, cross_out, norms)
    )
    kept, sent = call(deal_first_far, [low(144, 896)] * 2, (ids, kept, swap(sent, 1)))
    came = swap(sent, 2)
    (frames_low,) = sync(frames[0], sent)[:1]
    frames_wide = frames_low.astype(WIDE)
    rest = sync(cross_query, cross_kv, ffn_in, ffn_out, sent)[:4]
    rest_kept, rest_sent = call(deal_rest_core, [low(128, 1408)] * 2, (ids, *rest))
    rest_kept, rest_sent = call(
        deal_rest_far, [low(128, 1536)] * 2, (ids, rest_kept, swap(rest_sent, 1))
    )
    mixed, lines, norms = call(
        deal_first_last, [low(128, 768), low(128, 1024), wide(16, 1024)], (ids, kept, came)
    )
    gains, biases = norms[:3], norms[3:6]
    one, hat_one, inverse_one = norm_forward(frames_wide, gains[0], biases[0])
    mixed, lines, rest_sent, one = sync(mixed, lines, rest_sent, one)
    mixed_z = three_ways(mixed)
    mixed_x = row_swap(mixed, 1)
    lines_x = row_swap(lines, 1)
    rest_came = swap(rest_sent, 2)
    one_far, one_near = swap(one, 2), swap(one, 1)
    attend, ffn_block = call(
        deal_rest_last, [low(128, 1024), low(128, 2048)], (ids, rest_kept, rest_came)
    )
    lines = jnp.where((row & 1) == (here >> 1), lines, lines_x)
    *mixed_z, mixed_x, attend, lines, one_far, text, grad = sync(
        *mixed_z, mixed_x, attend, lines, one_far, text_states[0], out_grad[0]
    )
    mixed_x1 = row_swap(mixed_z[0], 1)
    mixed_x2 = row_swap(jnp.stack(mixed_z[1:]), 1)
    attend_z = three_ways(attend)
    one_all = join(ids, one, one_far, one_near, swap(one_far, 1))
    text_far, text_near = swap(text, 2), swap(text, 1)
    mixed_x1, mixed_x2, one_all, text_far = sync(mixed_x1, mixed_x2, one_all, text_far)
    (w_mixed,) = place(ids, (768,), [mixed, *mixed_z], [mixed_x, mixed_x1, mixed_x2])
    mixed_low = mm(one_all, w_mixed).astype(LOW)
    mixed_low, *attend_z, grad, attend, lines, ffn_block = sync(
        mixed_low, *attend_z, grad, attend, lines, ffn_block
    )
    w_ffn = gather_rows(ffn_block)
    lines_z = three_ways(lines)
    attend_x0, attend_x1 = row_swap(attend, 1), row_swap(attend_z[0], 1)
    attend_x2 = row_swap(jnp.stack(attend_z[1:]), 1)
    grad_far, grad_near = swap(grad, 2), swap(grad, 1)
    self_att, self_lse = call(
        self_forward, [low(count, inner), wide(4, count)], (ids, marks, mixed_low), resident=True
    )
    text_all = join(ids, text, text_far, text_near, swap(text_far, 1))
    self_att, text_all, *lines_z, attend_x0, attend_x1, attend_x2, grad_far = sync(
        self_att, text_all, *lines_z, attend_x0, attend_x1, attend_x2, grad_far
    )
    w_self, w_cross = place_lines(ids, lines, *lines_z)
    w_query, w_pairs = place(
        ids, (512, 512), [attend, *attend_z], [attend_x0, attend_x1, attend_x2]
    )
    received = scatter_slots(self_att, w_self, 0)
    hidden = frames_wide + received
    grad_all = join(ids, grad, grad_far, grad_near, swap(grad_far, 1))
    text_count = text_all.shape[0]
    pairs_own = mm(text_all, w_pairs).astype(LOW)
    pairs_other = swap(pairs_own, 2)
    w_cross_far = swap(sync(w_cross, pairs_own)[0], 2)
    two, hat_two, inverse_two = norm_forward(hidden, gains[1], biases[1])
    two_pair = gather_pair(two, ids)
    pair_count = two_pair.shape[0]
    query = mm(two_pair, w_query).astype(LOW)
    cross_att, cross_lse = call(
        cross_forward,
        [low(pair_count, 2 * inner), wide(8, pair_count)],
        (ids, marks, query, pairs_own, pairs_other),
        resident=True,
    )
    w_cross_both = join(ids, w_cross, w_cross_far)
    hidden_two = hidden + scatter_pair(cross_att, w_cross_both, 0)
    three, hat_three, inverse_three = norm_forward(hidden_two, gains[2], biases[2])
    three_all = gather_slots(three, ids)
    w_up, w_down = w_ffn[:, :width], w_ffn[:, width:]
    activ, slope = gelu_parts(mm(three_all, w_up))

    grad_up = (mm(grad_all, w_down, 1, 1) * slope).astype(LOW)
    grad_three = scatter_slots(grad_up, w_up, 1)
    ffn_sums = sum_rows(weight_grads(three_all, grad_up, activ, grad_all))
    output_part = scatter_slots(activ, w_down, 0, grad_three)
    part, gain_three, bias_three = norm_backward(grad_three, hat_three, inverse_three, gains[2])
    grad_two = out_grad[0].astype(WIDE) + part
    branch_two = gather_pair(grad_two.astype(LOW), ids)
    grad_cross = mm(branch_two, w_cross_both, 1, 1).astype(LOW)
    grad_query, pairs_mine, pairs_away = call(
        cross_backward,
        [low(pair_count, 2 * inner)] + [low(text_count, 2 * inner)] * 2,
        (ids, marks, query, pairs_own, pairs_other, grad_cross, cross_lse),
        resident=True,
    )
    grad_query, pairs_away, output_part = sync(grad_query, pairs_away, output_part)
    output = (hidden_two + output_part).astype(LOW)
    pairs_came = swap(pairs_away, 2)
    g_cross = mm(cross_att, branch_two, 0, 0).astype(LOW)
    g_query = mm(two_pair, grad_query, 0, 0).astype(LOW)
    (attend_sent,) = call(attend_x, [low(4, 128, 1024)], (ids, g_query, g_cross))
    attend_came = row_swap(attend_sent, 1)
    part, gain_two, bias_two = norm_backward(
        scatter_pair(grad_query, w_query, 1), hat_two, inverse_two, gains[1]
    )
    grad_hidden = grad_two + part
    grad_low, pairs_came = sync(grad_hidden.astype(LOW), pairs_came)
    grad_pairs = (pairs_mine.astype(WIDE) + pairs_came.astype(WIDE)).astype(LOW)
    g_pairs = mm(text_all, grad_pairs, 0, 0).astype(LOW)
    (pairs_sent,) = call(pairs_x, [low(4, 128, 512)], (ids, g_pairs))
    pairs_came = row_swap(pairs_sent, 1)
    branch = gather_slots(grad_low, ids)
    text_part = scatter_slots(grad_pairs, w_pairs, 1, branch)
    grad_self = mm(branch, w_self, 1, 1).astype(LOW)
    (grad_mixed,) = call(
        self_backward,
        [low(count, 3 * inner)],
        (ids, marks, mixed_low, grad_self, self_lse),
        scratch=[pltpu.VMEM((count, 128), WIDE), pltpu.VMEM((count, 128), WIDE)],
        resident=True,
    )
    g_self = mm(self_att, branch, 0, 0).astype(LOW)
    g_mixed = mm(one_all, grad_mixed, 0, 0).astype(LOW)
    mixed_sent = pick(g_mixed.reshape(4, 2, 128, 768), 1 - (row & 1), 1)
    grad_mixed, g_self, mixed_sent, attend_came, pairs_came, text_part = sync(
        grad_mixed, g_self, mixed_sent, attend_came, pairs_came, text_part
    )
    text_grad = text_part
    sums = [wide(128, 1024)] + [low(128, 1024)] * 3
    attend_own, *attend_parts = call(attend_along_z, sums, (ids, g_query, g_cross, attend_came))
    attend_parts = along_z(attend_parts)
    mixed_came = row_swap(mixed_sent, 1)
    pairs_own, *pairs_parts = call(pairs_along_z, sums, (ids, g_pairs, g_self, pairs_came))
    pairs_parts = along_z(pairs_parts)
    grad_one, mixed_came, *attend_parts = scatter_slots(
        grad_mixed, w_mixed, 1, None, (mixed_came, *attend_parts)
    )
    mixed_own, *mixed_parts = call(
        split_sums, [wide(128, 768)] + [low(128, 768)] * 3, (ids, g_mixed, mixed_came)
    )
    mixed_parts = along_z(mixed_parts)
    mixed_own, grad_one, *pairs_parts = sync(mixed_own, grad_one, *pairs_parts)
    part, gain_one, bias_one = norm_backward(grad_one, hat_one, inverse_one, gains[0])
    frame_grad = grad_hidden + part
    ffn_sums, *mixed_parts = sync(ffn_sums, *mixed_parts)
    d_up, d_down = return_ffn(ids, ffn_sums)
    norm_sums = reduce_norms(
        jnp.stack([gain_one, gain_two, gain_three, bias_one, bias_two, bias_three]), here
    )
    d_self, d_query, d_pairs, d_cross = return_attend(
        ids, attend_own, *attend_parts, pairs_own, *pairs_parts
    )
    d_mixed = return_mixed(ids, mixed_own, mixed_parts)
    return (
        output[None],
        frame_grad[None],
        text_grad[None],
        d_mixed,
        d_self,
        d_query,
        d_pairs,
        d_cross,
        d_up,
        d_down,
        norm_sums[:3],
        norm_sums[3:],
    )


def local_general(
    frames,
    text_states,
    frame_segments,
    text_lengths,
    self_in,
    self_out,
    cross_query,
    cross_kv,
    cross_out,
    ffn_in,
    ffn_out,
    norm_gains,
    norm_biases,
    out_grad,
):
    here = lax.axis_index("text")
    row = lax.axis_index("rows")
    ids = jnp.stack([here, row]).astype(jnp.int32)
    row_count = lax.axis_size("rows")
    width = frames.shape[2]
    count = frames.shape[1] * WAYS
    inner = width // WAYS

    chunk = ffn_out.shape[0] // WAYS
    norms = jnp.concatenate([norm_gains, norm_biases], axis=0)
    norms = ordered(norms, swap(norms, 2), here >> 1)
    norms = ordered(norms, swap(norms, 1), here & 1, 1)
    norms = jnp.moveaxis(norms, 2, 0).reshape(6, width).astype(WIDE)
    gains, biases = norms[:3], norms[3:]
    depth = ffn_in.shape[0]
    gate = norms
    w_mixed = gather_rows(side_by_side(exchange(deal(self_in, 3), here)))
    w_query = gather_rows(side_by_side(exchange(deal(cross_query, 1), here)))
    w_query = jnp.concatenate([w_query, swap(w_query, 2)], axis=1)
    w_pairs = gather_rows(side_by_side(exchange(deal(cross_kv, 2), here)))
    w_self = own_heads(self_out, here)
    w_cross = own_heads(cross_out, here)
    w_up = gather_rows(side_by_side(exchange(deal(ffn_in, row_count // WAYS), here)))
    w_down = ffn_out.reshape(WAYS, chunk, inner)
    w_down = gather_rows(side_by_side(exchange(w_down, here)))

    marks = mask_marks(frame_segments[0], text_lengths[0])

    frames_wide = frames[0].astype(WIDE)
    one, hat_one, inverse_one = norm_forward(frames_wide, gains[0], biases[0])
    one_all = gather_slots(after(one, gate), ids)
    text_all = gather_slots(after(text_states[0], one_all), ids)
    grad_all = gather_slots(after(out_grad[0], text_all), ids)
    one_all = after(one_all, text_all, grad_all)
    mixed = mm(one_all, w_mixed).astype(LOW)
    self_att, self_lse = call(
        self_forward,
        [shaped((count, inner), LOW), shaped((4, count), WIDE)],
        (ids, marks, mixed),
        resident=True,
    )
    hidden = frames_wide + scatter_slots(self_att, w_self, 0)
    two, hat_two, inverse_two = norm_forward(hidden, gains[1], biases[1])
    two_pair = gather_pair(two, ids)
    pair_count = two_pair.shape[0]
    text_count = text_all.shape[0]
    pairs_own = mm(text_all, w_pairs).astype(LOW)
    pairs_other = swap(pairs_own, 2)
    w_cross_both = join(ids, w_cross, swap(after(w_cross, pairs_other), 2))
    query = mm(two_pair, w_query).astype(LOW)
    cross_att, cross_lse = call(
        cross_forward,
        [shaped((pair_count, 2 * inner), LOW), shaped((8, pair_count), WIDE)],
        (ids, marks, query, pairs_own, pairs_other),
        resident=True,
    )
    hidden_two = hidden + scatter_pair(cross_att, w_cross_both, 0)
    three, hat_three, inverse_three = norm_forward(hidden_two, gains[2], biases[2])
    three_all = gather_slots(three, ids)
    up = mm(three_all, w_up)
    activ, slope = gelu_parts(up)

    grad_up = (mm(grad_all, w_down, 1, 1) * slope).astype(LOW)
    grad_three = scatter_slots(grad_up, w_up, 1)
    g_up = mm(three_all, grad_up, 0, 0).astype(LOW)
    g_down = mm(activ, grad_all, 0, 0).astype(LOW)
    output = (hidden_two + scatter_slots(activ, w_down, 0, grad_three)).astype(LOW)
    part, gain_three, bias_three = norm_backward(grad_three, hat_three, inverse_three, gains[2])
    grad_two = out_grad[0].astype(WIDE) + part
    branch_two = gather_pair(grad_two.astype(LOW), ids)
    grad_cross = mm(branch_two, w_cross_both, 1, 1).astype(LOW)
    g_cross = mm(cross_att, branch_two, 0, 0).astype(LOW)
    grad_query, pairs_mine, pairs_away = call(
        cross_backward,
        [shaped((pair_count, 2 * inner), LOW)] + [shaped((text_count, 2 * inner), LOW)] * 2,
        (ids, marks, query, pairs_own, pairs_other, grad_cross, cross_lse),
        resident=True,
    )
    part, gain_two, bias_two = norm_backward(
        scatter_pair(grad_query, w_query, 1), hat_two, inverse_two, gains[1]
    )
    grad_pairs = (pairs_mine.astype(WIDE) + swap(pairs_away, 2).astype(WIDE)).astype(LOW)
    g_query = mm(two_pair, grad_query, 0, 0).astype(LOW)
    g_pairs = mm(text_all, grad_pairs, 0, 0).astype(LOW)
    grad_hidden = grad_two + part
    grad_low = grad_hidden.astype(LOW)
    branch = gather_slots(grad_low, ids)
    text_grad = scatter_slots(grad_pairs, w_pairs, 1, branch)
    grad_self = mm(branch, w_self, 1, 1).astype(LOW)
    g_self = mm(self_att, branch, 0, 0).astype(LOW)
    (grad_mixed,) = call(
        self_backward,
        [shaped((count, 3 * inner), LOW)],
        (ids, marks, mixed, grad_self, self_lse),
        scratch=[pltpu.VMEM((count, 128), WIDE), pltpu.VMEM((count, 128), WIDE)],
        resident=True,
    )
    g_mixed = mm(one_all, grad_mixed, 0, 0).astype(LOW)
    part, gain_one, bias_one = norm_backward(
        scatter_slots(grad_mixed, w_mixed, 1), hat_one, inverse_one, gains[0]
    )
    frame_grad = grad_hidden + part

    norm_sums = reduce_norms(
        jnp.stack([gain_one, gain_two, gain_three, bias_one, bias_two, bias_three]), here
    )
    parts = jnp.concatenate([apart(sum_rows(g_up)), apart(sum_rows(g_down))], axis=1)
    parts = exchange(parts, here)
    d_up = undeal(parts[:, :depth], row_count // WAYS).astype(WIDE)
    d_down = parts[:, depth:].reshape(ffn_out.shape).astype(WIDE)
    g_query = g_query[:, :inner] + swap(g_query[:, inner:], 2)
    g_cross = g_cross[:inner] + swap(g_cross[inner:], 2)
    d_cross = return_heads(g_cross, here).astype(WIDE)
    d_self = return_heads(g_self, here).astype(WIDE)
    d_query = undeal(exchange(apart(sum_rows(g_query)), here), 1).astype(WIDE)
    d_pairs = undeal(exchange(apart(sum_rows(g_pairs)), here), 2).astype(WIDE)
    d_mixed = undeal(exchange(apart(sum_rows(g_mixed)), here), 3).astype(WIDE)
    return (
        output[None],
        frame_grad[None],
        text_grad[None],
        d_mixed,
        d_self,
        d_query,
        d_pairs,
        d_cross,
        d_up,
        d_down,
        norm_sums[:3],
        norm_sums[3:],
    )


def solution(mesh):
    in_specs = (
        P("rows", "text", None),
        P("rows", "text", None),
        P("rows", None),
        P("rows", None),
        P("rows", "text"),
        P("rows", "text"),
        P("rows", "text"),
        P("rows", "text"),
        P("rows", "text"),
        P("rows", "text"),
        P("rows", "text"),
        P(None, "text"),
        P(None, "text"),
        P("rows", "text", None),
    )
    out_specs = (
        P("rows", "text", None),
        P("rows", "text", None),
        P("rows", "text", None),
        P("rows", "text"),
        P("rows", "text"),
        P("rows", "text"),
        P("rows", "text"),
        P("rows", "text"),
        P("rows", "text"),
        P("rows", "text"),
        P(None, "text"),
        P(None, "text"),
    )
    local = local_grid if mesh.shape["rows"] == 8 else local_general
    return jax.shard_map(local, mesh=mesh, in_specs=in_specs, out_specs=out_specs, check_vma=False)
```

```python
import functools
import math

import jax
import jax.numpy as jnp
from jax import lax
from jax.experimental import pallas as pl
from jax.experimental.pallas import tpu as pltpu
from jax.sharding import PartitionSpec as P

HEADS = 16
WAYS = 4
SLOTS = (0, 2, 1, 3)
LOW = jnp.bfloat16
WIDE = jnp.float32
NEVER = -1e30


def mm(left, right, left_dim=1, right_dim=0):
    return lax.dot_general(
        left, right, (((left_dim,), (right_dim,)), ((), ())), preferred_element_type=WIDE
    )


def swap(values, mask):
    return lax.ppermute(values, "text", [(i, i ^ mask) for i in range(WAYS)])


def after(value, *events):
    return lax.optimization_barrier((value,) + events)[0]


def copy_all(pairs, sem):
    copies = [pltpu.make_async_copy(*pair, sem.at[i]) for i, pair in enumerate(pairs)]
    for copy in copies:
        copy.start()
    for copy in copies:
        copy.wait()


def join_rows(_, *refs):
    *blocks, whole, sem = refs
    size = whole.shape[0] // len(blocks)
    copy_all(
        [(block, whole.at[i * size : (i + 1) * size]) for i, block in enumerate(blocks)], sem
    )


def join(ids, *blocks):
    rows = sum(b.shape[0] for b in blocks)
    (whole,) = call(
        join_rows,
        [shaped((rows, blocks[0].shape[1]), LOW)],
        (ids, *blocks),
        own_copies=len(blocks),
    )
    return whole


def sync(*values):
    return lax.optimization_barrier(values)


def gather_slots(block, ids, *beside):
    near = swap(block, 1)
    far, *beside = sync(swap(block, 2), *beside)
    whole = join(ids, block, far, near, swap(far, 1))
    return (whole, *beside) if beside else whole


def scatter_slots(left, right, right_dim, gate=None, beside=()):
    half = left.shape[0] // 2
    block = half // 2
    away = mm(left[half:], right, 1, right_dim).astype(LOW)
    near = swap(away, 1)
    far = (mm(left[block:half], right, 1, right_dim) + near[block:].astype(WIDE)).astype(LOW)
    if gate is not None:
        far = after(far, gate)
    far, *beside = sync(swap(far, 2), *beside)
    here = mm(left[:block], right, 1, right_dim) + near[:block].astype(WIDE)
    result = here + far.astype(WIDE)
    return (result, *beside) if beside else result


def gather_pair(block, ids):
    return join(ids, block, swap(block, 1))


def scatter_pair(left, right, right_dim):
    half = left.shape[0] // 2
    away = mm(left[half:], right, 1, right_dim).astype(LOW)
    return mm(left[:half], right, 1, right_dim) + swap(away, 1).astype(WIDE)


def norm_forward(values, gain, bias):
    average = jnp.mean(values, axis=-1, keepdims=True)
    centred = values - average
    spread = jnp.mean(centred * centred, axis=-1, keepdims=True)
    inverse = lax.rsqrt(spread + 1e-05)
    hat = centred * inverse
    return (hat * gain + bias).astype(LOW), hat, inverse


def norm_backward(grad, hat, inverse, gain):
    weighted = grad * gain
    first = jnp.mean(weighted, axis=-1, keepdims=True)
    second = jnp.mean(weighted * hat, axis=-1, keepdims=True)
    return (
        (weighted - first - hat * second) * inverse,
        jnp.sum(grad * hat, axis=0),
        jnp.sum(grad, axis=0),
    )


def slot_of(index, here):
    other = index ^ here
    return ((other & 1) << 1) | (other >> 1)


def half_lanes(values, head):
    lane = lax.broadcasted_iota(jnp.int32, values.shape, 1)
    keep = (lane < 64) if head == 0 else (lane >= 64)
    return jnp.where(keep, values, jnp.zeros_like(values))


def nt(left, right):
    return mm(left, right, 1, 1)


def rows_at(ref, slot, size, pair, offset):
    start = pl.multiple_of(slot * size, size)
    return ref[pl.ds(start, size), offset + pair * 128 : offset + (pair + 1) * 128]


def transposed(values):
    return values.astype(WIDE).T


def self_forward(here_ref, marks_ref, mixed_ref, out_ref, lse_ref):
    here = here_ref[0]
    size = mixed_ref.shape[0] // WAYS
    down = lax.broadcasted_iota(jnp.int32, (size, size), 0)
    across = lax.broadcasted_iota(jnp.int32, (size, size), 1)
    for pair in range(2):
        keys = [rows_at(mixed_ref, slot_of(j, here), size, pair, 256) for j in range(WAYS)]
        values_t = [
            transposed(rows_at(mixed_ref, slot_of(j, here), size, pair, 512)).astype(LOW)
            for j in range(WAYS)
        ]
        for i in range(WAYS):
            mine = slot_of(i, here)
            query = rows_at(mixed_ref, mine, size, pair, 0) * LOW(0.125)
            first = marks_ref[0:1, i * size : (i + 1) * size]
            outs = []
            for head in range(2):
                scores = []
                for j in range(i + 1):
                    s = nt(half_lanes(keys[j], head), query)
                    allowed = (down + j * size) >= first
                    if j == i:
                        allowed = allowed & (down <= across)
                    scores.append(jnp.where(allowed, s, NEVER))
                top = jnp.max(scores[0], axis=0, keepdims=True)
                for s in scores[1:]:
                    top = jnp.maximum(top, jnp.max(s, axis=0, keepdims=True))
                total = jnp.zeros_like(top)
                result = jnp.zeros((64, size), WIDE)
                for j, s in enumerate(scores):
                    probs = jnp.exp(s - top)
                    total = total + jnp.sum(probs, axis=0, keepdims=True)
                    part = values_t[j][head * 64 : (head + 1) * 64]
                    result = result + mm(part, probs.astype(LOW))
                outs.append(result / total)
                lse_ref[2 * pair + head : 2 * pair + head + 1, i * size : (i + 1) * size] = (
                    top + jnp.log(total)
                )
            start = pl.multiple_of(mine * size, size)
            out_ref[pl.ds(start, size), pair * 128 : (pair + 1) * 128] = (
                jnp.concatenate(outs, axis=0).T.astype(LOW)
            )


def self_backward(here_ref, marks_ref, mixed_ref, grad_ref, lse_ref, out_ref, dk_ref, dv_ref):
    here = here_ref[0]
    size = mixed_ref.shape[0] // WAYS
    down = lax.broadcasted_iota(jnp.int32, (size, size), 0)
    across = lax.broadcasted_iota(jnp.int32, (size, size), 1)
    for pair in range(2):
        keys = [rows_at(mixed_ref, slot_of(j, here), size, pair, 256) for j in range(WAYS)]
        values = [rows_at(mixed_ref, slot_of(j, here), size, pair, 512) for j in range(WAYS)]
        keys_t = [transposed(k).astype(LOW) for k in keys]
        for i in reversed(range(WAYS)):
            mine = slot_of(i, here)
            query = rows_at(mixed_ref, mine, size, pair, 0) * LOW(0.125)
            grad = rows_at(grad_ref, mine, size, pair, 0)
            first = marks_ref[0:1, i * size : (i + 1) * size]
            grads_q = []
            dk_parts = [None] * (i + 1)
            dv_parts = [None] * (i + 1)
            for head in range(2):
                mass = lse_ref[2 * pair + head : 2 * pair + head + 1, i * size : (i + 1) * size]
                grad_head = half_lanes(grad, head)
                query_head = half_lanes(query, head)
                probs, grad_probs = [], []
                delta = jnp.zeros((1, size), WIDE)
                for j in range(i + 1):
                    s = nt(half_lanes(keys[j], head), query)
                    allowed = (down + j * size) >= first
                    if j == i:
                        allowed = allowed & (down <= across)
                    p = jnp.exp(jnp.where(allowed, s, NEVER) - mass)
                    dp = nt(half_lanes(values[j], head), grad)
                    delta = delta + jnp.sum(p * dp, axis=0, keepdims=True)
                    probs.append(p)
                    grad_probs.append(dp)
                grad_q = jnp.zeros((64, size), WIDE)
                for j in range(i + 1):
                    ds = (probs[j] * (grad_probs[j] - delta)).astype(LOW)
                    dv = mm(probs[j].astype(LOW), grad_head)
                    dk = mm(ds, query_head)
                    dv_parts[j] = dv if head == 0 else dv_parts[j] + dv
                    dk_parts[j] = dk if head == 0 else dk_parts[j] + dk
                    grad_q = grad_q + mm(keys_t[j][head * 64 : (head + 1) * 64], ds)
                grads_q.append(grad_q)
            start = pl.multiple_of(mine * size, size)
            out_ref[pl.ds(start, size), pair * 128 : (pair + 1) * 128] = (
                (jnp.concatenate(grads_q, axis=0) * 0.125).T.astype(LOW)
            )
            for j in range(i + 1):
                rows = slice(j * size, (j + 1) * size)
                if i == WAYS - 1:
                    dk_ref[rows] = dk_parts[j]
                    dv_ref[rows] = dv_parts[j]
                else:
                    dk_ref[rows] = dk_ref[rows] + dk_parts[j]
                    dv_ref[rows] = dv_ref[rows] + dv_parts[j]
        for j in range(WAYS):
            rows = slice(j * size, (j + 1) * size)
            start = pl.multiple_of(slot_of(j, here) * size, size)
            out_ref[pl.ds(start, size), 256 + pair * 128 : 256 + (pair + 1) * 128] = dk_ref[
                rows
            ].astype(LOW)
            out_ref[pl.ds(start, size), 512 + pair * 128 : 512 + (pair + 1) * 128] = dv_ref[
                rows
            ].astype(LOW)


def token_places(here, count, width):
    row = lax.broadcasted_iota(jnp.int32, (count, width), 0)
    size = count // WAYS
    place = row
    for slot, mask in enumerate(SLOTS):
        inside = (row >= slot * size) & (row < (slot + 1) * size)
        place = jnp.where(inside, row - slot * size + (here ^ mask) * size, place)
    return place


def text_allowed(here, marks_ref, block, size, count):
    start = pl.multiple_of((here ^ block) * size, size)
    low = marks_ref[1:2, pl.ds(start, size)]
    high = marks_ref[2:3, pl.ds(start, size)]
    places = [token_places(here, count, size), token_places(here ^ 2, count, size)]
    return [(place >= low) & (place < high) for place in places]


def cross_forward(here_ref, marks_ref, query_ref, own_ref, other_ref, out_ref, lse_ref):
    here = here_ref[0]
    size = query_ref.shape[0] // 2
    allowed = [text_allowed(here, marks_ref, b, size, own_ref.shape[0]) for b in range(2)]
    for pair in range(4):
        ref = (own_ref, other_ref)[pair // 2]
        column = (pair % 2) * 128
        keys = ref[:, column : column + 128]
        values_t = transposed(ref[:, 256 + column : 384 + column]).astype(LOW)
        for block in range(2):
            rows = slice(block * size, (block + 1) * size)
            query = query_ref[rows, pair * 128 : (pair + 1) * 128] * LOW(0.125)
            outs = []
            for head in range(2):
                s = nt(half_lanes(keys, head), query)
                s = jnp.where(allowed[block][pair // 2], s, NEVER)
                top = jnp.max(s, axis=0, keepdims=True)
                probs = jnp.exp(s - top)
                total = jnp.sum(probs, axis=0, keepdims=True)
                result = mm(values_t[head * 64 : (head + 1) * 64], probs.astype(LOW))
                outs.append(result / total)
                lse_ref[2 * pair + head : 2 * pair + head + 1, rows] = top + jnp.log(total)
            out_ref[rows, pair * 128 : (pair + 1) * 128] = (
                jnp.concatenate(outs, axis=0).T.astype(LOW)
            )


def cross_backward(
    here_ref, marks_ref, query_ref, own_ref, other_ref, grad_ref, lse_ref, dq_ref, down_ref, dother_ref
):
    here = here_ref[0]
    size = query_ref.shape[0] // 2
    allowed = [text_allowed(here, marks_ref, b, size, own_ref.shape[0]) for b in range(2)]
    for pair in range(4):
        ref, out = ((own_ref, down_ref), (other_ref, dother_ref))[pair // 2]
        column = (pair % 2) * 128
        keys = ref[:, column : column + 128]
        values = ref[:, 256 + column : 384 + column]
        keys_t = transposed(keys).astype(LOW)
        sum_k = jnp.zeros(keys.shape, WIDE)
        sum_v = jnp.zeros(keys.shape, WIDE)
        for block in range(2):
            rows = slice(block * size, (block + 1) * size)
            query = query_ref[rows, pair * 128 : (pair + 1) * 128] * LOW(0.125)
            grad = grad_ref[rows, pair * 128 : (pair + 1) * 128]
            grads_q = []
            for head in range(2):
                mass = lse_ref[2 * pair + head : 2 * pair + head + 1, rows]
                s = nt(half_lanes(keys, head), query)
                p = jnp.exp(jnp.where(allowed[block][pair // 2], s, NEVER) - mass)
                dp = nt(half_lanes(values, head), grad)
                delta = jnp.sum(p * dp, axis=0, keepdims=True)
                ds = (p * (dp - delta)).astype(LOW)
                sum_v = sum_v + mm(p.astype(LOW), half_lanes(grad, head))
                sum_k = sum_k + mm(ds, half_lanes(query, head))
                grads_q.append(mm(keys_t[head * 64 : (head + 1) * 64], ds))
            dq_ref[rows, pair * 128 : (pair + 1) * 128] = (
                (jnp.concatenate(grads_q, axis=0) * 0.125).T.astype(LOW)
            )
        out[:, column : column + 128] = sum_k.astype(LOW)
        out[:, 256 + column : 384 + column] = sum_v.astype(LOW)


def bring_in(body, number, ids_ref, *refs):
    scratch, sem = refs[len(refs) - number - 1 : -1], refs[-1]
    copies = [
        pltpu.make_async_copy(refs[i], scratch[i], sem.at[i]) for i in range(number)
    ]
    for copy in copies:
        copy.start()
    for copy in copies:
        copy.wait()
    body(ids_ref, *scratch, *refs[number : len(refs) - number - 1])


def call(body, outs, operands, scratch=(), resident=False, own_copies=0):
    vmem = pl.BlockSpec(memory_space=pltpu.VMEM)
    spec = vmem if resident else pl.BlockSpec(memory_space=pltpu.HBM)
    scratch = list(scratch)
    if own_copies:
        scratch.append(pltpu.SemaphoreType.DMA((own_copies,)))
    elif not resident:
        scratch = [pltpu.VMEM(v.shape, v.dtype) for v in operands[1:]]
        scratch.append(pltpu.SemaphoreType.DMA((len(scratch),)))
        body = functools.partial(bring_in, body, len(operands) - 1)
    moved = sum(v.size * v.dtype.itemsize for v in (*operands, *outs))
    return pl.pallas_call(
        body,
        out_shape=outs,
        in_specs=[pl.BlockSpec(memory_space=pltpu.SMEM)] + [spec for v in operands[1:]],
        out_specs=[vmem for v in outs],
        scratch_shapes=scratch,
        cost_estimate=pl.CostEstimate(flops=0, bytes_accessed=moved, transcendentals=0),
        compiler_params=pltpu.CompilerParams(vmem_limit_bytes=48 << 20),
    )(*operands)


def weight_block(left_a, right_a, left_b, right_b, out_ref):
    @pl.when(pl.program_id(0) == 0)
    def _():
        out_ref[...] = mm(left_a[...], right_a[...], 0, 0).astype(LOW)

    @pl.when(pl.program_id(0) == 1)
    def _():
        out_ref[...] = mm(left_b[...], right_b[...], 0, 0).astype(LOW)


def weight_grads(left_a, right_a, left_b, right_b):
    count, rows = left_a.shape
    columns = right_a.shape[1]
    tile = 256
    last = rows // tile - 1
    return pl.pallas_call(
        weight_block,
        grid=(2, rows // tile),
        out_shape=shaped((rows, 2 * columns), LOW),
        in_specs=[
            pl.BlockSpec((count, tile), lambda w, i: (0, jnp.where(w == 0, i, last))),
            pl.BlockSpec((count, columns), lambda w, i: (0, 0)),
            pl.BlockSpec((count, tile), lambda w, i: (0, jnp.where(w == 0, 0, i))),
            pl.BlockSpec((count, columns), lambda w, i: (0, 0)),
        ],
        out_specs=pl.BlockSpec((tile, columns), lambda w, i: (i, w)),
        cost_estimate=pl.CostEstimate(
            flops=4 * count * rows * columns,
            bytes_accessed=4 * count * (rows + columns) + 4 * rows * columns,
            transcendentals=0,
        ),
        compiler_params=pltpu.CompilerParams(vmem_limit_bytes=48 << 20),
    )(left_a, right_a, left_b, right_b)


def shaped(shape, dtype):
    return jax.ShapeDtypeStruct(shape, dtype)


def deal(matrix, groups):
    depth, width = matrix.shape
    piece = width // (groups * WAYS)
    return jnp.moveaxis(matrix.reshape(depth, groups, WAYS, piece), 2, 0).reshape(
        WAYS, depth, groups * piece
    )


def undeal(dealt, groups):
    _, depth, width = dealt.shape
    return jnp.moveaxis(dealt.reshape(WAYS, depth, groups, width // groups), 0, 2).reshape(
        depth, WAYS * width
    )


def pick(values, index, axis):
    return lax.dynamic_index_in_dim(values, index, axis, keepdims=False)


def ordered(mine, other, bit, axis=0):
    return jnp.stack([jnp.where(bit == 0, mine, other), jnp.where(bit == 0, other, mine)], axis)


def exchange(dealt, here, *gates):
    core, far = here & 1, here >> 1
    tail = dealt.shape[1:]
    dealt = dealt.reshape((2, 2) + tail)
    stage = ordered(pick(dealt, core, 1), swap(pick(dealt, 1 - core, 1), 1), core, 1)
    sent = pick(stage, 1 - far, 0)
    if gates:
        sent = after(sent, *gates)
    return ordered(pick(stage, far, 0), swap(sent, 2), far).reshape((WAYS,) + tail)


def side_by_side(parts):
    return jnp.moveaxis(parts, 0, 1).reshape(parts.shape[1], -1)


def apart(columns):
    depth, width = columns.shape
    return jnp.moveaxis(columns.reshape(depth, WAYS, width // WAYS), 1, 0)


def row_swap(values, mask):
    size = lax.axis_size("rows")
    return lax.ppermute(values, "rows", [(i, i ^ mask) for i in range(size)])


def gather_rows(block):
    return lax.all_gather(block, "rows", axis=0, tiled=True)


def sum_rows(whole):
    return lax.psum_scatter(whole, "rows", scatter_dimension=0, tiled=True)


def place_pieces(depth, splits, ids_ref, *refs):
    row, outs, sem = ids_ref[1], refs[7:-1], refs[-1]
    pairs = []
    for k in range(4):
        for flip in range(2):
            owner = (row ^ flip) ^ (2 * k)
            start = pl.multiple_of(owner * depth, depth)
            column = 0
            for index, width in enumerate(splits):
                columns = slice(column, column + width)
                if not flip:
                    piece = refs[k].at[:, columns]
                elif k < 2:
                    piece = refs[4 + k].at[:, columns]
                else:
                    piece = refs[6].at[k - 2, :, columns]
                pairs.append((piece, outs[index].at[pl.ds(start, depth)]))
                column += width
    copy_all(pairs, sem)


def place(ids, splits, pieces, others):
    depth = pieces[0].shape[0]
    return call(
        functools.partial(place_pieces, depth, splits),
        [shaped((8 * depth, width), LOW) for width in splits],
        (ids, *pieces, *others),
        own_copies=8 * len(splits),
    )


def place_line_pieces(ids_ref, *refs):
    far = ids_ref[1] >> 1
    height = refs[0].shape[0]
    pairs = []
    for k in range(4):
        start = pl.multiple_of((far ^ k) * height, height)
        pairs.append((refs[k], refs[4].at[pl.ds(start, height)]))
    copy_all(pairs, refs[5])


def place_line(ids, *pieces):
    whole = shaped((4 * pieces[0].shape[0], pieces[0].shape[1]), LOW)
    return call(place_line_pieces, [whole], (ids, *pieces), own_copies=4)[0]


def three_ways(block):
    return [row_swap(block, 2 * k) for k in range(1, 4)]


def split_sums(row_ref, whole_ref, sent_ref, own_ref, *low_refs):
    row = row_ref[1]
    x, far = row & 1, row >> 1
    depth = own_ref.shape[0]
    for k in range(4):
        owner = far ^ k
        start = pl.multiple_of((owner * 2 + x) * depth, depth)
        value = whole_ref[pl.ds(start, depth)].astype(WIDE) + sent_ref[owner].astype(WIDE)
        if k == 0:
            own_ref[...] = value
        else:
            low_refs[k - 1][...] = value.astype(LOW)


def choose(bit, zero, one):
    return jnp.where(bit == 0, zero, one)


def put(ref, column, *values):
    for value in values:
        ref[:, column : column + value.shape[1]] = value.astype(ref.dtype)
        column += value.shape[1]


def total(refs):
    value = refs[0][...]
    for ref in refs[1:]:
        value = value + ref[...].astype(WIDE)
    return value


def device_bits(ids_ref):
    here, row = ids_ref[0], ids_ref[1]
    return here & 1, here >> 1, row & 1, row >> 1


def keep_and_send(kept, sent, column, bit, zero, one):
    put(kept, column, choose(bit, zero, one))
    put(sent, column, choose(bit, one, zero))
    return column + zero.shape[1]


def deal_first_core(ids, self_in, self_out, cross_out, norms, kept, sent):
    core, _, _, _ = device_bits(ids)
    depth = self_in.shape[0]
    for y in range(2):
        for j in range(3):
            first, column = (4 * j + 2 * y) * 64, (3 * y + j) * 64
            zero, one = self_in[:, first : first + 64], self_in[:, first + 64 : first + 128]
            kept[:depth, column : column + 64] = choose(core, zero, one)
            sent[:depth, column : column + 64] = choose(core, one, zero)
    for index, ref in enumerate((self_out, cross_out)):
        rows = slice(64 * index, 64 * (index + 1))
        kept[rows, 384:] = choose(core, ref[:64], ref[64:])
        sent[rows, 384:] = choose(core, ref[64:], ref[:64])
    for ref in (kept, sent):
        ref[depth:] = jnp.zeros_like(ref[depth:])
        ref[depth : depth + norms.shape[0], :256] = norms[...]


def deal_first_far(ids, kept, came, far_kept, far_sent):
    core, y, _, _ = device_bits(ids)
    depth = 128
    column = 0
    sources = [choose(core, kept[...], came[...]), choose(core, came[...], kept[...])]
    for source in sources:
        columns = slice(column, column + 192)
        zero, one = source[:depth, :192], source[:depth, 192:384]
        far_kept[:depth, columns] = choose(y, zero, one)
        far_sent[:depth, columns] = choose(y, one, zero)
        column += 192
    for index, source in enumerate(sources):
        for ref in (far_kept, far_sent):
            ref[:depth, column : column + 256] = source[:depth, 384:]
            ref[depth:, index * 256 : (index + 1) * 256] = source[depth:, :256]
        column += 256
    for ref in (far_kept, far_sent):
        ref[depth:, 512:] = jnp.zeros_like(ref[depth:, 512:])


def deal_first_last(ids, kept, came, mixed, lines, norms):
    _, y, _, _ = device_bits(ids)
    zero, one = choose(y, kept[...], came[...]), choose(y, came[...], kept[...])
    put(mixed, 0, zero[:128, :384], one[:128, :384])
    put(lines, 0, zero[:128, 384:], one[:128, 384:])
    put(norms, 0, zero[128:, :512], one[128:, :512])


def deal_rest_core(ids, query, pairs, up, down, kept, sent):
    core, _, _, _ = device_bits(ids)
    column = 0
    for y in range(2):
        for r in range(2):
            first = (4 * r + 2 * y) * 128
            zero, one = up[:, first : first + 128], up[:, first + 128 : first + 256]
            column = keep_and_send(kept, sent, column, core, zero, one)
    for y in range(2):
        zero, one = [down[(2 * y + c) * 128 : (2 * y + c + 1) * 128] for c in range(2)]
        column = keep_and_send(kept, sent, column, core, zero, one)
    for y in range(2):
        for j in range(2):
            first = (4 * j + 2 * y) * 64
            zero, one = pairs[:, first : first + 64], pairs[:, first + 64 : first + 128]
            column = keep_and_send(kept, sent, column, core, zero, one)
    for y in range(2):
        zero, one = query[:, 128 * y : 128 * y + 64], query[:, 128 * y + 64 : 128 * y + 128]
        column = keep_and_send(kept, sent, column, core, zero, one)


def deal_rest_far(ids, kept, came, far_kept, far_sent):
    core, y, _, _ = device_bits(ids)
    sources = [choose(core, kept[...], came[...]), choose(core, came[...], kept[...])]
    column = 0
    for first, width in ((0, 256), (512, 256), (1024, 128)):
        for source in sources:
            zero = source[:, first : first + width]
            one = source[:, first + width : first + 2 * width]
            column = keep_and_send(far_kept, far_sent, column, y, zero, one)
    for source in sources:
        put(far_kept, column, source[:, 1280:])
        put(far_sent, column, source[:, 1280:])
        column += 128


def deal_rest_last(ids, kept, came, attend, ffn):
    _, y, _, _ = device_bits(ids)
    sources = [choose(y, kept[...], came[...]), choose(y, came[...], kept[...])]
    put(ffn, 0, *[s[:, :512] for s in sources], *[s[:, 512:1024] for s in sources])
    put(attend, 512, *[s[:, 1024:1280] for s in sources])
    for group in range(2):
        for place, source in enumerate(sources):
            for c in range(2):
                first = 1280 + c * 128
                zero = source[:, first + group * 64 : first + group * 64 + 64]
                one = source[:, first + (1 - group) * 64 : first + (1 - group) * 64 + 64]
                put(attend, group * 256 + (2 * place + c) * 64, choose(y, zero, one))


def ffn_far(ids, value, kept, sent):
    _, y, _, _ = device_bits(ids)
    for half in range(2):
        zero = value[:, half * 1024 : half * 1024 + 512]
        one = value[:, half * 1024 + 512 : half * 1024 + 1024]
        put(kept, half * 512, choose(y, zero, one))
        put(sent, half * 512, choose(y, one, zero))


def ffn_core(ids, kept, came, core_kept, core_sent):
    core, y, _, _ = device_bits(ids)
    mine, other = kept[...], came[...]
    column = 0
    for source in (choose(y, mine, other), choose(y, other, mine)):
        for half in range(2):
            zero = source[:, half * 512 : half * 512 + 256]
            one = source[:, half * 512 + 256 : half * 512 + 512]
            put(core_kept, column, choose(core, zero, one))
            put(core_sent, column, choose(core, one, zero))
            column += 256


def ffn_last(ids, kept, came, up, down):
    core, _, _, _ = device_bits(ids)
    mine, other = kept[...], came[...]
    for c, source in enumerate((choose(core, mine, other), choose(core, other, mine))):
        for y in range(2):
            sender = 2 * y + c
            for r in range(2):
                first = 512 * y + 128 * r
                put(up, (4 * r + sender) * 128, source[:, first : first + 128])
            rows = slice(sender * 128, (sender + 1) * 128)
            down[rows] = source[:, 512 * y + 256 : 512 * y + 512].astype(WIDE)


def mixed_far(ids, own, a, b, c, kept, sent):
    _, y, _, _ = device_bits(ids)
    value = total((own, a, b, c))
    put(kept, 0, choose(y, value[:, :384], value[:, 384:]))
    put(sent, 0, choose(y, value[:, 384:], value[:, :384]))


def mixed_core(ids, kept, came, core_kept, core_sent):
    core, y, _, _ = device_bits(ids)
    mine, other = kept[...], came[...].astype(WIDE)
    for index, source in enumerate((choose(y, mine, other), choose(y, other, mine))):
        put(core_kept, 192 * index, choose(core, source[:, :192], source[:, 192:]))
        put(core_sent, 192 * index, choose(core, source[:, 192:], source[:, :192]))


def mixed_last(ids, kept, came, mixed):
    core, _, _, _ = device_bits(ids)
    mine, other = kept[...], came[...].astype(WIDE)
    for c, source in enumerate((choose(core, mine, other), choose(core, other, mine))):
        for y in range(2):
            for j in range(3):
                first = 192 * y + 64 * j
                put(mixed, (4 * j + 2 * y + c) * 64, source[:, first : first + 64])


def attend_x(ids, query, cross, sent):
    _, y, x, _ = device_bits(ids)
    for z in range(4):
        start = pl.multiple_of((2 * z + 1 - x) * 128, 128)
        line = pl.multiple_of(((y ^ x ^ 1) * 4 + z) * 64, 64)
        sent[z, :, :512] = query[pl.ds(start, 128)]
        sent[z, :64, 512:] = cross[pl.ds(line, 64), :512]
        sent[z, 64:, 512:] = cross[pl.ds(line, 64), 512:]


def pairs_x(ids, pairs, sent):
    _, _, x, _ = device_bits(ids)
    for z in range(4):
        sent[z] = pairs[pl.ds(pl.multiple_of((2 * z + 1 - x) * 128, 128), 128)]


def attend_along_z(ids, query, cross, came, own, a, b, c):
    _, y, x, z = device_bits(ids)
    for k, ref in enumerate((own, a, b, c)):
        owner = z ^ k
        start = pl.multiple_of((2 * owner + x) * 128, 128)
        line = pl.multiple_of(((y ^ x) * 4 + owner) * 64, 64)
        moved = came[owner].astype(WIDE)
        value = query[pl.ds(start, 128)].astype(WIDE) + moved[:, :512]
        ref[:, :512] = value.astype(ref.dtype)
        value = cross[pl.ds(line, 64)].astype(WIDE)
        ref[:64, 512:] = (value[:, :512] + moved[:64, 512:]).astype(ref.dtype)
        ref[64:, 512:] = (value[:, 512:] + moved[64:, 512:]).astype(ref.dtype)


def pairs_along_z(ids, pairs, self_out, came, own, a, b, c):
    _, _, x, z = device_bits(ids)
    for k, ref in enumerate((own, a, b, c)):
        owner = z ^ k
        start = pl.multiple_of((2 * owner + x) * 128, 128)
        below = pl.multiple_of(owner * 64, 64)
        value = pairs[pl.ds(start, 128)].astype(WIDE) + came[owner].astype(WIDE)
        ref[:, :512] = value.astype(ref.dtype)
        ref[:64, 512:] = self_out[pl.ds(below, 64), :512].astype(ref.dtype)
        ref[64:, 512:] = self_out[pl.ds(below, 64), 512:].astype(ref.dtype)


def attend_total(ids, *refs):
    value, line = refs[8:]
    value[:, :1024] = total(refs[:4])
    value[:, 1024:] = total(refs[4:8])
    line[...] = value[:, 1536:].astype(LOW)


def attend_far(ids, value, line, kept, sent):
    _, y, _, _ = device_bits(ids)
    own = value[:, 1536:] + line[...].astype(WIDE)
    low_half = jnp.concatenate([own[:64], value[:64, 512:1024]], axis=0)
    high_half = jnp.concatenate([own[64:], value[64:, 512:1024]], axis=0)
    put(kept, 0, choose(y, low_half, high_half))
    put(sent, 0, choose(y, high_half, low_half))
    mine, other = value[:, :256], value[:, 256:512]
    for index, group in enumerate((choose(y, mine, other), choose(y, other, mine))):
        put(kept, 512 + 128 * index, choose(y, group[:, :128], group[:, 128:]))
        put(sent, 512 + 128 * index, choose(y, group[:, 128:], group[:, :128]))
    pairs = value[:, 1024:1536]
    put(kept, 768, choose(y, pairs[:, :256], pairs[:, 256:]))
    put(sent, 768, choose(y, pairs[:, 256:], pairs[:, :256]))


def attend_core(ids, kept, came, core_kept, core_sent):
    core, y, x, _ = device_bits(ids)
    mine, other = kept[...], came[...].astype(WIDE)
    owner = jnp.where(x == y, mine[:64, :512], other[:64, :512])
    lines = jnp.concatenate([owner, mine[64:, :512] + other[64:, :512]], axis=0)
    put(core_kept, 0, choose(core, lines[:, :256], lines[:, 256:]))
    put(core_sent, 0, choose(core, lines[:, 256:], lines[:, :256]))
    query = mine[:, 512:768] + other[:, 512:768]
    for group in range(2):
        zero, one = [query[:, 128 * group + 64 * c : 128 * group + 64 * c + 64] for c in range(2)]
        put(core_kept, 256 + 64 * group, choose(core, zero, one))
        put(core_sent, 256 + 64 * group, choose(core, one, zero))
    mine, other = mine[:, 768:], other[:, 768:]
    for index, source in enumerate((choose(y, mine, other), choose(y, other, mine))):
        put(core_kept, 384 + 128 * index, choose(core, source[:, :128], source[:, 128:]))
        put(core_sent, 384 + 128 * index, choose(core, source[:, 128:], source[:, :128]))


def attend_last(ids, kept, came, self_out, query, pairs, cross):
    core, _, _, _ = device_bits(ids)
    mine, other = kept[...], came[...].astype(WIDE)
    for c, source in enumerate((choose(core, mine, other), choose(core, other, mine))):
        self_out[64 * c : 64 * c + 64] = source[:64, :256]
        cross[64 * c : 64 * c + 64] = source[64:, :256]
        for y in range(2):
            put(query, 64 * (2 * y + c), source[:, 256 + 64 * y : 320 + 64 * y])
            for j in range(2):
                first = 384 + 128 * y + 64 * j
                put(pairs, 64 * (4 * j + 2 * y + c), source[:, first : first + 64])


def along_z(values):
    return [row_swap(v, 2 * (k + 1)) for k, v in enumerate(values)]


def return_ffn(ids, sums):
    low = lambda *shape: shaped(shape, LOW)
    wide = lambda *shape: shaped(shape, WIDE)
    kept, sent = call(ffn_far, [low(128, 1024)] * 2, (ids, sums))
    kept, sent = call(ffn_core, [low(128, 1024)] * 2, (ids, kept, swap(sent, 2)))
    return call(ffn_last, [wide(128, 1024), wide(512, 256)], (ids, kept, swap(sent, 1)))


def return_mixed(ids, own, parts):
    low = lambda *shape: shaped(shape, LOW)
    wide = lambda *shape: shaped(shape, WIDE)
    kept, sent = call(mixed_far, [wide(128, 384), low(128, 384)], (ids, own, *parts))
    kept, sent = call(mixed_core, [wide(128, 384), low(128, 384)], (ids, kept, swap(sent, 2)))
    (mixed,) = call(mixed_last, [wide(128, 768)], (ids, kept, swap(sent, 1)))
    return mixed


def return_attend(ids, *parts):
    low = lambda *shape: shaped(shape, LOW)
    wide = lambda *shape: shaped(shape, WIDE)
    value, line = call(attend_total, [wide(128, 2048), low(128, 512)], (ids, *parts))
    kept, sent = call(
        attend_far, [wide(128, 1024), low(128, 1024)], (ids, value, row_swap(line, 1))
    )
    kept, sent = call(attend_core, [wide(128, 640), low(128, 640)], (ids, kept, swap(sent, 2)))
    return call(
        attend_last,
        [wide(128, 256), wide(128, 256), wide(128, 512), wide(128, 256)],
        (ids, kept, swap(sent, 1)),
    )


def own_heads(matrix, here):
    rows = gather_rows(lax.all_gather(matrix, "text", axis=1, tiled=True))
    width = rows.shape[1]
    grouped = rows.reshape(HEADS // WAYS, WAYS, -1, width)
    return pick(grouped, here, 1).reshape(-1, width)


def return_heads(grad, here):
    count, width = grad.shape
    spread = jnp.zeros((HEADS // WAYS, WAYS, count * WAYS // HEADS, width), grad.dtype)
    spread = lax.dynamic_update_index_in_dim(
        spread, grad.reshape(HEADS // WAYS, 1, -1, width), here, 1
    )
    columns = lax.psum_scatter(
        spread.reshape(count * WAYS, width), "text", scatter_dimension=1, tiled=True
    )
    return sum_rows(columns)


def mask_marks(segments, lengths):
    clip = jnp.arange(lengths.shape[0], dtype=jnp.int32)
    ends = jnp.sum(jnp.where(clip[None, :] <= clip[:, None], lengths[None, :], 0), axis=1)
    begins = jnp.sum((segments[None, :] < clip[:, None]).astype(jnp.int32), axis=1)
    same = (segments[None, :] == clip[:, None]).astype(jnp.int32)
    rows = [begins, ends - lengths, ends] + [jnp.zeros_like(ends)] * 5
    return jnp.stack([jnp.sum(same * values[:, None], axis=0) for values in rows])


def gelu_parts(up):
    phi = 0.5 * (1.0 + lax.erf(up * math.sqrt(0.5)))
    slope = phi + up * (jnp.exp(-0.5 * up * up) * (1.0 / math.sqrt(2.0 * math.pi)))
    return lax.optimization_barrier(((up * phi).astype(LOW), slope))


def norms_core(ids, *refs):
    core, _, _, _ = device_bits(ids)
    kept, sent = refs[6:]
    for ref in (kept, sent):
        ref[...] = jnp.zeros_like(ref)
    for index, row in enumerate(refs[:6]):
        for y in range(2):
            zero, one = [row[:, (2 * y + c) * 256 : (2 * y + c + 1) * 256] for c in range(2)]
            columns = slice(256 * y, 256 * (y + 1))
            kept[index : index + 1, columns] = choose(core, zero, one)
            sent[index : index + 1, columns] = choose(core, one, zero)


def norms_far(ids, kept, came, far_kept, far_sent):
    _, y, _, _ = device_bits(ids)
    value = kept[...] + came[...]
    far_kept[...] = choose(y, value[:, :256], value[:, 256:])
    far_sent[...] = choose(y, value[:, 256:], value[:, :256])


def norms_over_text(ids, rows):
    wide = lambda *shape: shaped(shape, WIDE)
    kept, sent = call(norms_core, [wide(8, 512)] * 2, (ids, *[r[None] for r in rows]))
    kept, sent = call(norms_far, [wide(8, 256)] * 2, (ids, kept, swap(sent, 1)))
    return kept + swap(sent, 2)


def over_rows(sums):
    mask = 1
    while mask < lax.axis_size("rows"):
        sums = sums + row_swap(sums, mask)
        mask = 2 * mask
    return sums


def reduce_norms(rows, here):
    split = jnp.stack(rows).reshape(6, 2, 2, -1)
    split = pick(split, here & 1, 2) + swap(pick(split, 1 - (here & 1), 2), 1)
    return over_rows(pick(split, here >> 1, 1) + swap(pick(split, 1 - (here >> 1), 1), 2))


def local_grid(
    frames,
    text_states,
    frame_segments,
    text_lengths,
    self_in,
    self_out,
    cross_query,
    cross_kv,
    cross_out,
    ffn_in,
    ffn_out,
    norm_gains,
    norm_biases,
    out_grad,
):
    here, row = lax.axis_index("text"), lax.axis_index("rows")
    ids = jnp.stack([here, row]).astype(jnp.int32)
    width = frames.shape[2]
    count = frames.shape[1] * WAYS
    inner = width // WAYS
    low = lambda *shape: shaped(shape, LOW)
    wide = lambda *shape: shaped(shape, WIDE)
    marks = mask_marks(frame_segments[0], text_lengths[0])

    norms = jnp.concatenate([norm_gains, norm_biases], axis=0)
    kept, sent = call(
        deal_first_core, [low(144, 640)] * 2, (ids, self_in, self_out, cross_out, norms)
    )
    kept, sent = call(deal_first_far, [low(144, 896)] * 2, (ids, kept, swap(sent, 1)))
    came = swap(sent, 2)
    (frames_low,) = sync(frames[0], sent)[:1]
    frames_wide = frames_low.astype(WIDE)
    rest = sync(cross_query, cross_kv, ffn_in, ffn_out, sent)[:4]
    rest_kept, rest_sent = call(deal_rest_core, [low(128, 1408)] * 2, (ids, *rest))
    rest_kept, rest_sent = call(
        deal_rest_far, [low(128, 1536)] * 2, (ids, rest_kept, swap(rest_sent, 1))
    )
    mixed, lines, norms = call(
        deal_first_last, [low(128, 768), low(128, 1024), wide(16, 1024)], (ids, kept, came)
    )
    gains, biases = norms[:3], norms[3:6]
    one, hat_one, inverse_one = norm_forward(frames_wide, gains[0], biases[0])
    mixed, lines, rest_sent, one = sync(mixed, lines, rest_sent, one)
    mixed_z = three_ways(mixed)
    mixed_x = row_swap(mixed, 1)
    lines_x = row_swap(lines, 1)
    mixed_x1 = row_swap(mixed_z[0], 1)
    rest_came = swap(rest_sent, 2)
    one_far, one_near = swap(one, 2), swap(one, 1)
    attend, ffn_block = call(
        deal_rest_last, [low(128, 1024), low(128, 2048)], (ids, rest_kept, rest_came)
    )
    lines = jnp.where((row & 1) == (here >> 1), lines, lines_x)
    *mixed_z, mixed_x, mixed_x1, attend, lines, one_far, text, grad = sync(
        *mixed_z, mixed_x, mixed_x1, attend, lines, one_far, text_states[0], out_grad[0]
    )
    mixed_x2 = row_swap(jnp.stack(mixed_z[1:]), 1)
    self_line, cross_line = lines[:64], lines[64:]
    self_z = three_ways(self_line)
    attend_z = three_ways(attend)
    one_all = join(ids, one, one_far, one_near, swap(one_far, 1))
    text_far, text_near = swap(text, 2), swap(text, 1)
    mixed_x2, one_all, text_far, *self_z, ffn_block = sync(
        mixed_x2, one_all, text_far, *self_z, ffn_block
    )
    w_ffn = gather_rows(ffn_block)
    (w_mixed,) = place(ids, (768,), [mixed, *mixed_z], [mixed_x, mixed_x1, mixed_x2])
    mixed_low = mm(one_all, w_mixed).astype(LOW)
    w_self = place_line(ids, self_line, *self_z)
    mixed_low, *attend_z, grad, attend, cross_line, w_self = sync(
        mixed_low, *attend_z, grad, attend, cross_line, w_self
    )
    attend_x0, attend_x1 = row_swap(attend, 1), row_swap(attend_z[0], 1)
    attend_x2 = row_swap(jnp.stack(attend_z[1:]), 1)
    cross_z = three_ways(cross_line)
    grad_far, grad_near = swap(grad, 2), swap(grad, 1)
    self_att, self_lse = call(
        self_forward, [low(count, inner), wide(4, count)], (ids, marks, mixed_low), resident=True
    )
    text_all = join(ids, text, text_far, text_near, swap(text_far, 1))
    self_att, text_all, attend_x0, attend_x1, grad_far, *cross_z = sync(
        self_att, text_all, attend_x0, attend_x1, grad_far, *cross_z
    )
    received, attend_x2 = scatter_slots(self_att, w_self, 0, None, (attend_x2,))
    hidden = frames_wide + received
    w_query, w_pairs = place(
        ids, (512, 512), [attend, *attend_z], [attend_x0, attend_x1, attend_x2]
    )
    w_cross = place_line(ids, cross_line, *cross_z)
    grad_all = join(ids, grad, grad_far, grad_near, swap(grad_far, 1))
    text_count = text_all.shape[0]
    pairs_own = mm(text_all, w_pairs).astype(LOW)
    pairs_other = swap(pairs_own, 2)
    w_cross_far = swap(sync(w_cross, pairs_other)[0], 2)
    two, hat_two, inverse_two = norm_forward(hidden, gains[1], biases[1])
    two_pair = gather_pair(two, ids)
    pair_count = two_pair.shape[0]
    query = mm(two_pair, w_query).astype(LOW)
    cross_att, cross_lse = call(
        cross_forward,
        [low(pair_count, 2 * inner), wide(8, pair_count)],
        (ids, marks, query, pairs_own, pairs_other),
        resident=True,
    )
    w_cross_both = join(ids, w_cross, w_cross_far)
    hidden_two = hidden + scatter_pair(cross_att, w_cross_both, 0)
    three, hat_three, inverse_three = norm_forward(hidden_two, gains[2], biases[2])
    three_all = gather_slots(three, ids)
    w_up, w_down = w_ffn[:, :width], w_ffn[:, width:]
    activ, slope = gelu_parts(mm(three_all, w_up))

    grad_up = (mm(grad_all, w_down, 1, 1) * slope).astype(LOW)
    grad_three = scatter_slots(grad_up, w_up, 1)
    ffn_sums = sum_rows(weight_grads(three_all, grad_up, activ, grad_all))
    output_part = scatter_slots(activ, w_down, 0, grad_three)
    part, gain_three, bias_three = norm_backward(grad_three, hat_three, inverse_three, gains[2])
    grad_two = out_grad[0].astype(WIDE) + part
    branch_two = gather_pair(grad_two.astype(LOW), ids)
    grad_cross = mm(branch_two, w_cross_both, 1, 1).astype(LOW)
    grad_query, pairs_mine, pairs_away = call(
        cross_backward,
        [low(pair_count, 2 * inner)] + [low(text_count, 2 * inner)] * 2,
        (ids, marks, query, pairs_own, pairs_other, grad_cross, cross_lse),
        resident=True,
    )
    grad_query, pairs_away, output_part = sync(grad_query, pairs_away, output_part)
    output = (hidden_two + output_part).astype(LOW)
    pairs_came = swap(pairs_away, 2)
    g_cross = mm(cross_att, branch_two, 0, 0).astype(LOW)
    g_query = mm(two_pair, grad_query, 0, 0).astype(LOW)
    (attend_sent,) = call(attend_x, [low(4, 128, 1024)], (ids, g_query, g_cross))
    attend_came = row_swap(attend_sent, 1)
    part, gain_two, bias_two = norm_backward(
        scatter_pair(grad_query, w_query, 1), hat_two, inverse_two, gains[1]
    )
    grad_hidden = grad_two + part
    grad_low, pairs_came = sync(grad_hidden.astype(LOW), pairs_came)
    grad_pairs = (pairs_mine.astype(WIDE) + pairs_came.astype(WIDE)).astype(LOW)
    g_pairs = mm(text_all, grad_pairs, 0, 0).astype(LOW)
    (pairs_sent,) = call(pairs_x, [low(4, 128, 512)], (ids, g_pairs))
    pairs_came = row_swap(pairs_sent, 1)
    branch = gather_slots(grad_low, ids)
    text_part = scatter_slots(grad_pairs, w_pairs, 1, branch)
    grad_self = mm(branch, w_self, 1, 1).astype(LOW)
    (grad_mixed,) = call(
        self_backward,
        [low(count, 3 * inner)],
        (ids, marks, mixed_low, grad_self, self_lse),
        scratch=[pltpu.VMEM((count, 128), WIDE), pltpu.VMEM((count, 128), WIDE)],
        resident=True,
    )
    grad_mixed, attend_came, branch = sync(grad_mixed, attend_came, branch)
    sums = [wide(128, 1024)] + [low(128, 1024)] * 3
    attend_own, *attend_parts = call(attend_along_z, sums, (ids, g_query, g_cross, attend_came))
    attend_parts = along_z(attend_parts)
    g_mixed = mm(one_all, grad_mixed, 0, 0).astype(LOW)
    mixed_came = row_swap(pick(g_mixed.reshape(4, 2, 128, 768), 1 - (row & 1), 1), 1)
    g_self = mm(self_att, branch, 0, 0).astype(LOW)
    grad_one, g_self, text_part, pairs_came, *attend_parts = scatter_slots(
        grad_mixed, w_mixed, 1, None, (g_self, text_part, pairs_came, *attend_parts)
    )
    text_grad = text_part
    pairs_own, *pairs_parts = call(pairs_along_z, sums, (ids, g_pairs, g_self, pairs_came))
    pairs_parts = along_z(pairs_parts)
    grad_one, pairs_first = sync(grad_one, pairs_parts[0])
    part, gain_one, bias_one = norm_backward(grad_one, hat_one, inverse_one, gains[0])
    frame_grad = grad_hidden + part
    norm_sums = norms_over_text(
        ids, [gain_one, gain_two, gain_three, bias_one, bias_two, bias_three]
    )
    mixed_came, *pairs_parts = sync(mixed_came, pairs_first, *pairs_parts[1:])
    mixed_own, *mixed_parts = call(
        split_sums, [wide(128, 768)] + [low(128, 768)] * 3, (ids, g_mixed, mixed_came)
    )
    mixed_parts = along_z(mixed_parts)
    mixed_parts[0], norm_sums, ffn_sums, pairs_own = sync(
        mixed_parts[0], norm_sums, ffn_sums, pairs_own
    )
    norm_sums = over_rows(norm_sums)
    d_up, d_down = return_ffn(ids, ffn_sums)
    d_self, d_query, d_pairs, d_cross = return_attend(
        ids, attend_own, *attend_parts, pairs_own, *pairs_parts
    )
    d_mixed = return_mixed(ids, mixed_own, mixed_parts)
    return (
        output[None],
        frame_grad[None],
        text_grad[None],
        d_mixed,
        d_self,
        d_query,
        d_pairs,
        d_cross,
        d_up,
        d_down,
        norm_sums[:3],
        norm_sums[3:6],
    )


def local_general(
    frames,
    text_states,
    frame_segments,
    text_lengths,
    self_in,
    self_out,
    cross_query,
    cross_kv,
    cross_out,
    ffn_in,
    ffn_out,
    norm_gains,
    norm_biases,
    out_grad,
):
    here = lax.axis_index("text")
    row = lax.axis_index("rows")
    ids = jnp.stack([here, row]).astype(jnp.int32)
    row_count = lax.axis_size("rows")
    width = frames.shape[2]
    count = frames.shape[1] * WAYS
    inner = width // WAYS

    chunk = ffn_out.shape[0] // WAYS
    norms = jnp.concatenate([norm_gains, norm_biases], axis=0)
    norms = ordered(norms, swap(norms, 2), here >> 1)
    norms = ordered(norms, swap(norms, 1), here & 1, 1)
    norms = jnp.moveaxis(norms, 2, 0).reshape(6, width).astype(WIDE)
    gains, biases = norms[:3], norms[3:]
    depth = ffn_in.shape[0]
    gate = norms
    w_mixed = gather_rows(side_by_side(exchange(deal(self_in, 3), here)))
    w_query = gather_rows(side_by_side(exchange(deal(cross_query, 1), here)))
    w_query = jnp.concatenate([w_query, swap(w_query, 2)], axis=1)
    w_pairs = gather_rows(side_by_side(exchange(deal(cross_kv, 2), here)))
    w_self = own_heads(self_out, here)
    w_cross = own_heads(cross_out, here)
    w_up = gather_rows(side_by_side(exchange(deal(ffn_in, row_count // WAYS), here)))
    w_down = ffn_out.reshape(WAYS, chunk, inner)
    w_down = gather_rows(side_by_side(exchange(w_down, here)))

    marks = mask_marks(frame_segments[0], text_lengths[0])

    frames_wide = frames[0].astype(WIDE)
    one, hat_one, inverse_one = norm_forward(frames_wide, gains[0], biases[0])
    one_all = gather_slots(after(one, gate), ids)
    text_all = gather_slots(after(text_states[0], one_all), ids)
    grad_all = gather_slots(after(out_grad[0], text_all), ids)
    one_all = after(one_all, text_all, grad_all)
    mixed = mm(one_all, w_mixed).astype(LOW)
    self_att, self_lse = call(
        self_forward,
        [shaped((count, inner), LOW), shaped((4, count), WIDE)],
        (ids, marks, mixed),
        resident=True,
    )
    hidden = frames_wide + scatter_slots(self_att, w_self, 0)
    two, hat_two, inverse_two = norm_forward(hidden, gains[1], biases[1])
    two_pair = gather_pair(two, ids)
    pair_count = two_pair.shape[0]
    text_count = text_all.shape[0]
    pairs_own = mm(text_all, w_pairs).astype(LOW)
    pairs_other = swap(pairs_own, 2)
    w_cross_both = join(ids, w_cross, swap(after(w_cross, pairs_other), 2))
    query = mm(two_pair, w_query).astype(LOW)
    cross_att, cross_lse = call(
        cross_forward,
        [shaped((pair_count, 2 * inner), LOW), shaped((8, pair_count), WIDE)],
        (ids, marks, query, pairs_own, pairs_other),
        resident=True,
    )
    hidden_two = hidden + scatter_pair(cross_att, w_cross_both, 0)
    three, hat_three, inverse_three = norm_forward(hidden_two, gains[2], biases[2])
    three_all = gather_slots(three, ids)
    up = mm(three_all, w_up)
    activ, slope = gelu_parts(up)

    grad_up = (mm(grad_all, w_down, 1, 1) * slope).astype(LOW)
    grad_three = scatter_slots(grad_up, w_up, 1)
    g_up = mm(three_all, grad_up, 0, 0).astype(LOW)
    g_down = mm(activ, grad_all, 0, 0).astype(LOW)
    output = (hidden_two + scatter_slots(activ, w_down, 0, grad_three)).astype(LOW)
    part, gain_three, bias_three = norm_backward(grad_three, hat_three, inverse_three, gains[2])
    grad_two = out_grad[0].astype(WIDE) + part
    branch_two = gather_pair(grad_two.astype(LOW), ids)
    grad_cross = mm(branch_two, w_cross_both, 1, 1).astype(LOW)
    g_cross = mm(cross_att, branch_two, 0, 0).astype(LOW)
    grad_query, pairs_mine, pairs_away = call(
        cross_backward,
        [shaped((pair_count, 2 * inner), LOW)] + [shaped((text_count, 2 * inner), LOW)] * 2,
        (ids, marks, query, pairs_own, pairs_other, grad_cross, cross_lse),
        resident=True,
    )
    part, gain_two, bias_two = norm_backward(
        scatter_pair(grad_query, w_query, 1), hat_two, inverse_two, gains[1]
    )
    grad_pairs = (pairs_mine.astype(WIDE) + swap(pairs_away, 2).astype(WIDE)).astype(LOW)
    g_query = mm(two_pair, grad_query, 0, 0).astype(LOW)
    g_pairs = mm(text_all, grad_pairs, 0, 0).astype(LOW)
    grad_hidden = grad_two + part
    grad_low = grad_hidden.astype(LOW)
    branch = gather_slots(grad_low, ids)
    text_grad = scatter_slots(grad_pairs, w_pairs, 1, branch)
    grad_self = mm(branch, w_self, 1, 1).astype(LOW)
    g_self = mm(self_att, branch, 0, 0).astype(LOW)
    (grad_mixed,) = call(
        self_backward,
        [shaped((count, 3 * inner), LOW)],
        (ids, marks, mixed, grad_self, self_lse),
        scratch=[pltpu.VMEM((count, 128), WIDE), pltpu.VMEM((count, 128), WIDE)],
        resident=True,
    )
    g_mixed = mm(one_all, grad_mixed, 0, 0).astype(LOW)
    part, gain_one, bias_one = norm_backward(
        scatter_slots(grad_mixed, w_mixed, 1), hat_one, inverse_one, gains[0]
    )
    frame_grad = grad_hidden + part

    norm_sums = reduce_norms(
        [gain_one, gain_two, gain_three, bias_one, bias_two, bias_three], here
    )
    parts = jnp.concatenate([apart(sum_rows(g_up)), apart(sum_rows(g_down))], axis=1)
    parts = exchange(parts, here)
    d_up = undeal(parts[:, :depth], row_count // WAYS).astype(WIDE)
    d_down = parts[:, depth:].reshape(ffn_out.shape).astype(WIDE)
    g_query = g_query[:, :inner] + swap(g_query[:, inner:], 2)
    g_cross = g_cross[:inner] + swap(g_cross[inner:], 2)
    d_cross = return_heads(g_cross, here).astype(WIDE)
    d_self = return_heads(g_self, here).astype(WIDE)
    d_query = undeal(exchange(apart(sum_rows(g_query)), here), 1).astype(WIDE)
    d_pairs = undeal(exchange(apart(sum_rows(g_pairs)), here), 2).astype(WIDE)
    d_mixed = undeal(exchange(apart(sum_rows(g_mixed)), here), 3).astype(WIDE)
    return (
        output[None],
        frame_grad[None],
        text_grad[None],
        d_mixed,
        d_self,
        d_query,
        d_pairs,
        d_cross,
        d_up,
        d_down,
        norm_sums[:3],
        norm_sums[3:],
    )


def solution(mesh):
    in_specs = (
        P("rows", "text", None),
        P("rows", "text", None),
        P("rows", None),
        P("rows", None),
        P("rows", "text"),
        P("rows", "text"),
        P("rows", "text"),
        P("rows", "text"),
        P("rows", "text"),
        P("rows", "text"),
        P("rows", "text"),
        P(None, "text"),
        P(None, "text"),
        P("rows", "text", None),
    )
    out_specs = (
        P("rows", "text", None),
        P("rows", "text", None),
        P("rows", "text", None),
        P("rows", "text"),
        P("rows", "text"),
        P("rows", "text"),
        P("rows", "text"),
        P("rows", "text"),
        P("rows", "text"),
        P("rows", "text"),
        P(None, "text"),
        P(None, "text"),
    )
    local = local_grid if mesh.shape["rows"] == 8 else local_general
    return jax.shard_map(local, mesh=mesh, in_specs=in_specs, out_specs=out_specs, check_vma=False)
```

```python
import functools
import math

import jax
import jax.numpy as jnp
from jax import lax
from jax.experimental import pallas as pl
from jax.experimental.pallas import tpu as pltpu
from jax.sharding import PartitionSpec as P

HEADS = 16
WAYS = 4
SLOTS = (0, 2, 1, 3)
LOW = jnp.bfloat16
WIDE = jnp.float32
NEVER = -1e30


def mm(left, right, left_dim=1, right_dim=0):
    return lax.dot_general(
        left, right, (((left_dim,), (right_dim,)), ((), ())), preferred_element_type=WIDE
    )


def swap(values, mask):
    return lax.ppermute(values, "text", [(i, i ^ mask) for i in range(WAYS)])


def after(value, *events):
    return lax.optimization_barrier((value,) + events)[0]


def copy_all(pairs, sem):
    copies = [pltpu.make_async_copy(*pair, sem.at[i]) for i, pair in enumerate(pairs)]
    for copy in copies:
        copy.start()
    for copy in copies:
        copy.wait()


def join_rows(_, *refs):
    *blocks, whole, sem = refs
    size = whole.shape[0] // len(blocks)
    copy_all(
        [(block, whole.at[i * size : (i + 1) * size]) for i, block in enumerate(blocks)], sem
    )


def join(ids, *blocks):
    rows = sum(b.shape[0] for b in blocks)
    (whole,) = call(
        join_rows,
        [shaped((rows, blocks[0].shape[1]), LOW)],
        (ids, *blocks),
        own_copies=len(blocks),
    )
    return whole


def sync(*values):
    return lax.optimization_barrier(values)


def gather_slots(block, ids, *beside):
    near = swap(block, 1)
    far, *beside = sync(swap(block, 2), *beside)
    whole = join(ids, block, far, near, swap(far, 1))
    return (whole, *beside) if beside else whole


def scatter_slots(left, right, right_dim, gate=None, beside=()):
    half = left.shape[0] // 2
    block = half // 2
    away = mm(left[half:], right, 1, right_dim).astype(LOW)
    near = swap(away, 1)
    far = (mm(left[block:half], right, 1, right_dim) + near[block:].astype(WIDE)).astype(LOW)
    if gate is not None:
        far = after(far, gate)
    far, *beside = sync(swap(far, 2), *beside)
    here = mm(left[:block], right, 1, right_dim) + near[:block].astype(WIDE)
    result = here + far.astype(WIDE)
    return (result, *beside) if beside else result


def gather_pair(block, ids):
    return join(ids, block, swap(block, 1))


def scatter_pair(left, right, right_dim):
    half = left.shape[0] // 2
    away = mm(left[half:], right, 1, right_dim).astype(LOW)
    return mm(left[:half], right, 1, right_dim) + swap(away, 1).astype(WIDE)


def norm_forward(values, gain, bias):
    average = jnp.mean(values, axis=-1, keepdims=True)
    centred = values - average
    spread = jnp.mean(centred * centred, axis=-1, keepdims=True)
    inverse = lax.rsqrt(spread + 1e-05)
    hat = centred * inverse
    return (hat * gain + bias).astype(LOW), hat, inverse


def norm_backward(grad, hat, inverse, gain):
    weighted = grad * gain
    first = jnp.mean(weighted, axis=-1, keepdims=True)
    second = jnp.mean(weighted * hat, axis=-1, keepdims=True)
    return (
        (weighted - first - hat * second) * inverse,
        jnp.sum(grad * hat, axis=0),
        jnp.sum(grad, axis=0),
    )


def slot_of(index, here):
    other = index ^ here
    return ((other & 1) << 1) | (other >> 1)


def half_lanes(values, head):
    lane = lax.broadcasted_iota(jnp.int32, values.shape, 1)
    keep = (lane < 64) if head == 0 else (lane >= 64)
    return jnp.where(keep, values, jnp.zeros_like(values))


def nt(left, right):
    return mm(left, right, 1, 1)


def rows_at(ref, slot, size, pair, offset):
    start = pl.multiple_of(slot * size, size)
    return ref[pl.ds(start, size), offset + pair * 128 : offset + (pair + 1) * 128]


def transposed(values):
    return values.astype(WIDE).T


def self_forward(here_ref, marks_ref, mixed_ref, out_ref, lse_ref):
    here = here_ref[0]
    size = mixed_ref.shape[0] // WAYS
    down = lax.broadcasted_iota(jnp.int32, (size, size), 0)
    across = lax.broadcasted_iota(jnp.int32, (size, size), 1)
    for pair in range(2):
        keys = [rows_at(mixed_ref, slot_of(j, here), size, pair, 256) for j in range(WAYS)]
        values_t = [
            transposed(rows_at(mixed_ref, slot_of(j, here), size, pair, 512)).astype(LOW)
            for j in range(WAYS)
        ]
        for i in range(WAYS):
            mine = slot_of(i, here)
            query = rows_at(mixed_ref, mine, size, pair, 0) * LOW(0.125)
            first = marks_ref[0:1, i * size : (i + 1) * size]
            outs = []
            for head in range(2):
                scores = []
                for j in range(i + 1):
                    s = nt(half_lanes(keys[j], head), query)
                    allowed = (down + j * size) >= first
                    if j == i:
                        allowed = allowed & (down <= across)
                    scores.append(jnp.where(allowed, s, NEVER))
                top = jnp.max(scores[0], axis=0, keepdims=True)
                for s in scores[1:]:
                    top = jnp.maximum(top, jnp.max(s, axis=0, keepdims=True))
                total = jnp.zeros_like(top)
                result = jnp.zeros((64, size), WIDE)
                for j, s in enumerate(scores):
                    probs = jnp.exp(s - top)
                    total = total + jnp.sum(probs, axis=0, keepdims=True)
                    part = values_t[j][head * 64 : (head + 1) * 64]
                    result = result + mm(part, probs.astype(LOW))
                outs.append(result / total)
                lse_ref[2 * pair + head : 2 * pair + head + 1, i * size : (i + 1) * size] = (
                    top + jnp.log(total)
                )
            start = pl.multiple_of(mine * size, size)
            out_ref[pl.ds(start, size), pair * 128 : (pair + 1) * 128] = (
                jnp.concatenate(outs, axis=0).T.astype(LOW)
            )


def self_backward(here_ref, marks_ref, mixed_ref, grad_ref, lse_ref, out_ref, dk_ref, dv_ref):
    here = here_ref[0]
    size = mixed_ref.shape[0] // WAYS
    down = lax.broadcasted_iota(jnp.int32, (size, size), 0)
    across = lax.broadcasted_iota(jnp.int32, (size, size), 1)
    for pair in range(2):
        keys = [rows_at(mixed_ref, slot_of(j, here), size, pair, 256) for j in range(WAYS)]
        values = [rows_at(mixed_ref, slot_of(j, here), size, pair, 512) for j in range(WAYS)]
        keys_t = [transposed(k).astype(LOW) for k in keys]
        for i in reversed(range(WAYS)):
            mine = slot_of(i, here)
            query = rows_at(mixed_ref, mine, size, pair, 0) * LOW(0.125)
            grad = rows_at(grad_ref, mine, size, pair, 0)
            first = marks_ref[0:1, i * size : (i + 1) * size]
            grads_q = []
            dk_parts = [None] * (i + 1)
            dv_parts = [None] * (i + 1)
            for head in range(2):
                mass = lse_ref[2 * pair + head : 2 * pair + head + 1, i * size : (i + 1) * size]
                grad_head = half_lanes(grad, head)
                query_head = half_lanes(query, head)
                probs, grad_probs = [], []
                delta = jnp.zeros((1, size), WIDE)
                for j in range(i + 1):
                    s = nt(half_lanes(keys[j], head), query)
                    allowed = (down + j * size) >= first
                    if j == i:
                        allowed = allowed & (down <= across)
                    p = jnp.exp(jnp.where(allowed, s, NEVER) - mass)
                    dp = nt(half_lanes(values[j], head), grad)
                    delta = delta + jnp.sum(p * dp, axis=0, keepdims=True)
                    probs.append(p)
                    grad_probs.append(dp)
                grad_q = jnp.zeros((64, size), WIDE)
                for j in range(i + 1):
                    ds = (probs[j] * (grad_probs[j] - delta)).astype(LOW)
                    dv = mm(probs[j].astype(LOW), grad_head)
                    dk = mm(ds, query_head)
                    dv_parts[j] = dv if head == 0 else dv_parts[j] + dv
                    dk_parts[j] = dk if head == 0 else dk_parts[j] + dk
                    grad_q = grad_q + mm(keys_t[j][head * 64 : (head + 1) * 64], ds)
                grads_q.append(grad_q)
            start = pl.multiple_of(mine * size, size)
            out_ref[pl.ds(start, size), pair * 128 : (pair + 1) * 128] = (
                (jnp.concatenate(grads_q, axis=0) * 0.125).T.astype(LOW)
            )
            for j in range(i + 1):
                rows = slice(j * size, (j + 1) * size)
                if i == WAYS - 1:
                    dk_ref[rows] = dk_parts[j]
                    dv_ref[rows] = dv_parts[j]
                else:
                    dk_ref[rows] = dk_ref[rows] + dk_parts[j]
                    dv_ref[rows] = dv_ref[rows] + dv_parts[j]
        for j in range(WAYS):
            rows = slice(j * size, (j + 1) * size)
            start = pl.multiple_of(slot_of(j, here) * size, size)
            out_ref[pl.ds(start, size), 256 + pair * 128 : 256 + (pair + 1) * 128] = dk_ref[
                rows
            ].astype(LOW)
            out_ref[pl.ds(start, size), 512 + pair * 128 : 512 + (pair + 1) * 128] = dv_ref[
                rows
            ].astype(LOW)


def token_places(here, count, width):
    row = lax.broadcasted_iota(jnp.int32, (count, width), 0)
    size = count // WAYS
    place = row
    for slot, mask in enumerate(SLOTS):
        inside = (row >= slot * size) & (row < (slot + 1) * size)
        place = jnp.where(inside, row - slot * size + (here ^ mask) * size, place)
    return place


def text_allowed(here, marks_ref, block, size, count):
    start = pl.multiple_of((here ^ block) * size, size)
    low = marks_ref[1:2, pl.ds(start, size)]
    high = marks_ref[2:3, pl.ds(start, size)]
    places = [token_places(here, count, size), token_places(here ^ 2, count, size)]
    return [(place >= low) & (place < high) for place in places]


def cross_forward(here_ref, marks_ref, query_ref, own_ref, other_ref, out_ref, lse_ref):
    here = here_ref[0]
    size = query_ref.shape[0] // 2
    allowed = [text_allowed(here, marks_ref, b, size, own_ref.shape[0]) for b in range(2)]
    for pair in range(4):
        ref = (own_ref, other_ref)[pair // 2]
        column = (pair % 2) * 128
        keys = ref[:, column : column + 128]
        values_t = transposed(ref[:, 256 + column : 384 + column]).astype(LOW)
        for block in range(2):
            rows = slice(block * size, (block + 1) * size)
            query = query_ref[rows, pair * 128 : (pair + 1) * 128] * LOW(0.125)
            outs = []
            for head in range(2):
                s = nt(half_lanes(keys, head), query)
                s = jnp.where(allowed[block][pair // 2], s, NEVER)
                top = jnp.max(s, axis=0, keepdims=True)
                probs = jnp.exp(s - top)
                total = jnp.sum(probs, axis=0, keepdims=True)
                result = mm(values_t[head * 64 : (head + 1) * 64], probs.astype(LOW))
                outs.append(result / total)
                lse_ref[2 * pair + head : 2 * pair + head + 1, rows] = top + jnp.log(total)
            out_ref[rows, pair * 128 : (pair + 1) * 128] = (
                jnp.concatenate(outs, axis=0).T.astype(LOW)
            )


def cross_backward(
    here_ref, marks_ref, query_ref, own_ref, other_ref, grad_ref, lse_ref, dq_ref, down_ref, dother_ref
):
    here = here_ref[0]
    size = query_ref.shape[0] // 2
    allowed = [text_allowed(here, marks_ref, b, size, own_ref.shape[0]) for b in range(2)]
    for pair in range(4):
        ref, out = ((own_ref, down_ref), (other_ref, dother_ref))[pair // 2]
        column = (pair % 2) * 128
        keys = ref[:, column : column + 128]
        values = ref[:, 256 + column : 384 + column]
        keys_t = transposed(keys).astype(LOW)
        sum_k = jnp.zeros(keys.shape, WIDE)
        sum_v = jnp.zeros(keys.shape, WIDE)
        for block in range(2):
            rows = slice(block * size, (block + 1) * size)
            query = query_ref[rows, pair * 128 : (pair + 1) * 128] * LOW(0.125)
            grad = grad_ref[rows, pair * 128 : (pair + 1) * 128]
            grads_q = []
            for head in range(2):
                mass = lse_ref[2 * pair + head : 2 * pair + head + 1, rows]
                s = nt(half_lanes(keys, head), query)
                p = jnp.exp(jnp.where(allowed[block][pair // 2], s, NEVER) - mass)
                dp = nt(half_lanes(values, head), grad)
                delta = jnp.sum(p * dp, axis=0, keepdims=True)
                ds = (p * (dp - delta)).astype(LOW)
                sum_v = sum_v + mm(p.astype(LOW), half_lanes(grad, head))
                sum_k = sum_k + mm(ds, half_lanes(query, head))
                grads_q.append(mm(keys_t[head * 64 : (head + 1) * 64], ds))
            dq_ref[rows, pair * 128 : (pair + 1) * 128] = (
                (jnp.concatenate(grads_q, axis=0) * 0.125).T.astype(LOW)
            )
        out[:, column : column + 128] = sum_k.astype(LOW)
        out[:, 256 + column : 384 + column] = sum_v.astype(LOW)


def bring_in(body, number, ids_ref, *refs):
    scratch, sem = refs[len(refs) - number - 1 : -1], refs[-1]
    copies = [
        pltpu.make_async_copy(refs[i], scratch[i], sem.at[i]) for i in range(number)
    ]
    for copy in copies:
        copy.start()
    for copy in copies:
        copy.wait()
    body(ids_ref, *scratch, *refs[number : len(refs) - number - 1])


def call(body, outs, operands, scratch=(), resident=False, own_copies=0):
    vmem = pl.BlockSpec(memory_space=pltpu.VMEM)
    spec = vmem if resident else pl.BlockSpec(memory_space=pltpu.HBM)
    scratch = list(scratch)
    if own_copies:
        scratch.append(pltpu.SemaphoreType.DMA((own_copies,)))
    elif not resident:
        scratch = [pltpu.VMEM(v.shape, v.dtype) for v in operands[1:]]
        scratch.append(pltpu.SemaphoreType.DMA((len(scratch),)))
        body = functools.partial(bring_in, body, len(operands) - 1)
    moved = sum(v.size * v.dtype.itemsize for v in (*operands, *outs))
    return pl.pallas_call(
        body,
        out_shape=outs,
        in_specs=[pl.BlockSpec(memory_space=pltpu.SMEM)] + [spec for v in operands[1:]],
        out_specs=[vmem for v in outs],
        scratch_shapes=scratch,
        cost_estimate=pl.CostEstimate(flops=0, bytes_accessed=moved, transcendentals=0),
        compiler_params=pltpu.CompilerParams(vmem_limit_bytes=48 << 20),
    )(*operands)


def weight_block(left_a, right_a, left_b, right_b, out_ref):
    @pl.when(pl.program_id(0) == 0)
    def _():
        out_ref[...] = mm(left_a[...], right_a[...], 0, 0).astype(LOW)

    @pl.when(pl.program_id(0) == 1)
    def _():
        out_ref[...] = mm(left_b[...], right_b[...], 0, 0).astype(LOW)


def weight_grads(left_a, right_a, left_b, right_b):
    count, rows = left_a.shape
    columns = right_a.shape[1]
    tile = 256
    last = rows // tile - 1
    return pl.pallas_call(
        weight_block,
        grid=(2, rows // tile),
        out_shape=shaped((rows, 2 * columns), LOW),
        in_specs=[
            pl.BlockSpec((count, tile), lambda w, i: (0, jnp.where(w == 0, i, last))),
            pl.BlockSpec((count, columns), lambda w, i: (0, 0)),
            pl.BlockSpec((count, tile), lambda w, i: (0, jnp.where(w == 0, 0, i))),
            pl.BlockSpec((count, columns), lambda w, i: (0, 0)),
        ],
        out_specs=pl.BlockSpec((tile, columns), lambda w, i: (i, w)),
        cost_estimate=pl.CostEstimate(
            flops=4 * count * rows * columns,
            bytes_accessed=4 * count * (rows + columns) + 4 * rows * columns,
            transcendentals=0,
        ),
        compiler_params=pltpu.CompilerParams(vmem_limit_bytes=48 << 20),
    )(left_a, right_a, left_b, right_b)


def shaped(shape, dtype):
    return jax.ShapeDtypeStruct(shape, dtype)


def deal(matrix, groups):
    depth, width = matrix.shape
    piece = width // (groups * WAYS)
    return jnp.moveaxis(matrix.reshape(depth, groups, WAYS, piece), 2, 0).reshape(
        WAYS, depth, groups * piece
    )


def undeal(dealt, groups):
    _, depth, width = dealt.shape
    return jnp.moveaxis(dealt.reshape(WAYS, depth, groups, width // groups), 0, 2).reshape(
        depth, WAYS * width
    )


def pick(values, index, axis):
    return lax.dynamic_index_in_dim(values, index, axis, keepdims=False)


def ordered(mine, other, bit, axis=0):
    return jnp.stack([jnp.where(bit == 0, mine, other), jnp.where(bit == 0, other, mine)], axis)


def exchange(dealt, here, *gates):
    core, far = here & 1, here >> 1
    tail = dealt.shape[1:]
    dealt = dealt.reshape((2, 2) + tail)
    stage = ordered(pick(dealt, core, 1), swap(pick(dealt, 1 - core, 1), 1), core, 1)
    sent = pick(stage, 1 - far, 0)
    if gates:
        sent = after(sent, *gates)
    return ordered(pick(stage, far, 0), swap(sent, 2), far).reshape((WAYS,) + tail)


def side_by_side(parts):
    return jnp.moveaxis(parts, 0, 1).reshape(parts.shape[1], -1)


def apart(columns):
    depth, width = columns.shape
    return jnp.moveaxis(columns.reshape(depth, WAYS, width // WAYS), 1, 0)


def row_swap(values, mask):
    size = lax.axis_size("rows")
    return lax.ppermute(values, "rows", [(i, i ^ mask) for i in range(size)])


def gather_rows(block):
    return lax.all_gather(block, "rows", axis=0, tiled=True)


def sum_rows(whole):
    return lax.psum_scatter(whole, "rows", scatter_dimension=0, tiled=True)


def place_pieces(depth, splits, ids_ref, *refs):
    row, outs, sem = ids_ref[1], refs[7:-1], refs[-1]
    pairs = []
    for k in range(4):
        for flip in range(2):
            owner = (row ^ flip) ^ (2 * k)
            start = pl.multiple_of(owner * depth, depth)
            column = 0
            for index, width in enumerate(splits):
                columns = slice(column, column + width)
                if not flip:
                    piece = refs[k].at[:, columns]
                elif k < 2:
                    piece = refs[4 + k].at[:, columns]
                else:
                    piece = refs[6].at[k - 2, :, columns]
                pairs.append((piece, outs[index].at[pl.ds(start, depth)]))
                column += width
    copy_all(pairs, sem)


def place(ids, splits, pieces, others):
    depth = pieces[0].shape[0]
    return call(
        functools.partial(place_pieces, depth, splits),
        [shaped((8 * depth, width), LOW) for width in splits],
        (ids, *pieces, *others),
        own_copies=8 * len(splits),
    )


def place_line_pieces(ids_ref, *refs):
    far = ids_ref[1] >> 1
    height = refs[0].shape[0]
    pairs = []
    for k in range(4):
        start = pl.multiple_of((far ^ k) * height, height)
        pairs.append((refs[k], refs[4].at[pl.ds(start, height)]))
    copy_all(pairs, refs[5])


def place_line(ids, *pieces):
    whole = shaped((4 * pieces[0].shape[0], pieces[0].shape[1]), LOW)
    return call(place_line_pieces, [whole], (ids, *pieces), own_copies=4)[0]


def three_ways(block):
    return [row_swap(block, 2 * k) for k in range(1, 4)]


def split_sums(row_ref, whole_ref, sent_ref, own_ref, *low_refs):
    row = row_ref[1]
    x, far = row & 1, row >> 1
    depth = own_ref.shape[0]
    for k in range(4):
        owner = far ^ k
        start = pl.multiple_of((owner * 2 + x) * depth, depth)
        value = whole_ref[pl.ds(start, depth)].astype(WIDE) + sent_ref[owner].astype(WIDE)
        if k == 0:
            own_ref[...] = value
        else:
            low_refs[k - 1][...] = value.astype(LOW)


def choose(bit, zero, one):
    return jnp.where(bit == 0, zero, one)


def put(ref, column, *values):
    for value in values:
        ref[:, column : column + value.shape[1]] = value.astype(ref.dtype)
        column += value.shape[1]


def total(refs):
    value = refs[0][...]
    for ref in refs[1:]:
        value = value + ref[...].astype(WIDE)
    return value


def device_bits(ids_ref):
    here, row = ids_ref[0], ids_ref[1]
    return here & 1, here >> 1, row & 1, row >> 1


def keep_and_send(kept, sent, column, bit, zero, one):
    put(kept, column, choose(bit, zero, one))
    put(sent, column, choose(bit, one, zero))
    return column + zero.shape[1]


def deal_first_core(ids, self_in, self_out, cross_out, norms, kept, sent):
    core, _, _, _ = device_bits(ids)
    depth = self_in.shape[0]
    for y in range(2):
        for j in range(3):
            first, column = (4 * j + 2 * y) * 64, (3 * y + j) * 64
            zero, one = self_in[:, first : first + 64], self_in[:, first + 64 : first + 128]
            kept[:depth, column : column + 64] = choose(core, zero, one)
            sent[:depth, column : column + 64] = choose(core, one, zero)
    for index, ref in enumerate((self_out, cross_out)):
        rows = slice(64 * index, 64 * (index + 1))
        kept[rows, 384:] = choose(core, ref[:64], ref[64:])
        sent[rows, 384:] = choose(core, ref[64:], ref[:64])
    for ref in (kept, sent):
        ref[depth:] = jnp.zeros_like(ref[depth:])
        ref[depth : depth + norms.shape[0], :256] = norms[...]


def deal_first_far(ids, kept, came, far_kept, far_sent):
    core, y, _, _ = device_bits(ids)
    depth = 128
    column = 0
    sources = [choose(core, kept[...], came[...]), choose(core, came[...], kept[...])]
    for source in sources:
        columns = slice(column, column + 192)
        zero, one = source[:depth, :192], source[:depth, 192:384]
        far_kept[:depth, columns] = choose(y, zero, one)
        far_sent[:depth, columns] = choose(y, one, zero)
        column += 192
    for index, source in enumerate(sources):
        for ref in (far_kept, far_sent):
            ref[:depth, column : column + 256] = source[:depth, 384:]
            ref[depth:, index * 256 : (index + 1) * 256] = source[depth:, :256]
        column += 256
    for ref in (far_kept, far_sent):
        ref[depth:, 512:] = jnp.zeros_like(ref[depth:, 512:])


def deal_first_last(ids, kept, came, mixed, lines, norms):
    _, y, _, _ = device_bits(ids)
    zero, one = choose(y, kept[...], came[...]), choose(y, came[...], kept[...])
    put(mixed, 0, zero[:128, :384], one[:128, :384])
    put(lines, 0, zero[:128, 384:], one[:128, 384:])
    put(norms, 0, zero[128:, :512], one[128:, :512])


def deal_rest_core(ids, query, pairs, up, down, kept, sent):
    core, _, _, _ = device_bits(ids)
    column = 0
    for y in range(2):
        for r in range(2):
            first = (4 * r + 2 * y) * 128
            zero, one = up[:, first : first + 128], up[:, first + 128 : first + 256]
            column = keep_and_send(kept, sent, column, core, zero, one)
    for y in range(2):
        zero, one = [down[(2 * y + c) * 128 : (2 * y + c + 1) * 128] for c in range(2)]
        column = keep_and_send(kept, sent, column, core, zero, one)
    for y in range(2):
        for j in range(2):
            first = (4 * j + 2 * y) * 64
            zero, one = pairs[:, first : first + 64], pairs[:, first + 64 : first + 128]
            column = keep_and_send(kept, sent, column, core, zero, one)
    for y in range(2):
        zero, one = query[:, 128 * y : 128 * y + 64], query[:, 128 * y + 64 : 128 * y + 128]
        column = keep_and_send(kept, sent, column, core, zero, one)


def deal_rest_far(ids, kept, came, far_kept, far_sent):
    core, y, _, _ = device_bits(ids)
    sources = [choose(core, kept[...], came[...]), choose(core, came[...], kept[...])]
    column = 0
    for first, width in ((0, 256), (512, 256), (1024, 128)):
        for source in sources:
            zero = source[:, first : first + width]
            one = source[:, first + width : first + 2 * width]
            column = keep_and_send(far_kept, far_sent, column, y, zero, one)
    for source in sources:
        put(far_kept, column, source[:, 1280:])
        put(far_sent, column, source[:, 1280:])
        column += 128


def deal_rest_last(ids, kept, came, attend, ffn):
    _, y, _, _ = device_bits(ids)
    sources = [choose(y, kept[...], came[...]), choose(y, came[...], kept[...])]
    put(ffn, 0, *[s[:, :512] for s in sources], *[s[:, 512:1024] for s in sources])
    put(attend, 512, *[s[:, 1024:1280] for s in sources])
    for group in range(2):
        for place, source in enumerate(sources):
            for c in range(2):
                first = 1280 + c * 128
                zero = source[:, first + group * 64 : first + group * 64 + 64]
                one = source[:, first + (1 - group) * 64 : first + (1 - group) * 64 + 64]
                put(attend, group * 256 + (2 * place + c) * 64, choose(y, zero, one))


def ffn_far(ids, value, kept, sent):
    _, y, _, _ = device_bits(ids)
    for half in range(2):
        zero = value[:, half * 1024 : half * 1024 + 512]
        one = value[:, half * 1024 + 512 : half * 1024 + 1024]
        put(kept, half * 512, choose(y, zero, one))
        put(sent, half * 512, choose(y, one, zero))


def ffn_core(ids, kept, came, core_kept, core_sent):
    core, y, _, _ = device_bits(ids)
    mine, other = kept[...], came[...]
    column = 0
    for source in (choose(y, mine, other), choose(y, other, mine)):
        for half in range(2):
            zero = source[:, half * 512 : half * 512 + 256]
            one = source[:, half * 512 + 256 : half * 512 + 512]
            put(core_kept, column, choose(core, zero, one))
            put(core_sent, column, choose(core, one, zero))
            column += 256


def ffn_last(ids, kept, came, up, down):
    core, _, _, _ = device_bits(ids)
    mine, other = kept[...], came[...]
    for c, source in enumerate((choose(core, mine, other), choose(core, other, mine))):
        for y in range(2):
            sender = 2 * y + c
            for r in range(2):
                first = 512 * y + 128 * r
                put(up, (4 * r + sender) * 128, source[:, first : first + 128])
            rows = slice(sender * 128, (sender + 1) * 128)
            down[rows] = source[:, 512 * y + 256 : 512 * y + 512].astype(WIDE)


def mixed_far(ids, own, a, b, c, kept, sent):
    _, y, _, _ = device_bits(ids)
    value = total((own, a, b, c))
    put(kept, 0, choose(y, value[:, :384], value[:, 384:]))
    put(sent, 0, choose(y, value[:, 384:], value[:, :384]))


def mixed_core(ids, kept, came, core_kept, core_sent):
    core, y, _, _ = device_bits(ids)
    mine, other = kept[...], came[...].astype(WIDE)
    for index, source in enumerate((choose(y, mine, other), choose(y, other, mine))):
        put(core_kept, 192 * index, choose(core, source[:, :192], source[:, 192:]))
        put(core_sent, 192 * index, choose(core, source[:, 192:], source[:, :192]))


def mixed_last(ids, kept, came, mixed):
    core, _, _, _ = device_bits(ids)
    mine, other = kept[...], came[...].astype(WIDE)
    for c, source in enumerate((choose(core, mine, other), choose(core, other, mine))):
        for y in range(2):
            for j in range(3):
                first = 192 * y + 64 * j
                put(mixed, (4 * j + 2 * y + c) * 64, source[:, first : first + 64])


def attend_x(ids, query, cross, sent):
    _, y, x, _ = device_bits(ids)
    for z in range(4):
        start = pl.multiple_of((2 * z + 1 - x) * 128, 128)
        line = pl.multiple_of(((y ^ x ^ 1) * 4 + z) * 64, 64)
        sent[z, :, :512] = query[pl.ds(start, 128)]
        sent[z, :64, 512:] = cross[pl.ds(line, 64), :512]
        sent[z, 64:, 512:] = cross[pl.ds(line, 64), 512:]


def pairs_x(ids, pairs, sent):
    _, _, x, _ = device_bits(ids)
    for z in range(4):
        sent[z] = pairs[pl.ds(pl.multiple_of((2 * z + 1 - x) * 128, 128), 128)]


def attend_along_z(ids, query, cross, came, own, a, b, c):
    _, y, x, z = device_bits(ids)
    for k, ref in enumerate((own, a, b, c)):
        owner = z ^ k
        start = pl.multiple_of((2 * owner + x) * 128, 128)
        line = pl.multiple_of(((y ^ x) * 4 + owner) * 64, 64)
        moved = came[owner].astype(WIDE)
        value = query[pl.ds(start, 128)].astype(WIDE) + moved[:, :512]
        ref[:, :512] = value.astype(ref.dtype)
        value = cross[pl.ds(line, 64)].astype(WIDE)
        ref[:64, 512:] = (value[:, :512] + moved[:64, 512:]).astype(ref.dtype)
        ref[64:, 512:] = (value[:, 512:] + moved[64:, 512:]).astype(ref.dtype)


def pairs_along_z(ids, pairs, self_out, came, own, a, b, c):
    _, _, x, z = device_bits(ids)
    for k, ref in enumerate((own, a, b, c)):
        owner = z ^ k
        start = pl.multiple_of((2 * owner + x) * 128, 128)
        below = pl.multiple_of(owner * 64, 64)
        value = pairs[pl.ds(start, 128)].astype(WIDE) + came[owner].astype(WIDE)
        ref[:, :512] = value.astype(ref.dtype)
        ref[:64, 512:] = self_out[pl.ds(below, 64), :512].astype(ref.dtype)
        ref[64:, 512:] = self_out[pl.ds(below, 64), 512:].astype(ref.dtype)


def attend_total(ids, *refs):
    value, line = refs[8:]
    value[:, :1024] = total(refs[:4])
    value[:, 1024:] = total(refs[4:8])
    line[...] = value[:, 1536:].astype(LOW)


def attend_far(ids, value, line, kept, sent):
    _, y, _, _ = device_bits(ids)
    own = value[:, 1536:] + line[...].astype(WIDE)
    low_half = jnp.concatenate([own[:64], value[:64, 512:1024]], axis=0)
    high_half = jnp.concatenate([own[64:], value[64:, 512:1024]], axis=0)
    put(kept, 0, choose(y, low_half, high_half))
    put(sent, 0, choose(y, high_half, low_half))
    mine, other = value[:, :256], value[:, 256:512]
    for index, group in enumerate((choose(y, mine, other), choose(y, other, mine))):
        put(kept, 512 + 128 * index, choose(y, group[:, :128], group[:, 128:]))
        put(sent, 512 + 128 * index, choose(y, group[:, 128:], group[:, :128]))
    pairs = value[:, 1024:1536]
    put(kept, 768, choose(y, pairs[:, :256], pairs[:, 256:]))
    put(sent, 768, choose(y, pairs[:, 256:], pairs[:, :256]))


def attend_core(ids, kept, came, core_kept, core_sent):
    core, y, x, _ = device_bits(ids)
    mine, other = kept[...], came[...].astype(WIDE)
    owner = jnp.where(x == y, mine[:64, :512], other[:64, :512])
    lines = jnp.concatenate([owner, mine[64:, :512] + other[64:, :512]], axis=0)
    put(core_kept, 0, choose(core, lines[:, :256], lines[:, 256:]))
    put(core_sent, 0, choose(core, lines[:, 256:], lines[:, :256]))
    query = mine[:, 512:768] + other[:, 512:768]
    for group in range(2):
        zero, one = [query[:, 128 * group + 64 * c : 128 * group + 64 * c + 64] for c in range(2)]
        put(core_kept, 256 + 64 * group, choose(core, zero, one))
        put(core_sent, 256 + 64 * group, choose(core, one, zero))
    mine, other = mine[:, 768:], other[:, 768:]
    for index, source in enumerate((choose(y, mine, other), choose(y, other, mine))):
        put(core_kept, 384 + 128 * index, choose(core, source[:, :128], source[:, 128:]))
        put(core_sent, 384 + 128 * index, choose(core, source[:, 128:], source[:, :128]))


def attend_last(ids, kept, came, self_out, query, pairs, cross):
    core, _, _, _ = device_bits(ids)
    mine, other = kept[...], came[...].astype(WIDE)
    for c, source in enumerate((choose(core, mine, other), choose(core, other, mine))):
        self_out[64 * c : 64 * c + 64] = source[:64, :256]
        cross[64 * c : 64 * c + 64] = source[64:, :256]
        for y in range(2):
            put(query, 64 * (2 * y + c), source[:, 256 + 64 * y : 320 + 64 * y])
            for j in range(2):
                first = 384 + 128 * y + 64 * j
                put(pairs, 64 * (4 * j + 2 * y + c), source[:, first : first + 64])


def along_z(values):
    return [row_swap(v, 2 * (k + 1)) for k, v in enumerate(values)]


def return_ffn(ids, sums):
    low = lambda *shape: shaped(shape, LOW)
    wide = lambda *shape: shaped(shape, WIDE)
    kept, sent = call(ffn_far, [low(128, 1024)] * 2, (ids, sums))
    kept, sent = call(ffn_core, [low(128, 1024)] * 2, (ids, kept, swap(sent, 2)))
    return call(ffn_last, [wide(128, 1024), wide(512, 256)], (ids, kept, swap(sent, 1)))


def return_mixed(ids, own, parts):
    low = lambda *shape: shaped(shape, LOW)
    wide = lambda *shape: shaped(shape, WIDE)
    kept, sent = call(mixed_far, [wide(128, 384), low(128, 384)], (ids, own, *parts))
    kept, sent = call(mixed_core, [wide(128, 384), low(128, 384)], (ids, kept, swap(sent, 2)))
    (mixed,) = call(mixed_last, [wide(128, 768)], (ids, kept, swap(sent, 1)))
    return mixed


def return_attend(ids, *parts):
    low = lambda *shape: shaped(shape, LOW)
    wide = lambda *shape: shaped(shape, WIDE)
    value, line = call(attend_total, [wide(128, 2048), low(128, 512)], (ids, *parts))
    kept, sent = call(
        attend_far, [wide(128, 1024), low(128, 1024)], (ids, value, row_swap(line, 1))
    )
    kept, sent = call(attend_core, [wide(128, 640), low(128, 640)], (ids, kept, swap(sent, 2)))
    return call(
        attend_last,
        [wide(128, 256), wide(128, 256), wide(128, 512), wide(128, 256)],
        (ids, kept, swap(sent, 1)),
    )


def own_heads(matrix, here):
    rows = gather_rows(lax.all_gather(matrix, "text", axis=1, tiled=True))
    width = rows.shape[1]
    grouped = rows.reshape(HEADS // WAYS, WAYS, -1, width)
    return pick(grouped, here, 1).reshape(-1, width)


def return_heads(grad, here):
    count, width = grad.shape
    spread = jnp.zeros((HEADS // WAYS, WAYS, count * WAYS // HEADS, width), grad.dtype)
    spread = lax.dynamic_update_index_in_dim(
        spread, grad.reshape(HEADS // WAYS, 1, -1, width), here, 1
    )
    columns = lax.psum_scatter(
        spread.reshape(count * WAYS, width), "text", scatter_dimension=1, tiled=True
    )
    return sum_rows(columns)


def mask_marks(segments, lengths):
    clip = jnp.arange(lengths.shape[0], dtype=jnp.int32)
    ends = jnp.sum(jnp.where(clip[None, :] <= clip[:, None], lengths[None, :], 0), axis=1)
    begins = jnp.sum((segments[None, :] < clip[:, None]).astype(jnp.int32), axis=1)
    same = (segments[None, :] == clip[:, None]).astype(jnp.int32)
    rows = [begins, ends - lengths, ends] + [jnp.zeros_like(ends)] * 5
    return jnp.stack([jnp.sum(same * values[:, None], axis=0) for values in rows])


def gelu_parts(up):
    phi = 0.5 * (1.0 + lax.erf(up * math.sqrt(0.5)))
    slope = phi + up * (jnp.exp(-0.5 * up * up) * (1.0 / math.sqrt(2.0 * math.pi)))
    return lax.optimization_barrier(((up * phi).astype(LOW), slope))


def norms_core(ids, *refs):
    core, _, _, _ = device_bits(ids)
    kept, sent = refs[6:]
    for ref in (kept, sent):
        ref[...] = jnp.zeros_like(ref)
    for index, row in enumerate(refs[:6]):
        for y in range(2):
            zero, one = [row[:, (2 * y + c) * 256 : (2 * y + c + 1) * 256] for c in range(2)]
            columns = slice(256 * y, 256 * (y + 1))
            kept[index : index + 1, columns] = choose(core, zero, one)
            sent[index : index + 1, columns] = choose(core, one, zero)


def norms_far(ids, kept, came, far_kept, far_sent):
    _, y, _, _ = device_bits(ids)
    value = kept[...] + came[...]
    far_kept[...] = choose(y, value[:, :256], value[:, 256:])
    far_sent[...] = choose(y, value[:, 256:], value[:, :256])


def norms_over_text(ids, rows):
    wide = lambda *shape: shaped(shape, WIDE)
    kept, sent = call(norms_core, [wide(8, 512)] * 2, (ids, *[r[None] for r in rows]))
    kept, sent = call(norms_far, [wide(8, 256)] * 2, (ids, kept, swap(sent, 1)))
    return kept + swap(sent, 2)


def over_rows(sums):
    mask = 1
    while mask < lax.axis_size("rows"):
        sums = sums + row_swap(sums, mask)
        mask = 2 * mask
    return sums


def reduce_norms(rows, here):
    split = jnp.stack(rows).reshape(6, 2, 2, -1)
    split = pick(split, here & 1, 2) + swap(pick(split, 1 - (here & 1), 2), 1)
    return over_rows(pick(split, here >> 1, 1) + swap(pick(split, 1 - (here >> 1), 1), 2))


def local_grid(
    frames,
    text_states,
    frame_segments,
    text_lengths,
    self_in,
    self_out,
    cross_query,
    cross_kv,
    cross_out,
    ffn_in,
    ffn_out,
    norm_gains,
    norm_biases,
    out_grad,
):
    here, row = lax.axis_index("text"), lax.axis_index("rows")
    ids = jnp.stack([here, row]).astype(jnp.int32)
    width = frames.shape[2]
    count = frames.shape[1] * WAYS
    inner = width // WAYS
    low = lambda *shape: shaped(shape, LOW)
    wide = lambda *shape: shaped(shape, WIDE)
    marks = mask_marks(frame_segments[0], text_lengths[0])

    norms = jnp.concatenate([norm_gains, norm_biases], axis=0)
    kept, sent = call(
        deal_first_core, [low(144, 640)] * 2, (ids, self_in, self_out, cross_out, norms)
    )
    kept, sent = call(deal_first_far, [low(144, 896)] * 2, (ids, kept, swap(sent, 1)))
    came = swap(sent, 2)
    (frames_low,) = sync(frames[0], sent)[:1]
    frames_wide = frames_low.astype(WIDE)
    rest = sync(cross_query, cross_kv, ffn_in, ffn_out, sent)[:4]
    rest_kept, rest_sent = call(deal_rest_core, [low(128, 1408)] * 2, (ids, *rest))
    rest_kept, rest_sent = call(
        deal_rest_far, [low(128, 1536)] * 2, (ids, rest_kept, swap(rest_sent, 1))
    )
    mixed, lines, norms = call(
        deal_first_last, [low(128, 768), low(128, 1024), wide(16, 1024)], (ids, kept, came)
    )
    gains, biases = norms[:3], norms[3:6]
    one, hat_one, inverse_one = norm_forward(frames_wide, gains[0], biases[0])
    mixed, lines, rest_sent, one = sync(mixed, lines, rest_sent, one)
    mixed_z = three_ways(mixed)
    mixed_x = row_swap(mixed, 1)
    lines_x = row_swap(lines, 1)
    mixed_x1 = row_swap(mixed_z[0], 1)
    rest_came = swap(rest_sent, 2)
    one_far, one_near = swap(one, 2), swap(one, 1)
    attend, ffn_block = call(
        deal_rest_last, [low(128, 1024), low(128, 2048)], (ids, rest_kept, rest_came)
    )
    lines = jnp.where((row & 1) == (here >> 1), lines, lines_x)
    *mixed_z, mixed_x, mixed_x1, attend, lines, one_far, text, grad = sync(
        *mixed_z, mixed_x, mixed_x1, attend, lines, one_far, text_states[0], out_grad[0]
    )
    mixed_x2 = row_swap(jnp.stack(mixed_z[1:]), 1)
    self_line, cross_line = lines[:64], lines[64:]
    self_z = three_ways(self_line)
    attend_z = three_ways(attend)
    one_all = join(ids, one, one_far, one_near, swap(one_far, 1))
    text_far, text_near = swap(text, 2), swap(text, 1)
    mixed_x2, one_all, text_far, *self_z, ffn_block = sync(
        mixed_x2, one_all, text_far, *self_z, ffn_block
    )
    w_ffn = gather_rows(ffn_block)
    (w_mixed,) = place(ids, (768,), [mixed, *mixed_z], [mixed_x, mixed_x1, mixed_x2])
    mixed_low = mm(one_all, w_mixed).astype(LOW)
    w_self = place_line(ids, self_line, *self_z)
    mixed_low, *attend_z, grad, attend, cross_line, w_self = sync(
        mixed_low, *attend_z, grad, attend, cross_line, w_self
    )
    attend_x0, attend_x1 = row_swap(attend, 1), row_swap(attend_z[0], 1)
    attend_x2 = row_swap(jnp.stack(attend_z[1:]), 1)
    cross_z = three_ways(cross_line)
    grad_far, grad_near = swap(grad, 2), swap(grad, 1)
    self_att, self_lse = call(
        self_forward, [low(count, inner), wide(4, count)], (ids, marks, mixed_low), resident=True
    )
    text_all = join(ids, text, text_far, text_near, swap(text_far, 1))
    self_att, text_all, attend_x0, attend_x1, grad_far, *cross_z = sync(
        self_att, text_all, attend_x0, attend_x1, grad_far, *cross_z
    )
    received, attend_x2 = scatter_slots(self_att, w_self, 0, None, (attend_x2,))
    hidden = frames_wide + received
    w_query, w_pairs = place(
        ids, (512, 512), [attend, *attend_z], [attend_x0, attend_x1, attend_x2]
    )
    w_cross = place_line(ids, cross_line, *cross_z)
    grad_all = join(ids, grad, grad_far, grad_near, swap(grad_far, 1))
    text_count = text_all.shape[0]
    pairs_own = mm(text_all, w_pairs).astype(LOW)
    pairs_other = swap(pairs_own, 2)
    w_cross_far = swap(sync(w_cross, pairs_other)[0], 2)
    two, hat_two, inverse_two = norm_forward(hidden, gains[1], biases[1])
    two_pair = gather_pair(two, ids)
    pair_count = two_pair.shape[0]
    query = mm(two_pair, w_query).astype(LOW)
    cross_att, cross_lse = call(
        cross_forward,
        [low(pair_count, 2 * inner), wide(8, pair_count)],
        (ids, marks, query, pairs_own, pairs_other),
        resident=True,
    )
    w_cross_both = join(ids, w_cross, w_cross_far)
    hidden_two = hidden + scatter_pair(cross_att, w_cross_both, 0)
    three, hat_three, inverse_three = norm_forward(hidden_two, gains[2], biases[2])
    three_all = gather_slots(three, ids)
    w_up, w_down = w_ffn[:, :width], w_ffn[:, width:]
    activ, slope = gelu_parts(mm(three_all, w_up))

    grad_up = (mm(grad_all, w_down, 1, 1) * slope).astype(LOW)
    g_ffn = weight_grads(three_all, grad_up, activ, grad_all)
    grad_three, g_ffn = scatter_slots(grad_up, w_up, 1, None, (g_ffn,))
    ffn_sums = sum_rows(g_ffn)
    output_part = scatter_slots(activ, w_down, 0, grad_three)
    part, gain_three, bias_three = norm_backward(grad_three, hat_three, inverse_three, gains[2])
    grad_two = out_grad[0].astype(WIDE) + part
    branch_two = gather_pair(grad_two.astype(LOW), ids)
    grad_cross = mm(branch_two, w_cross_both, 1, 1).astype(LOW)
    grad_query, pairs_mine, pairs_away = call(
        cross_backward,
        [low(pair_count, 2 * inner)] + [low(text_count, 2 * inner)] * 2,
        (ids, marks, query, pairs_own, pairs_other, grad_cross, cross_lse),
        resident=True,
    )
    grad_query, pairs_away, output_part = sync(grad_query, pairs_away, output_part)
    output = (hidden_two + output_part).astype(LOW)
    pairs_came = swap(pairs_away, 2)
    g_cross = mm(cross_att, branch_two, 0, 0).astype(LOW)
    g_query = mm(two_pair, grad_query, 0, 0).astype(LOW)
    (attend_sent,) = call(attend_x, [low(4, 128, 1024)], (ids, g_query, g_cross))
    attend_came = row_swap(attend_sent, 1)
    part, gain_two, bias_two = norm_backward(
        scatter_pair(grad_query, w_query, 1), hat_two, inverse_two, gains[1]
    )
    grad_hidden = grad_two + part
    grad_low, pairs_came = sync(grad_hidden.astype(LOW), pairs_came)
    grad_pairs = (pairs_mine.astype(WIDE) + pairs_came.astype(WIDE)).astype(LOW)
    g_pairs = mm(text_all, grad_pairs, 0, 0).astype(LOW)
    (pairs_sent,) = call(pairs_x, [low(4, 128, 512)], (ids, g_pairs))
    pairs_came = row_swap(pairs_sent, 1)
    branch = gather_slots(grad_low, ids)
    text_part = scatter_slots(grad_pairs, w_pairs, 1, branch)
    grad_self = mm(branch, w_self, 1, 1).astype(LOW)
    (grad_mixed,) = call(
        self_backward,
        [low(count, 3 * inner)],
        (ids, marks, mixed_low, grad_self, self_lse),
        scratch=[pltpu.VMEM((count, 128), WIDE), pltpu.VMEM((count, 128), WIDE)],
        resident=True,
    )
    grad_mixed, attend_came, branch = sync(grad_mixed, attend_came, branch)
    sums = [wide(128, 1024)] + [low(128, 1024)] * 3
    attend_own, *attend_parts = call(attend_along_z, sums, (ids, g_query, g_cross, attend_came))
    attend_parts = along_z(attend_parts)
    g_mixed = mm(one_all, grad_mixed, 0, 0).astype(LOW)
    mixed_came = row_swap(pick(g_mixed.reshape(4, 2, 128, 768), 1 - (row & 1), 1), 1)
    g_self = mm(self_att, branch, 0, 0).astype(LOW)
    grad_one, g_self, text_part, pairs_came, *attend_parts = scatter_slots(
        grad_mixed, w_mixed, 1, None, (g_self, text_part, pairs_came, *attend_parts)
    )
    text_grad = text_part
    pairs_own, *pairs_parts = call(pairs_along_z, sums, (ids, g_pairs, g_self, pairs_came))
    pairs_parts = along_z(pairs_parts)
    grad_one, pairs_first = sync(grad_one, pairs_parts[0])
    part, gain_one, bias_one = norm_backward(grad_one, hat_one, inverse_one, gains[0])
    frame_grad = grad_hidden + part
    norm_sums = norms_over_text(
        ids, [gain_one, gain_two, gain_three, bias_one, bias_two, bias_three]
    )
    mixed_came, *pairs_parts = sync(mixed_came, pairs_first, *pairs_parts[1:])
    mixed_own, *mixed_parts = call(
        split_sums, [wide(128, 768)] + [low(128, 768)] * 3, (ids, g_mixed, mixed_came)
    )
    mixed_parts = along_z(mixed_parts)
    mixed_parts[0], norm_sums, ffn_sums, pairs_own = sync(
        mixed_parts[0], norm_sums, ffn_sums, pairs_own
    )
    norm_sums = over_rows(norm_sums)
    d_up, d_down = return_ffn(ids, ffn_sums)
    d_self, d_query, d_pairs, d_cross = return_attend(
        ids, attend_own, *attend_parts, pairs_own, *pairs_parts
    )
    d_mixed = return_mixed(ids, mixed_own, mixed_parts)
    return (
        output[None],
        frame_grad[None],
        text_grad[None],
        d_mixed,
        d_self,
        d_query,
        d_pairs,
        d_cross,
        d_up,
        d_down,
        norm_sums[:3],
        norm_sums[3:6],
    )


def local_general(
    frames,
    text_states,
    frame_segments,
    text_lengths,
    self_in,
    self_out,
    cross_query,
    cross_kv,
    cross_out,
    ffn_in,
    ffn_out,
    norm_gains,
    norm_biases,
    out_grad,
):
    here = lax.axis_index("text")
    row = lax.axis_index("rows")
    ids = jnp.stack([here, row]).astype(jnp.int32)
    row_count = lax.axis_size("rows")
    width = frames.shape[2]
    count = frames.shape[1] * WAYS
    inner = width // WAYS

    chunk = ffn_out.shape[0] // WAYS
    norms = jnp.concatenate([norm_gains, norm_biases], axis=0)
    norms = ordered(norms, swap(norms, 2), here >> 1)
    norms = ordered(norms, swap(norms, 1), here & 1, 1)
    norms = jnp.moveaxis(norms, 2, 0).reshape(6, width).astype(WIDE)
    gains, biases = norms[:3], norms[3:]
    depth = ffn_in.shape[0]
    gate = norms
    w_mixed = gather_rows(side_by_side(exchange(deal(self_in, 3), here)))
    w_query = gather_rows(side_by_side(exchange(deal(cross_query, 1), here)))
    w_query = jnp.concatenate([w_query, swap(w_query, 2)], axis=1)
    w_pairs = gather_rows(side_by_side(exchange(deal(cross_kv, 2), here)))
    w_self = own_heads(self_out, here)
    w_cross = own_heads(cross_out, here)
    w_up = gather_rows(side_by_side(exchange(deal(ffn_in, row_count // WAYS), here)))
    w_down = ffn_out.reshape(WAYS, chunk, inner)
    w_down = gather_rows(side_by_side(exchange(w_down, here)))

    marks = mask_marks(frame_segments[0], text_lengths[0])

    frames_wide = frames[0].astype(WIDE)
    one, hat_one, inverse_one = norm_forward(frames_wide, gains[0], biases[0])
    one_all = gather_slots(after(one, gate), ids)
    text_all = gather_slots(after(text_states[0], one_all), ids)
    grad_all = gather_slots(after(out_grad[0], text_all), ids)
    one_all = after(one_all, text_all, grad_all)
    mixed = mm(one_all, w_mixed).astype(LOW)
    self_att, self_lse = call(
        self_forward,
        [shaped((count, inner), LOW), shaped((4, count), WIDE)],
        (ids, marks, mixed),
        resident=True,
    )
    hidden = frames_wide + scatter_slots(self_att, w_self, 0)
    two, hat_two, inverse_two = norm_forward(hidden, gains[1], biases[1])
    two_pair = gather_pair(two, ids)
    pair_count = two_pair.shape[0]
    text_count = text_all.shape[0]
    pairs_own = mm(text_all, w_pairs).astype(LOW)
    pairs_other = swap(pairs_own, 2)
    w_cross_both = join(ids, w_cross, swap(after(w_cross, pairs_other), 2))
    query = mm(two_pair, w_query).astype(LOW)
    cross_att, cross_lse = call(
        cross_forward,
        [shaped((pair_count, 2 * inner), LOW), shaped((8, pair_count), WIDE)],
        (ids, marks, query, pairs_own, pairs_other),
        resident=True,
    )
    hidden_two = hidden + scatter_pair(cross_att, w_cross_both, 0)
    three, hat_three, inverse_three = norm_forward(hidden_two, gains[2], biases[2])
    three_all = gather_slots(three, ids)
    up = mm(three_all, w_up)
    activ, slope = gelu_parts(up)

    grad_up = (mm(grad_all, w_down, 1, 1) * slope).astype(LOW)
    grad_three = scatter_slots(grad_up, w_up, 1)
    g_up = mm(three_all, grad_up, 0, 0).astype(LOW)
    g_down = mm(activ, grad_all, 0, 0).astype(LOW)
    output = (hidden_two + scatter_slots(activ, w_down, 0, grad_three)).astype(LOW)
    part, gain_three, bias_three = norm_backward(grad_three, hat_three, inverse_three, gains[2])
    grad_two = out_grad[0].astype(WIDE) + part
    branch_two = gather_pair(grad_two.astype(LOW), ids)
    grad_cross = mm(branch_two, w_cross_both, 1, 1).astype(LOW)
    g_cross = mm(cross_att, branch_two, 0, 0).astype(LOW)
    grad_query, pairs_mine, pairs_away = call(
        cross_backward,
        [shaped((pair_count, 2 * inner), LOW)] + [shaped((text_count, 2 * inner), LOW)] * 2,
        (ids, marks, query, pairs_own, pairs_other, grad_cross, cross_lse),
        resident=True,
    )
    part, gain_two, bias_two = norm_backward(
        scatter_pair(grad_query, w_query, 1), hat_two, inverse_two, gains[1]
    )
    grad_pairs = (pairs_mine.astype(WIDE) + swap(pairs_away, 2).astype(WIDE)).astype(LOW)
    g_query = mm(two_pair, grad_query, 0, 0).astype(LOW)
    g_pairs = mm(text_all, grad_pairs, 0, 0).astype(LOW)
    grad_hidden = grad_two + part
    grad_low = grad_hidden.astype(LOW)
    branch = gather_slots(grad_low, ids)
    text_grad = scatter_slots(grad_pairs, w_pairs, 1, branch)
    grad_self = mm(branch, w_self, 1, 1).astype(LOW)
    g_self = mm(self_att, branch, 0, 0).astype(LOW)
    (grad_mixed,) = call(
        self_backward,
        [shaped((count, 3 * inner), LOW)],
        (ids, marks, mixed, grad_self, self_lse),
        scratch=[pltpu.VMEM((count, 128), WIDE), pltpu.VMEM((count, 128), WIDE)],
        resident=True,
    )
    g_mixed = mm(one_all, grad_mixed, 0, 0).astype(LOW)
    part, gain_one, bias_one = norm_backward(
        scatter_slots(grad_mixed, w_mixed, 1), hat_one, inverse_one, gains[0]
    )
    frame_grad = grad_hidden + part

    norm_sums = reduce_norms(
        [gain_one, gain_two, gain_three, bias_one, bias_two, bias_three], here
    )
    parts = jnp.concatenate([apart(sum_rows(g_up)), apart(sum_rows(g_down))], axis=1)
    parts = exchange(parts, here)
    d_up = undeal(parts[:, :depth], row_count // WAYS).astype(WIDE)
    d_down = parts[:, depth:].reshape(ffn_out.shape).astype(WIDE)
    g_query = g_query[:, :inner] + swap(g_query[:, inner:], 2)
    g_cross = g_cross[:inner] + swap(g_cross[inner:], 2)
    d_cross = return_heads(g_cross, here).astype(WIDE)
    d_self = return_heads(g_self, here).astype(WIDE)
    d_query = undeal(exchange(apart(sum_rows(g_query)), here), 1).astype(WIDE)
    d_pairs = undeal(exchange(apart(sum_rows(g_pairs)), here), 2).astype(WIDE)
    d_mixed = undeal(exchange(apart(sum_rows(g_mixed)), here), 3).astype(WIDE)
    return (
        output[None],
        frame_grad[None],
        text_grad[None],
        d_mixed,
        d_self,
        d_query,
        d_pairs,
        d_cross,
        d_up,
        d_down,
        norm_sums[:3],
        norm_sums[3:],
    )


def solution(mesh):
    in_specs = (
        P("rows", "text", None),
        P("rows", "text", None),
        P("rows", None),
        P("rows", None),
        P("rows", "text"),
        P("rows", "text"),
        P("rows", "text"),
        P("rows", "text"),
        P("rows", "text"),
        P("rows", "text"),
        P("rows", "text"),
        P(None, "text"),
        P(None, "text"),
        P("rows", "text", None),
    )
    out_specs = (
        P("rows", "text", None),
        P("rows", "text", None),
        P("rows", "text", None),
        P("rows", "text"),
        P("rows", "text"),
        P("rows", "text"),
        P("rows", "text"),
        P("rows", "text"),
        P("rows", "text"),
        P("rows", "text"),
        P(None, "text"),
        P(None, "text"),
    )
    local = local_grid if mesh.shape["rows"] == 8 else local_general
    return jax.shard_map(local, mesh=mesh, in_specs=in_specs, out_specs=out_specs, check_vma=False)
```

```python
import functools
import math

import jax
import jax.numpy as jnp
from jax import lax
from jax.experimental import pallas as pl
from jax.experimental.pallas import tpu as pltpu
from jax.sharding import PartitionSpec as P

HEADS = 16
WAYS = 4
SLOTS = (0, 2, 1, 3)
LOW = jnp.bfloat16
WIDE = jnp.float32
NEVER = -1e30


def mm(left, right, left_dim=1, right_dim=0):
    return lax.dot_general(
        left, right, (((left_dim,), (right_dim,)), ((), ())), preferred_element_type=WIDE
    )


def swap(values, mask):
    return lax.ppermute(values, "text", [(i, i ^ mask) for i in range(WAYS)])


def after(value, *events):
    return lax.optimization_barrier((value,) + events)[0]


def copy_all(pairs, sem):
    copies = [pltpu.make_async_copy(*pair, sem.at[i]) for i, pair in enumerate(pairs)]
    for copy in copies:
        copy.start()
    for copy in copies:
        copy.wait()


def join_rows(_, *refs):
    *blocks, whole, sem = refs
    size = whole.shape[0] // len(blocks)
    copy_all(
        [(block, whole.at[i * size : (i + 1) * size]) for i, block in enumerate(blocks)], sem
    )


def join(ids, *blocks):
    rows = sum(b.shape[0] for b in blocks)
    (whole,) = call(
        join_rows,
        [shaped((rows, blocks[0].shape[1]), LOW)],
        (ids, *blocks),
        own_copies=len(blocks),
    )
    return whole


def sync(*values):
    return lax.optimization_barrier(values)


def gather_slots(block, ids, *beside):
    near = swap(block, 1)
    far, *beside = sync(swap(block, 2), *beside)
    whole = join(ids, block, far, near, swap(far, 1))
    return (whole, *beside) if beside else whole


def scatter_slots(left, right, right_dim, gate=None, beside=()):
    half = left.shape[0] // 2
    block = half // 2
    away = mm(left[half:], right, 1, right_dim).astype(LOW)
    near = swap(away, 1)
    far = (mm(left[block:half], right, 1, right_dim) + near[block:].astype(WIDE)).astype(LOW)
    if gate is not None:
        far = after(far, gate)
    far, *beside = sync(swap(far, 2), *beside)
    here = mm(left[:block], right, 1, right_dim) + near[:block].astype(WIDE)
    result = here + far.astype(WIDE)
    return (result, *beside) if beside else result


def gather_pair(block, ids):
    return join(ids, block, swap(block, 1))


def scatter_pair(left, right, right_dim):
    half = left.shape[0] // 2
    away = mm(left[half:], right, 1, right_dim).astype(LOW)
    return mm(left[:half], right, 1, right_dim) + swap(away, 1).astype(WIDE)


def norm_forward(values, gain, bias):
    average = jnp.mean(values, axis=-1, keepdims=True)
    centred = values - average
    spread = jnp.mean(centred * centred, axis=-1, keepdims=True)
    inverse = lax.rsqrt(spread + 1e-05)
    hat = centred * inverse
    return (hat * gain + bias).astype(LOW), hat, inverse


def norm_backward(grad, hat, inverse, gain):
    weighted = grad * gain
    first = jnp.mean(weighted, axis=-1, keepdims=True)
    second = jnp.mean(weighted * hat, axis=-1, keepdims=True)
    return (
        (weighted - first - hat * second) * inverse,
        jnp.sum(grad * hat, axis=0),
        jnp.sum(grad, axis=0),
    )


def slot_of(index, here):
    other = index ^ here
    return ((other & 1) << 1) | (other >> 1)


def half_lanes(values, head):
    lane = lax.broadcasted_iota(jnp.int32, values.shape, 1)
    keep = (lane < 64) if head == 0 else (lane >= 64)
    return jnp.where(keep, values, jnp.zeros_like(values))


def nt(left, right):
    return mm(left, right, 1, 1)


def rows_at(ref, slot, size, pair, offset):
    start = pl.multiple_of(slot * size, size)
    return ref[pl.ds(start, size), offset + pair * 128 : offset + (pair + 1) * 128]


def transposed(values):
    return values.astype(WIDE).T


def self_forward(here_ref, marks_ref, mixed_ref, out_ref, lse_ref):
    here = here_ref[0]
    size = mixed_ref.shape[0] // WAYS
    down = lax.broadcasted_iota(jnp.int32, (size, size), 0)
    across = lax.broadcasted_iota(jnp.int32, (size, size), 1)
    for pair in range(2):
        keys = [rows_at(mixed_ref, slot_of(j, here), size, pair, 256) for j in range(WAYS)]
        values_t = [
            transposed(rows_at(mixed_ref, slot_of(j, here), size, pair, 512)).astype(LOW)
            for j in range(WAYS)
        ]
        for i in range(WAYS):
            mine = slot_of(i, here)
            query = rows_at(mixed_ref, mine, size, pair, 0) * LOW(0.125)
            first = marks_ref[0:1, i * size : (i + 1) * size]
            outs = []
            for head in range(2):
                scores = []
                for j in range(i + 1):
                    s = nt(half_lanes(keys[j], head), query)
                    allowed = (down + j * size) >= first
                    if j == i:
                        allowed = allowed & (down <= across)
                    scores.append(jnp.where(allowed, s, NEVER))
                top = jnp.max(scores[0], axis=0, keepdims=True)
                for s in scores[1:]:
                    top = jnp.maximum(top, jnp.max(s, axis=0, keepdims=True))
                total = jnp.zeros_like(top)
                result = jnp.zeros((64, size), WIDE)
                for j, s in enumerate(scores):
                    probs = jnp.exp(s - top)
                    total = total + jnp.sum(probs, axis=0, keepdims=True)
                    part = values_t[j][head * 64 : (head + 1) * 64]
                    result = result + mm(part, probs.astype(LOW))
                outs.append(result / total)
                lse_ref[2 * pair + head : 2 * pair + head + 1, i * size : (i + 1) * size] = (
                    top + jnp.log(total)
                )
            start = pl.multiple_of(mine * size, size)
            out_ref[pl.ds(start, size), pair * 128 : (pair + 1) * 128] = (
                jnp.concatenate(outs, axis=0).T.astype(LOW)
            )


def self_backward(here_ref, marks_ref, mixed_ref, grad_ref, lse_ref, out_ref, dk_ref, dv_ref):
    here = here_ref[0]
    size = mixed_ref.shape[0] // WAYS
    down = lax.broadcasted_iota(jnp.int32, (size, size), 0)
    across = lax.broadcasted_iota(jnp.int32, (size, size), 1)
    for pair in range(2):
        keys = [rows_at(mixed_ref, slot_of(j, here), size, pair, 256) for j in range(WAYS)]
        values = [rows_at(mixed_ref, slot_of(j, here), size, pair, 512) for j in range(WAYS)]
        keys_t = [transposed(k).astype(LOW) for k in keys]
        for i in reversed(range(WAYS)):
            mine = slot_of(i, here)
            query = rows_at(mixed_ref, mine, size, pair, 0) * LOW(0.125)
            grad = rows_at(grad_ref, mine, size, pair, 0)
            first = marks_ref[0:1, i * size : (i + 1) * size]
            grads_q = []
            dk_parts = [None] * (i + 1)
            dv_parts = [None] * (i + 1)
            for head in range(2):
                mass = lse_ref[2 * pair + head : 2 * pair + head + 1, i * size : (i + 1) * size]
                grad_head = half_lanes(grad, head)
                query_head = half_lanes(query, head)
                probs, grad_probs = [], []
                delta = jnp.zeros((1, size), WIDE)
                for j in range(i + 1):
                    s = nt(half_lanes(keys[j], head), query)
                    allowed = (down + j * size) >= first
                    if j == i:
                        allowed = allowed & (down <= across)
                    p = jnp.exp(jnp.where(allowed, s, NEVER) - mass)
                    dp = nt(half_lanes(values[j], head), grad)
                    delta = delta + jnp.sum(p * dp, axis=0, keepdims=True)
                    probs.append(p)
                    grad_probs.append(dp)
                grad_q = jnp.zeros((64, size), WIDE)
                for j in range(i + 1):
                    ds = (probs[j] * (grad_probs[j] - delta)).astype(LOW)
                    dv = mm(probs[j].astype(LOW), grad_head)
                    dk = mm(ds, query_head)
                    dv_parts[j] = dv if head == 0 else dv_parts[j] + dv
                    dk_parts[j] = dk if head == 0 else dk_parts[j] + dk
                    grad_q = grad_q + mm(keys_t[j][head * 64 : (head + 1) * 64], ds)
                grads_q.append(grad_q)
            start = pl.multiple_of(mine * size, size)
            out_ref[pl.ds(start, size), pair * 128 : (pair + 1) * 128] = (
                (jnp.concatenate(grads_q, axis=0) * 0.125).T.astype(LOW)
            )
            for j in range(i + 1):
                rows = slice(j * size, (j + 1) * size)
                if i == WAYS - 1:
                    dk_ref[rows] = dk_parts[j]
                    dv_ref[rows] = dv_parts[j]
                else:
                    dk_ref[rows] = dk_ref[rows] + dk_parts[j]
                    dv_ref[rows] = dv_ref[rows] + dv_parts[j]
        for j in range(WAYS):
            rows = slice(j * size, (j + 1) * size)
            start = pl.multiple_of(slot_of(j, here) * size, size)
            out_ref[pl.ds(start, size), 256 + pair * 128 : 256 + (pair + 1) * 128] = dk_ref[
                rows
            ].astype(LOW)
            out_ref[pl.ds(start, size), 512 + pair * 128 : 512 + (pair + 1) * 128] = dv_ref[
                rows
            ].astype(LOW)


def token_places(here, count, width):
    row = lax.broadcasted_iota(jnp.int32, (count, width), 0)
    size = count // WAYS
    place = row
    for slot, mask in enumerate(SLOTS):
        inside = (row >= slot * size) & (row < (slot + 1) * size)
        place = jnp.where(inside, row - slot * size + (here ^ mask) * size, place)
    return place


def text_allowed(here, marks_ref, block, size, count):
    start = pl.multiple_of((here ^ block) * size, size)
    low = marks_ref[1:2, pl.ds(start, size)]
    high = marks_ref[2:3, pl.ds(start, size)]
    places = [token_places(here, count, size), token_places(here ^ 2, count, size)]
    return [(place >= low) & (place < high) for place in places]


def cross_forward(here_ref, marks_ref, query_ref, own_ref, other_ref, out_ref, lse_ref):
    here = here_ref[0]
    size = query_ref.shape[0] // 2
    allowed = [text_allowed(here, marks_ref, b, size, own_ref.shape[0]) for b in range(2)]
    for pair in range(4):
        ref = (own_ref, other_ref)[pair // 2]
        column = (pair % 2) * 128
        keys = ref[:, column : column + 128]
        values_t = transposed(ref[:, 256 + column : 384 + column]).astype(LOW)
        for block in range(2):
            rows = slice(block * size, (block + 1) * size)
            query = query_ref[rows, pair * 128 : (pair + 1) * 128] * LOW(0.125)
            outs = []
            for head in range(2):
                s = nt(half_lanes(keys, head), query)
                s = jnp.where(allowed[block][pair // 2], s, NEVER)
                top = jnp.max(s, axis=0, keepdims=True)
                probs = jnp.exp(s - top)
                total = jnp.sum(probs, axis=0, keepdims=True)
                result = mm(values_t[head * 64 : (head + 1) * 64], probs.astype(LOW))
                outs.append(result / total)
                lse_ref[2 * pair + head : 2 * pair + head + 1, rows] = top + jnp.log(total)
            out_ref[rows, pair * 128 : (pair + 1) * 128] = (
                jnp.concatenate(outs, axis=0).T.astype(LOW)
            )


def cross_backward(
    here_ref, marks_ref, query_ref, own_ref, other_ref, grad_ref, lse_ref, dq_ref, down_ref, dother_ref
):
    here = here_ref[0]
    size = query_ref.shape[0] // 2
    allowed = [text_allowed(here, marks_ref, b, size, own_ref.shape[0]) for b in range(2)]
    for pair in range(4):
        ref, out = ((own_ref, down_ref), (other_ref, dother_ref))[pair // 2]
        column = (pair % 2) * 128
        keys = ref[:, column : column + 128]
        values = ref[:, 256 + column : 384 + column]
        keys_t = transposed(keys).astype(LOW)
        sum_k = jnp.zeros(keys.shape, WIDE)
        sum_v = jnp.zeros(keys.shape, WIDE)
        for block in range(2):
            rows = slice(block * size, (block + 1) * size)
            query = query_ref[rows, pair * 128 : (pair + 1) * 128] * LOW(0.125)
            grad = grad_ref[rows, pair * 128 : (pair + 1) * 128]
            grads_q = []
            for head in range(2):
                mass = lse_ref[2 * pair + head : 2 * pair + head + 1, rows]
                s = nt(half_lanes(keys, head), query)
                p = jnp.exp(jnp.where(allowed[block][pair // 2], s, NEVER) - mass)
                dp = nt(half_lanes(values, head), grad)
                delta = jnp.sum(p * dp, axis=0, keepdims=True)
                ds = (p * (dp - delta)).astype(LOW)
                sum_v = sum_v + mm(p.astype(LOW), half_lanes(grad, head))
                sum_k = sum_k + mm(ds, half_lanes(query, head))
                grads_q.append(mm(keys_t[head * 64 : (head + 1) * 64], ds))
            dq_ref[rows, pair * 128 : (pair + 1) * 128] = (
                (jnp.concatenate(grads_q, axis=0) * 0.125).T.astype(LOW)
            )
        out[:, column : column + 128] = sum_k.astype(LOW)
        out[:, 256 + column : 384 + column] = sum_v.astype(LOW)


def bring_in(body, number, ids_ref, *refs):
    scratch, sem = refs[len(refs) - number - 1 : -1], refs[-1]
    copies = [
        pltpu.make_async_copy(refs[i], scratch[i], sem.at[i]) for i in range(number)
    ]
    for copy in copies:
        copy.start()
    for copy in copies:
        copy.wait()
    body(ids_ref, *scratch, *refs[number : len(refs) - number - 1])


def call(body, outs, operands, scratch=(), resident=False, own_copies=0):
    vmem = pl.BlockSpec(memory_space=pltpu.VMEM)
    spec = vmem if resident else pl.BlockSpec(memory_space=pltpu.HBM)
    scratch = list(scratch)
    if own_copies:
        scratch.append(pltpu.SemaphoreType.DMA((own_copies,)))
    elif not resident:
        scratch = [pltpu.VMEM(v.shape, v.dtype) for v in operands[1:]]
        scratch.append(pltpu.SemaphoreType.DMA((len(scratch),)))
        body = functools.partial(bring_in, body, len(operands) - 1)
    moved = sum(v.size * v.dtype.itemsize for v in (*operands, *outs))
    return pl.pallas_call(
        body,
        out_shape=outs,
        in_specs=[pl.BlockSpec(memory_space=pltpu.SMEM)] + [spec for v in operands[1:]],
        out_specs=[vmem for v in outs],
        scratch_shapes=scratch,
        cost_estimate=pl.CostEstimate(flops=0, bytes_accessed=moved, transcendentals=0),
        compiler_params=pltpu.CompilerParams(vmem_limit_bytes=48 << 20),
    )(*operands)


def weight_block(left_a, right_a, left_b, right_b, out_ref):
    @pl.when(pl.program_id(0) == 0)
    def _():
        out_ref[...] = mm(left_a[...], right_a[...], 0, 0).astype(LOW)

    @pl.when(pl.program_id(0) == 1)
    def _():
        out_ref[...] = mm(left_b[...], right_b[...], 0, 0).astype(LOW)


def weight_grads(left_a, right_a, left_b, right_b):
    count, rows = left_a.shape
    columns = right_a.shape[1]
    tile = 256
    last = rows // tile - 1
    return pl.pallas_call(
        weight_block,
        grid=(2, rows // tile),
        out_shape=shaped((rows, 2 * columns), LOW),
        in_specs=[
            pl.BlockSpec((count, tile), lambda w, i: (0, jnp.where(w == 0, i, last))),
            pl.BlockSpec((count, columns), lambda w, i: (0, 0)),
            pl.BlockSpec((count, tile), lambda w, i: (0, jnp.where(w == 0, 0, i))),
            pl.BlockSpec((count, columns), lambda w, i: (0, 0)),
        ],
        out_specs=pl.BlockSpec((tile, columns), lambda w, i: (i, w)),
        cost_estimate=pl.CostEstimate(
            flops=4 * count * rows * columns,
            bytes_accessed=4 * count * (rows + columns) + 4 * rows * columns,
            transcendentals=0,
        ),
        compiler_params=pltpu.CompilerParams(vmem_limit_bytes=48 << 20),
    )(left_a, right_a, left_b, right_b)


def shaped(shape, dtype):
    return jax.ShapeDtypeStruct(shape, dtype)


def deal(matrix, groups):
    depth, width = matrix.shape
    piece = width // (groups * WAYS)
    return jnp.moveaxis(matrix.reshape(depth, groups, WAYS, piece), 2, 0).reshape(
        WAYS, depth, groups * piece
    )


def undeal(dealt, groups):
    _, depth, width = dealt.shape
    return jnp.moveaxis(dealt.reshape(WAYS, depth, groups, width // groups), 0, 2).reshape(
        depth, WAYS * width
    )


def pick(values, index, axis):
    return lax.dynamic_index_in_dim(values, index, axis, keepdims=False)


def ordered(mine, other, bit, axis=0):
    return jnp.stack([jnp.where(bit == 0, mine, other), jnp.where(bit == 0, other, mine)], axis)


def exchange(dealt, here, *gates):
    core, far = here & 1, here >> 1
    tail = dealt.shape[1:]
    dealt = dealt.reshape((2, 2) + tail)
    stage = ordered(pick(dealt, core, 1), swap(pick(dealt, 1 - core, 1), 1), core, 1)
    sent = pick(stage, 1 - far, 0)
    if gates:
        sent = after(sent, *gates)
    return ordered(pick(stage, far, 0), swap(sent, 2), far).reshape((WAYS,) + tail)


def side_by_side(parts):
    return jnp.moveaxis(parts, 0, 1).reshape(parts.shape[1], -1)


def apart(columns):
    depth, width = columns.shape
    return jnp.moveaxis(columns.reshape(depth, WAYS, width // WAYS), 1, 0)


def row_swap(values, mask):
    size = lax.axis_size("rows")
    return lax.ppermute(values, "rows", [(i, i ^ mask) for i in range(size)])


def gather_rows(block):
    return lax.all_gather(block, "rows", axis=0, tiled=True)


def sum_rows(whole):
    return lax.psum_scatter(whole, "rows", scatter_dimension=0, tiled=True)


def place_pieces(depth, splits, ids_ref, *refs):
    row, outs, sem = ids_ref[1], refs[7:-1], refs[-1]
    pairs = []
    for k in range(4):
        for flip in range(2):
            owner = (row ^ flip) ^ (2 * k)
            start = pl.multiple_of(owner * depth, depth)
            column = 0
            for index, width in enumerate(splits):
                columns = slice(column, column + width)
                if not flip:
                    piece = refs[k].at[:, columns]
                elif k < 2:
                    piece = refs[4 + k].at[:, columns]
                else:
                    piece = refs[6].at[k - 2, :, columns]
                pairs.append((piece, outs[index].at[pl.ds(start, depth)]))
                column += width
    copy_all(pairs, sem)


def place(ids, splits, pieces, others):
    depth = pieces[0].shape[0]
    return call(
        functools.partial(place_pieces, depth, splits),
        [shaped((8 * depth, width), LOW) for width in splits],
        (ids, *pieces, *others),
        own_copies=8 * len(splits),
    )


def place_line_pieces(ids_ref, *refs):
    far = ids_ref[1] >> 1
    height = refs[0].shape[0]
    pairs = []
    for k in range(4):
        start = pl.multiple_of((far ^ k) * height, height)
        pairs.append((refs[k], refs[4].at[pl.ds(start, height)]))
    copy_all(pairs, refs[5])


def place_line(ids, *pieces):
    whole = shaped((4 * pieces[0].shape[0], pieces[0].shape[1]), LOW)
    return call(place_line_pieces, [whole], (ids, *pieces), own_copies=4)[0]


def three_ways(block):
    return [row_swap(block, 2 * k) for k in range(1, 4)]


def split_sums(row_ref, whole_ref, sent_ref, own_ref, *low_refs):
    row = row_ref[1]
    x, far = row & 1, row >> 1
    depth = own_ref.shape[0]
    for k in range(4):
        owner = far ^ k
        start = pl.multiple_of((owner * 2 + x) * depth, depth)
        value = whole_ref[pl.ds(start, depth)].astype(WIDE) + sent_ref[owner].astype(WIDE)
        if k == 0:
            own_ref[...] = value
        else:
            low_refs[k - 1][...] = value.astype(LOW)


def choose(bit, zero, one):
    return jnp.where(bit == 0, zero, one)


def put(ref, column, *values):
    for value in values:
        ref[:, column : column + value.shape[1]] = value.astype(ref.dtype)
        column += value.shape[1]


def total(refs):
    value = refs[0][...]
    for ref in refs[1:]:
        value = value + ref[...].astype(WIDE)
    return value


def device_bits(ids_ref):
    here, row = ids_ref[0], ids_ref[1]
    return here & 1, here >> 1, row & 1, row >> 1


def keep_and_send(kept, sent, column, bit, zero, one):
    put(kept, column, choose(bit, zero, one))
    put(sent, column, choose(bit, one, zero))
    return column + zero.shape[1]


def deal_first_core(ids, self_in, self_out, cross_out, norms, kept, sent):
    core, _, _, _ = device_bits(ids)
    depth = self_in.shape[0]
    for y in range(2):
        for j in range(3):
            first, column = (4 * j + 2 * y) * 64, (3 * y + j) * 64
            zero, one = self_in[:, first : first + 64], self_in[:, first + 64 : first + 128]
            kept[:depth, column : column + 64] = choose(core, zero, one)
            sent[:depth, column : column + 64] = choose(core, one, zero)
    for index, ref in enumerate((self_out, cross_out)):
        rows = slice(64 * index, 64 * (index + 1))
        kept[rows, 384:] = choose(core, ref[:64], ref[64:])
        sent[rows, 384:] = choose(core, ref[64:], ref[:64])
    for ref in (kept, sent):
        ref[depth:] = jnp.zeros_like(ref[depth:])
        ref[depth : depth + norms.shape[0], :256] = norms[...]


def deal_first_far(ids, kept, came, far_kept, far_sent):
    core, y, _, _ = device_bits(ids)
    depth = 128
    column = 0
    sources = [choose(core, kept[...], came[...]), choose(core, came[...], kept[...])]
    for source in sources:
        columns = slice(column, column + 192)
        zero, one = source[:depth, :192], source[:depth, 192:384]
        far_kept[:depth, columns] = choose(y, zero, one)
        far_sent[:depth, columns] = choose(y, one, zero)
        column += 192
    for index, source in enumerate(sources):
        for ref in (far_kept, far_sent):
            ref[:depth, column : column + 256] = source[:depth, 384:]
            ref[depth:, index * 256 : (index + 1) * 256] = source[depth:, :256]
        column += 256
    for ref in (far_kept, far_sent):
        ref[depth:, 512:] = jnp.zeros_like(ref[depth:, 512:])


def deal_first_last(ids, kept, came, mixed, lines, norms):
    _, y, _, _ = device_bits(ids)
    zero, one = choose(y, kept[...], came[...]), choose(y, came[...], kept[...])
    put(mixed, 0, zero[:128, :384], one[:128, :384])
    put(lines, 0, zero[:128, 384:], one[:128, 384:])
    put(norms, 0, zero[128:, :512], one[128:, :512])


def deal_rest_core(ids, query, pairs, up, down, kept, sent):
    core, _, _, _ = device_bits(ids)
    column = 0
    for y in range(2):
        for r in range(2):
            first = (4 * r + 2 * y) * 128
            zero, one = up[:, first : first + 128], up[:, first + 128 : first + 256]
            column = keep_and_send(kept, sent, column, core, zero, one)
    for y in range(2):
        zero, one = [down[(2 * y + c) * 128 : (2 * y + c + 1) * 128] for c in range(2)]
        column = keep_and_send(kept, sent, column, core, zero, one)
    for y in range(2):
        for j in range(2):
            first = (4 * j + 2 * y) * 64
            zero, one = pairs[:, first : first + 64], pairs[:, first + 64 : first + 128]
            column = keep_and_send(kept, sent, column, core, zero, one)
    for y in range(2):
        zero, one = query[:, 128 * y : 128 * y + 64], query[:, 128 * y + 64 : 128 * y + 128]
        column = keep_and_send(kept, sent, column, core, zero, one)


def deal_rest_far(ids, kept, came, far_kept, far_sent):
    core, y, _, _ = device_bits(ids)
    sources = [choose(core, kept[...], came[...]), choose(core, came[...], kept[...])]
    column = 0
    for first, width in ((0, 256), (512, 256), (1024, 128)):
        for source in sources:
            zero = source[:, first : first + width]
            one = source[:, first + width : first + 2 * width]
            column = keep_and_send(far_kept, far_sent, column, y, zero, one)
    for source in sources:
        put(far_kept, column, source[:, 1280:])
        put(far_sent, column, source[:, 1280:])
        column += 128


def deal_rest_last(ids, kept, came, attend, ffn):
    _, y, _, _ = device_bits(ids)
    sources = [choose(y, kept[...], came[...]), choose(y, came[...], kept[...])]
    put(ffn, 0, *[s[:, :512] for s in sources], *[s[:, 512:1024] for s in sources])
    put(attend, 512, *[s[:, 1024:1280] for s in sources])
    for group in range(2):
        for place, source in enumerate(sources):
            for c in range(2):
                first = 1280 + c * 128
                zero = source[:, first + group * 64 : first + group * 64 + 64]
                one = source[:, first + (1 - group) * 64 : first + (1 - group) * 64 + 64]
                put(attend, group * 256 + (2 * place + c) * 64, choose(y, zero, one))


def ffn_far(ids, value, kept, sent):
    _, y, _, _ = device_bits(ids)
    for half in range(2):
        zero = value[:, half * 1024 : half * 1024 + 512]
        one = value[:, half * 1024 + 512 : half * 1024 + 1024]
        put(kept, half * 512, choose(y, zero, one))
        put(sent, half * 512, choose(y, one, zero))


def ffn_core(ids, kept, came, core_kept, core_sent):
    core, y, _, _ = device_bits(ids)
    mine, other = kept[...], came[...]
    column = 0
    for source in (choose(y, mine, other), choose(y, other, mine)):
        for half in range(2):
            zero = source[:, half * 512 : half * 512 + 256]
            one = source[:, half * 512 + 256 : half * 512 + 512]
            put(core_kept, column, choose(core, zero, one))
            put(core_sent, column, choose(core, one, zero))
            column += 256


def ffn_last(ids, kept, came, up, down):
    core, _, _, _ = device_bits(ids)
    mine, other = kept[...], came[...]
    for c, source in enumerate((choose(core, mine, other), choose(core, other, mine))):
        for y in range(2):
            sender = 2 * y + c
            for r in range(2):
                first = 512 * y + 128 * r
                put(up, (4 * r + sender) * 128, source[:, first : first + 128])
            rows = slice(sender * 128, (sender + 1) * 128)
            down[rows] = source[:, 512 * y + 256 : 512 * y + 512].astype(WIDE)


def mixed_far(ids, own, a, b, c, kept, sent):
    _, y, _, _ = device_bits(ids)
    value = total((own, a, b, c))
    put(kept, 0, choose(y, value[:, :384], value[:, 384:]))
    put(sent, 0, choose(y, value[:, 384:], value[:, :384]))


def mixed_core(ids, kept, came, core_kept, core_sent):
    core, y, _, _ = device_bits(ids)
    mine, other = kept[...], came[...].astype(WIDE)
    for index, source in enumerate((choose(y, mine, other), choose(y, other, mine))):
        put(core_kept, 192 * index, choose(core, source[:, :192], source[:, 192:]))
        put(core_sent, 192 * index, choose(core, source[:, 192:], source[:, :192]))


def mixed_last(ids, kept, came, mixed):
    core, _, _, _ = device_bits(ids)
    mine, other = kept[...], came[...].astype(WIDE)
    for c, source in enumerate((choose(core, mine, other), choose(core, other, mine))):
        for y in range(2):
            for j in range(3):
                first = 192 * y + 64 * j
                put(mixed, (4 * j + 2 * y + c) * 64, source[:, first : first + 64])


def attend_x(ids, query, cross, sent):
    _, y, x, _ = device_bits(ids)
    for z in range(4):
        start = pl.multiple_of((2 * z + 1 - x) * 128, 128)
        line = pl.multiple_of(((y ^ x ^ 1) * 4 + z) * 64, 64)
        sent[z, :, :512] = query[pl.ds(start, 128)]
        sent[z, :64, 512:] = cross[pl.ds(line, 64), :512]
        sent[z, 64:, 512:] = cross[pl.ds(line, 64), 512:]


def pairs_x(ids, pairs, sent):
    _, _, x, _ = device_bits(ids)
    for z in range(4):
        sent[z] = pairs[pl.ds(pl.multiple_of((2 * z + 1 - x) * 128, 128), 128)]


def attend_along_z(ids, query, cross, came, own, a, b, c):
    _, y, x, z = device_bits(ids)
    for k, ref in enumerate((own, a, b, c)):
        owner = z ^ k
        start = pl.multiple_of((2 * owner + x) * 128, 128)
        line = pl.multiple_of(((y ^ x) * 4 + owner) * 64, 64)
        moved = came[owner].astype(WIDE)
        value = query[pl.ds(start, 128)].astype(WIDE) + moved[:, :512]
        ref[:, :512] = value.astype(ref.dtype)
        value = cross[pl.ds(line, 64)].astype(WIDE)
        ref[:64, 512:] = (value[:, :512] + moved[:64, 512:]).astype(ref.dtype)
        ref[64:, 512:] = (value[:, 512:] + moved[64:, 512:]).astype(ref.dtype)


def pairs_along_z(ids, pairs, self_out, came, own, a, b, c):
    _, _, x, z = device_bits(ids)
    for k, ref in enumerate((own, a, b, c)):
        owner = z ^ k
        start = pl.multiple_of((2 * owner + x) * 128, 128)
        below = pl.multiple_of(owner * 64, 64)
        value = pairs[pl.ds(start, 128)].astype(WIDE) + came[owner].astype(WIDE)
        ref[:, :512] = value.astype(ref.dtype)
        ref[:64, 512:] = self_out[pl.ds(below, 64), :512].astype(ref.dtype)
        ref[64:, 512:] = self_out[pl.ds(below, 64), 512:].astype(ref.dtype)


def attend_total(ids, *refs):
    value, line = refs[8:]
    value[:, :1024] = total(refs[:4])
    value[:, 1024:] = total(refs[4:8])
    line[...] = value[:, 1536:].astype(LOW)


def attend_far(ids, value, line, kept, sent):
    _, y, _, _ = device_bits(ids)
    own = value[:, 1536:] + line[...].astype(WIDE)
    low_half = jnp.concatenate([own[:64], value[:64, 512:1024]], axis=0)
    high_half = jnp.concatenate([own[64:], value[64:, 512:1024]], axis=0)
    put(kept, 0, choose(y, low_half, high_half))
    put(sent, 0, choose(y, high_half, low_half))
    mine, other = value[:, :256], value[:, 256:512]
    for index, group in enumerate((choose(y, mine, other), choose(y, other, mine))):
        put(kept, 512 + 128 * index, choose(y, group[:, :128], group[:, 128:]))
        put(sent, 512 + 128 * index, choose(y, group[:, 128:], group[:, :128]))
    pairs = value[:, 1024:1536]
    put(kept, 768, choose(y, pairs[:, :256], pairs[:, 256:]))
    put(sent, 768, choose(y, pairs[:, 256:], pairs[:, :256]))


def attend_core(ids, kept, came, core_kept, core_sent):
    core, y, x, _ = device_bits(ids)
    mine, other = kept[...], came[...].astype(WIDE)
    owner = jnp.where(x == y, mine[:64, :512], other[:64, :512])
    lines = jnp.concatenate([owner, mine[64:, :512] + other[64:, :512]], axis=0)
    put(core_kept, 0, choose(core, lines[:, :256], lines[:, 256:]))
    put(core_sent, 0, choose(core, lines[:, 256:], lines[:, :256]))
    query = mine[:, 512:768] + other[:, 512:768]
    for group in range(2):
        zero, one = [query[:, 128 * group + 64 * c : 128 * group + 64 * c + 64] for c in range(2)]
        put(core_kept, 256 + 64 * group, choose(core, zero, one))
        put(core_sent, 256 + 64 * group, choose(core, one, zero))
    mine, other = mine[:, 768:], other[:, 768:]
    for index, source in enumerate((choose(y, mine, other), choose(y, other, mine))):
        put(core_kept, 384 + 128 * index, choose(core, source[:, :128], source[:, 128:]))
        put(core_sent, 384 + 128 * index, choose(core, source[:, 128:], source[:, :128]))


def attend_last(ids, kept, came, self_out, query, pairs, cross):
    core, _, _, _ = device_bits(ids)
    mine, other = kept[...], came[...].astype(WIDE)
    for c, source in enumerate((choose(core, mine, other), choose(core, other, mine))):
        self_out[64 * c : 64 * c + 64] = source[:64, :256]
        cross[64 * c : 64 * c + 64] = source[64:, :256]
        for y in range(2):
            put(query, 64 * (2 * y + c), source[:, 256 + 64 * y : 320 + 64 * y])
            for j in range(2):
                first = 384 + 128 * y + 64 * j
                put(pairs, 64 * (4 * j + 2 * y + c), source[:, first : first + 64])


def along_z(values):
    return [row_swap(v, 2 * (k + 1)) for k, v in enumerate(values)]


def return_ffn(ids, sums):
    low = lambda *shape: shaped(shape, LOW)
    wide = lambda *shape: shaped(shape, WIDE)
    kept, sent = call(ffn_far, [low(128, 1024)] * 2, (ids, sums))
    kept, sent = call(ffn_core, [low(128, 1024)] * 2, (ids, kept, swap(sent, 2)))
    return call(ffn_last, [wide(128, 1024), wide(512, 256)], (ids, kept, swap(sent, 1)))


def return_mixed(ids, own, parts):
    low = lambda *shape: shaped(shape, LOW)
    wide = lambda *shape: shaped(shape, WIDE)
    kept, sent = call(mixed_far, [wide(128, 384), low(128, 384)], (ids, own, *parts))
    kept, sent = call(mixed_core, [wide(128, 384), low(128, 384)], (ids, kept, swap(sent, 2)))
    (mixed,) = call(mixed_last, [wide(128, 768)], (ids, kept, swap(sent, 1)))
    return mixed


def return_attend(ids, *parts):
    low = lambda *shape: shaped(shape, LOW)
    wide = lambda *shape: shaped(shape, WIDE)
    value, line = call(attend_total, [wide(128, 2048), low(128, 512)], (ids, *parts))
    kept, sent = call(
        attend_far, [wide(128, 1024), low(128, 1024)], (ids, value, row_swap(line, 1))
    )
    kept, sent = call(attend_core, [wide(128, 640), low(128, 640)], (ids, kept, swap(sent, 2)))
    return call(
        attend_last,
        [wide(128, 256), wide(128, 256), wide(128, 512), wide(128, 256)],
        (ids, kept, swap(sent, 1)),
    )


def own_heads(matrix, here):
    rows = gather_rows(lax.all_gather(matrix, "text", axis=1, tiled=True))
    width = rows.shape[1]
    grouped = rows.reshape(HEADS // WAYS, WAYS, -1, width)
    return pick(grouped, here, 1).reshape(-1, width)


def return_heads(grad, here):
    count, width = grad.shape
    spread = jnp.zeros((HEADS // WAYS, WAYS, count * WAYS // HEADS, width), grad.dtype)
    spread = lax.dynamic_update_index_in_dim(
        spread, grad.reshape(HEADS // WAYS, 1, -1, width), here, 1
    )
    columns = lax.psum_scatter(
        spread.reshape(count * WAYS, width), "text", scatter_dimension=1, tiled=True
    )
    return sum_rows(columns)


def mask_marks(segments, lengths):
    clip = jnp.arange(lengths.shape[0], dtype=jnp.int32)
    ends = jnp.sum(jnp.where(clip[None, :] <= clip[:, None], lengths[None, :], 0), axis=1)
    begins = jnp.sum((segments[None, :] < clip[:, None]).astype(jnp.int32), axis=1)
    same = (segments[None, :] == clip[:, None]).astype(jnp.int32)
    rows = [begins, ends - lengths, ends] + [jnp.zeros_like(ends)] * 5
    return jnp.stack([jnp.sum(same * values[:, None], axis=0) for values in rows])


def gelu_parts(up):
    phi = 0.5 * (1.0 + lax.erf(up * math.sqrt(0.5)))
    slope = phi + up * (jnp.exp(-0.5 * up * up) * (1.0 / math.sqrt(2.0 * math.pi)))
    return lax.optimization_barrier(((up * phi).astype(LOW), slope))


def norms_core(ids, *refs):
    core, _, _, _ = device_bits(ids)
    kept, sent = refs[6:]
    for ref in (kept, sent):
        ref[...] = jnp.zeros_like(ref)
    for index, row in enumerate(refs[:6]):
        for y in range(2):
            zero, one = [row[:, (2 * y + c) * 256 : (2 * y + c + 1) * 256] for c in range(2)]
            columns = slice(256 * y, 256 * (y + 1))
            kept[index : index + 1, columns] = choose(core, zero, one)
            sent[index : index + 1, columns] = choose(core, one, zero)


def norms_far(ids, kept, came, far_kept, far_sent):
    _, y, _, _ = device_bits(ids)
    value = kept[...] + came[...]
    far_kept[...] = choose(y, value[:, :256], value[:, 256:])
    far_sent[...] = choose(y, value[:, 256:], value[:, :256])


def norms_over_text(ids, rows):
    wide = lambda *shape: shaped(shape, WIDE)
    kept, sent = call(norms_core, [wide(8, 512)] * 2, (ids, *[r[None] for r in rows]))
    kept, sent = call(norms_far, [wide(8, 256)] * 2, (ids, kept, swap(sent, 1)))
    return kept + swap(sent, 2)


def over_rows(sums):
    mask = 1
    while mask < lax.axis_size("rows"):
        sums = sums + row_swap(sums, mask)
        mask = 2 * mask
    return sums


def reduce_norms(rows, here):
    split = jnp.stack(rows).reshape(6, 2, 2, -1)
    split = pick(split, here & 1, 2) + swap(pick(split, 1 - (here & 1), 2), 1)
    return over_rows(pick(split, here >> 1, 1) + swap(pick(split, 1 - (here >> 1), 1), 2))


def local_grid(
    frames,
    text_states,
    frame_segments,
    text_lengths,
    self_in,
    self_out,
    cross_query,
    cross_kv,
    cross_out,
    ffn_in,
    ffn_out,
    norm_gains,
    norm_biases,
    out_grad,
):
    here, row = lax.axis_index("text"), lax.axis_index("rows")
    ids = jnp.stack([here, row]).astype(jnp.int32)
    width = frames.shape[2]
    count = frames.shape[1] * WAYS
    inner = width // WAYS
    low = lambda *shape: shaped(shape, LOW)
    wide = lambda *shape: shaped(shape, WIDE)
    marks = mask_marks(frame_segments[0], text_lengths[0])

    norms = jnp.concatenate([norm_gains, norm_biases], axis=0)
    kept, sent = call(
        deal_first_core, [low(144, 640)] * 2, (ids, self_in, self_out, cross_out, norms)
    )
    kept, sent = call(deal_first_far, [low(144, 896)] * 2, (ids, kept, swap(sent, 1)))
    came = swap(sent, 2)
    (frames_low,) = sync(frames[0], sent)[:1]
    frames_wide = frames_low.astype(WIDE)
    rest = sync(cross_query, cross_kv, ffn_in, ffn_out, sent)[:4]
    rest_kept, rest_sent = call(deal_rest_core, [low(128, 1408)] * 2, (ids, *rest))
    rest_kept, rest_sent = call(
        deal_rest_far, [low(128, 1536)] * 2, (ids, rest_kept, swap(rest_sent, 1))
    )
    mixed, lines, norms = call(
        deal_first_last, [low(128, 768), low(128, 1024), wide(16, 1024)], (ids, kept, came)
    )
    gains, biases = norms[:3], norms[3:6]
    one, hat_one, inverse_one = norm_forward(frames_wide, gains[0], biases[0])
    mixed, lines, rest_sent, one = sync(mixed, lines, rest_sent, one)
    mixed_z = three_ways(mixed)
    mixed_x = row_swap(mixed, 1)
    lines_x = row_swap(lines, 1)
    mixed_x1 = row_swap(mixed_z[0], 1)
    rest_came = swap(rest_sent, 2)
    one_far, one_near = swap(one, 2), swap(one, 1)
    attend, ffn_block = call(
        deal_rest_last, [low(128, 1024), low(128, 2048)], (ids, rest_kept, rest_came)
    )
    lines = jnp.where((row & 1) == (here >> 1), lines, lines_x)
    *mixed_z, mixed_x, mixed_x1, attend, lines, one_far, text, grad = sync(
        *mixed_z, mixed_x, mixed_x1, attend, lines, one_far, text_states[0], out_grad[0]
    )
    mixed_x2 = row_swap(jnp.stack(mixed_z[1:]), 1)
    self_line, cross_line = lines[:64], lines[64:]
    self_z = three_ways(self_line)
    attend_z = three_ways(attend)
    attend_x0 = row_swap(attend, 1)
    one_all = join(ids, one, one_far, one_near, swap(one_far, 1))
    text_far, text_near = swap(text, 2), swap(text, 1)
    mixed_x2, one_all, text_far, *self_z, ffn_block = sync(
        mixed_x2, one_all, text_far, *self_z, ffn_block
    )
    w_ffn = gather_rows(ffn_block)
    (w_mixed,) = place(ids, (768,), [mixed, *mixed_z], [mixed_x, mixed_x1, mixed_x2])
    mixed_low = mm(one_all, w_mixed).astype(LOW)
    w_self = place_line(ids, self_line, *self_z)
    mixed_low, *attend_z, grad, attend, cross_line, w_self, attend_x0 = sync(
        mixed_low, *attend_z, grad, attend, cross_line, w_self, attend_x0
    )
    attend_x1 = row_swap(attend_z[0], 1)
    attend_x2 = row_swap(jnp.stack(attend_z[1:]), 1)
    cross_z = three_ways(cross_line)
    grad_far, grad_near = swap(grad, 2), swap(grad, 1)
    self_att, self_lse = call(
        self_forward, [low(count, inner), wide(4, count)], (ids, marks, mixed_low), resident=True
    )
    text_all = join(ids, text, text_far, text_near, swap(text_far, 1))
    self_att, text_all, attend_x0, attend_x1, grad_far, *cross_z = sync(
        self_att, text_all, attend_x0, attend_x1, grad_far, *cross_z
    )
    received, attend_x2 = scatter_slots(self_att, w_self, 0, None, (attend_x2,))
    hidden = frames_wide + received
    w_query, w_pairs = place(
        ids, (512, 512), [attend, *attend_z], [attend_x0, attend_x1, attend_x2]
    )
    w_cross = place_line(ids, cross_line, *cross_z)
    grad_all = join(ids, grad, grad_far, grad_near, swap(grad_far, 1))
    text_count = text_all.shape[0]
    pairs_own = mm(text_all, w_pairs).astype(LOW)
    pairs_other = swap(pairs_own, 2)
    w_cross_far = swap(sync(w_cross, pairs_other)[0], 2)
    two, hat_two, inverse_two = norm_forward(hidden, gains[1], biases[1])
    two_pair = gather_pair(two, ids)
    pair_count = two_pair.shape[0]
    query = mm(two_pair, w_query).astype(LOW)
    cross_att, cross_lse = call(
        cross_forward,
        [low(pair_count, 2 * inner), wide(8, pair_count)],
        (ids, marks, query, pairs_own, pairs_other),
        resident=True,
    )
    w_cross_both = join(ids, w_cross, w_cross_far)
    hidden_two = hidden + scatter_pair(cross_att, w_cross_both, 0)
    three, hat_three, inverse_three = norm_forward(hidden_two, gains[2], biases[2])
    three_all = gather_slots(three, ids)
    w_up, w_down = w_ffn[:, :width], w_ffn[:, width:]
    activ, slope = gelu_parts(mm(three_all, w_up))

    grad_up = (mm(grad_all, w_down, 1, 1) * slope).astype(LOW)
    g_ffn = weight_grads(three_all, grad_up, activ, grad_all)
    grad_three, g_ffn = scatter_slots(grad_up, w_up, 1, None, (g_ffn,))
    ffn_sums = sum_rows(g_ffn)
    output_part = scatter_slots(activ, w_down, 0, grad_three)
    part, gain_three, bias_three = norm_backward(grad_three, hat_three, inverse_three, gains[2])
    grad_two = out_grad[0].astype(WIDE) + part
    branch_two = gather_pair(grad_two.astype(LOW), ids)
    grad_cross = mm(branch_two, w_cross_both, 1, 1).astype(LOW)
    grad_query, pairs_mine, pairs_away = call(
        cross_backward,
        [low(pair_count, 2 * inner)] + [low(text_count, 2 * inner)] * 2,
        (ids, marks, query, pairs_own, pairs_other, grad_cross, cross_lse),
        resident=True,
    )
    grad_query, pairs_away, output_part = sync(grad_query, pairs_away, output_part)
    output = (hidden_two + output_part).astype(LOW)
    pairs_came = swap(pairs_away, 2)
    g_cross = mm(cross_att, branch_two, 0, 0).astype(LOW)
    g_query = mm(two_pair, grad_query, 0, 0).astype(LOW)
    (attend_sent,) = call(attend_x, [low(4, 128, 1024)], (ids, g_query, g_cross))
    attend_came = row_swap(attend_sent, 1)
    part, gain_two, bias_two = norm_backward(
        scatter_pair(grad_query, w_query, 1), hat_two, inverse_two, gains[1]
    )
    grad_hidden = grad_two + part
    grad_low, pairs_came = sync(grad_hidden.astype(LOW), pairs_came)
    grad_pairs = (pairs_mine.astype(WIDE) + pairs_came.astype(WIDE)).astype(LOW)
    g_pairs = mm(text_all, grad_pairs, 0, 0).astype(LOW)
    (pairs_sent,) = call(pairs_x, [low(4, 128, 512)], (ids, g_pairs))
    pairs_came = row_swap(pairs_sent, 1)
    branch = gather_slots(grad_low, ids)
    text_part = scatter_slots(grad_pairs, w_pairs, 1, branch)
    grad_self = mm(branch, w_self, 1, 1).astype(LOW)
    (grad_mixed,) = call(
        self_backward,
        [low(count, 3 * inner)],
        (ids, marks, mixed_low, grad_self, self_lse),
        scratch=[pltpu.VMEM((count, 128), WIDE), pltpu.VMEM((count, 128), WIDE)],
        resident=True,
    )
    grad_mixed, attend_came, branch = sync(grad_mixed, attend_came, branch)
    sums = [wide(128, 1024)] + [low(128, 1024)] * 3
    attend_own, *attend_parts = call(attend_along_z, sums, (ids, g_query, g_cross, attend_came))
    attend_parts = along_z(attend_parts)
    g_mixed = mm(one_all, grad_mixed, 0, 0).astype(LOW)
    mixed_came = row_swap(pick(g_mixed.reshape(4, 2, 128, 768), 1 - (row & 1), 1), 1)
    g_self = mm(self_att, branch, 0, 0).astype(LOW)
    grad_one, g_self, text_part, pairs_came, *attend_parts = scatter_slots(
        grad_mixed, w_mixed, 1, None, (g_self, text_part, pairs_came, *attend_parts)
    )
    text_grad = text_part
    pairs_own, *pairs_parts = call(pairs_along_z, sums, (ids, g_pairs, g_self, pairs_came))
    pairs_parts = along_z(pairs_parts)
    grad_one, pairs_first = sync(grad_one, pairs_parts[0])
    part, gain_one, bias_one = norm_backward(grad_one, hat_one, inverse_one, gains[0])
    frame_grad = grad_hidden + part
    norm_sums = norms_over_text(
        ids, [gain_one, gain_two, gain_three, bias_one, bias_two, bias_three]
    )
    mixed_came, *pairs_parts = sync(mixed_came, pairs_first, *pairs_parts[1:])
    mixed_own, *mixed_parts = call(
        split_sums, [wide(128, 768)] + [low(128, 768)] * 3, (ids, g_mixed, mixed_came)
    )
    mixed_parts = along_z(mixed_parts)
    mixed_parts[0], norm_sums, ffn_sums, pairs_own = sync(
        mixed_parts[0], norm_sums, ffn_sums, pairs_own
    )
    norm_sums = over_rows(norm_sums)
    d_up, d_down = return_ffn(ids, ffn_sums)
    d_self, d_query, d_pairs, d_cross = return_attend(
        ids, attend_own, *attend_parts, pairs_own, *pairs_parts
    )
    d_mixed = return_mixed(ids, mixed_own, mixed_parts)
    return (
        output[None],
        frame_grad[None],
        text_grad[None],
        d_mixed,
        d_self,
        d_query,
        d_pairs,
        d_cross,
        d_up,
        d_down,
        norm_sums[:3],
        norm_sums[3:6],
    )


def local_general(
    frames,
    text_states,
    frame_segments,
    text_lengths,
    self_in,
    self_out,
    cross_query,
    cross_kv,
    cross_out,
    ffn_in,
    ffn_out,
    norm_gains,
    norm_biases,
    out_grad,
):
    here = lax.axis_index("text")
    row = lax.axis_index("rows")
    ids = jnp.stack([here, row]).astype(jnp.int32)
    row_count = lax.axis_size("rows")
    width = frames.shape[2]
    count = frames.shape[1] * WAYS
    inner = width // WAYS

    chunk = ffn_out.shape[0] // WAYS
    norms = jnp.concatenate([norm_gains, norm_biases], axis=0)
    norms = ordered(norms, swap(norms, 2), here >> 1)
    norms = ordered(norms, swap(norms, 1), here & 1, 1)
    norms = jnp.moveaxis(norms, 2, 0).reshape(6, width).astype(WIDE)
    gains, biases = norms[:3], norms[3:]
    depth = ffn_in.shape[0]
    gate = norms
    w_mixed = gather_rows(side_by_side(exchange(deal(self_in, 3), here)))
    w_query = gather_rows(side_by_side(exchange(deal(cross_query, 1), here)))
    w_query = jnp.concatenate([w_query, swap(w_query, 2)], axis=1)
    w_pairs = gather_rows(side_by_side(exchange(deal(cross_kv, 2), here)))
    w_self = own_heads(self_out, here)
    w_cross = own_heads(cross_out, here)
    w_up = gather_rows(side_by_side(exchange(deal(ffn_in, row_count // WAYS), here)))
    w_down = ffn_out.reshape(WAYS, chunk, inner)
    w_down = gather_rows(side_by_side(exchange(w_down, here)))

    marks = mask_marks(frame_segments[0], text_lengths[0])

    frames_wide = frames[0].astype(WIDE)
    one, hat_one, inverse_one = norm_forward(frames_wide, gains[0], biases[0])
    one_all = gather_slots(after(one, gate), ids)
    text_all = gather_slots(after(text_states[0], one_all), ids)
    grad_all = gather_slots(after(out_grad[0], text_all), ids)
    one_all = after(one_all, text_all, grad_all)
    mixed = mm(one_all, w_mixed).astype(LOW)
    self_att, self_lse = call(
        self_forward,
        [shaped((count, inner), LOW), shaped((4, count), WIDE)],
        (ids, marks, mixed),
        resident=True,
    )
    hidden = frames_wide + scatter_slots(self_att, w_self, 0)
    two, hat_two, inverse_two = norm_forward(hidden, gains[1], biases[1])
    two_pair = gather_pair(two, ids)
    pair_count = two_pair.shape[0]
    text_count = text_all.shape[0]
    pairs_own = mm(text_all, w_pairs).astype(LOW)
    pairs_other = swap(pairs_own, 2)
    w_cross_both = join(ids, w_cross, swap(after(w_cross, pairs_other), 2))
    query = mm(two_pair, w_query).astype(LOW)
    cross_att, cross_lse = call(
        cross_forward,
        [shaped((pair_count, 2 * inner), LOW), shaped((8, pair_count), WIDE)],
        (ids, marks, query, pairs_own, pairs_other),
        resident=True,
    )
    hidden_two = hidden + scatter_pair(cross_att, w_cross_both, 0)
    three, hat_three, inverse_three = norm_forward(hidden_two, gains[2], biases[2])
    three_all = gather_slots(three, ids)
    up = mm(three_all, w_up)
    activ, slope = gelu_parts(up)

    grad_up = (mm(grad_all, w_down, 1, 1) * slope).astype(LOW)
    grad_three = scatter_slots(grad_up, w_up, 1)
    g_up = mm(three_all, grad_up, 0, 0).astype(LOW)
    g_down = mm(activ, grad_all, 0, 0).astype(LOW)
    output = (hidden_two + scatter_slots(activ, w_down, 0, grad_three)).astype(LOW)
    part, gain_three, bias_three = norm_backward(grad_three, hat_three, inverse_three, gains[2])
    grad_two = out_grad[0].astype(WIDE) + part
    branch_two = gather_pair(grad_two.astype(LOW), ids)
    grad_cross = mm(branch_two, w_cross_both, 1, 1).astype(LOW)
    g_cross = mm(cross_att, branch_two, 0, 0).astype(LOW)
    grad_query, pairs_mine, pairs_away = call(
        cross_backward,
        [shaped((pair_count, 2 * inner), LOW)] + [shaped((text_count, 2 * inner), LOW)] * 2,
        (ids, marks, query, pairs_own, pairs_other, grad_cross, cross_lse),
        resident=True,
    )
    part, gain_two, bias_two = norm_backward(
        scatter_pair(grad_query, w_query, 1), hat_two, inverse_two, gains[1]
    )
    grad_pairs = (pairs_mine.astype(WIDE) + swap(pairs_away, 2).astype(WIDE)).astype(LOW)
    g_query = mm(two_pair, grad_query, 0, 0).astype(LOW)
    g_pairs = mm(text_all, grad_pairs, 0, 0).astype(LOW)
    grad_hidden = grad_two + part
    grad_low = grad_hidden.astype(LOW)
    branch = gather_slots(grad_low, ids)
    text_grad = scatter_slots(grad_pairs, w_pairs, 1, branch)
    grad_self = mm(branch, w_self, 1, 1).astype(LOW)
    g_self = mm(self_att, branch, 0, 0).astype(LOW)
    (grad_mixed,) = call(
        self_backward,
        [shaped((count, 3 * inner), LOW)],
        (ids, marks, mixed, grad_self, self_lse),
        scratch=[pltpu.VMEM((count, 128), WIDE), pltpu.VMEM((count, 128), WIDE)],
        resident=True,
    )
    g_mixed = mm(one_all, grad_mixed, 0, 0).astype(LOW)
    part, gain_one, bias_one = norm_backward(
        scatter_slots(grad_mixed, w_mixed, 1), hat_one, inverse_one, gains[0]
    )
    frame_grad = grad_hidden + part

    norm_sums = reduce_norms(
        [gain_one, gain_two, gain_three, bias_one, bias_two, bias_three], here
    )
    parts = jnp.concatenate([apart(sum_rows(g_up)), apart(sum_rows(g_down))], axis=1)
    parts = exchange(parts, here)
    d_up = undeal(parts[:, :depth], row_count // WAYS).astype(WIDE)
    d_down = parts[:, depth:].reshape(ffn_out.shape).astype(WIDE)
    g_query = g_query[:, :inner] + swap(g_query[:, inner:], 2)
    g_cross = g_cross[:inner] + swap(g_cross[inner:], 2)
    d_cross = return_heads(g_cross, here).astype(WIDE)
    d_self = return_heads(g_self, here).astype(WIDE)
    d_query = undeal(exchange(apart(sum_rows(g_query)), here), 1).astype(WIDE)
    d_pairs = undeal(exchange(apart(sum_rows(g_pairs)), here), 2).astype(WIDE)
    d_mixed = undeal(exchange(apart(sum_rows(g_mixed)), here), 3).astype(WIDE)
    return (
        output[None],
        frame_grad[None],
        text_grad[None],
        d_mixed,
        d_self,
        d_query,
        d_pairs,
        d_cross,
        d_up,
        d_down,
        norm_sums[:3],
        norm_sums[3:],
    )


def solution(mesh):
    in_specs = (
        P("rows", "text", None),
        P("rows", "text", None),
        P("rows", None),
        P("rows", None),
        P("rows", "text"),
        P("rows", "text"),
        P("rows", "text"),
        P("rows", "text"),
        P("rows", "text"),
        P("rows", "text"),
        P("rows", "text"),
        P(None, "text"),
        P(None, "text"),
        P("rows", "text", None),
    )
    out_specs = (
        P("rows", "text", None),
        P("rows", "text", None),
        P("rows", "text", None),
        P("rows", "text"),
        P("rows", "text"),
        P("rows", "text"),
        P("rows", "text"),
        P("rows", "text"),
        P("rows", "text"),
        P("rows", "text"),
        P(None, "text"),
        P(None, "text"),
    )
    local = local_grid if mesh.shape["rows"] == 8 else local_general
    return jax.shard_map(local, mesh=mesh, in_specs=in_specs, out_specs=out_specs, check_vma=False)
```
